32 devices in a mesh: ctx: 16 (over z, y, x), fsdp: 2 (over core).
Axes of the slice: x: 2, y: 2, z: 4, core: 2. Of those that a mesh axis runs over, the one named last changes fastest.
Arguments:
- layer_input: bfloat16 [2, 2048, 4544], P('fsdp', 'ctx'), may hold values from -6 to 6
- cotangent: bfloat16 [2, 2048, 4544], P('fsdp', 'ctx'), may hold values from -6 to 6
- norm_gain: float32 [4544], replicated, may hold values from 0.5 to 1.5
- norm_bias: float32 [4544], replicated, may hold values from -3 to 3
- qkv_weight: bfloat16 [4544, 4672], P('ctx', 'fsdp'), may hold values from -1 to 1
- up_weight: bfloat16 [4544, 18176], P('ctx', 'fsdp'), may hold values from -0.09375 to 0.09375
- dense_weight: bfloat16 [4544, 4544], P('ctx', 'fsdp'), may hold values from -0.75 to 0.75
- down_weight: bfloat16 [4544, 18176], P('ctx', 'fsdp'), may hold values from -0.046875 to 0.046875
Outputs:
- layer_output: bfloat16 [2, 2048, 4544], P('fsdp', 'ctx')
- input_grad: float32 [2, 2048, 4544], P('fsdp', 'ctx')
- gain_grad: float32 [4544], replicated
- bias_grad: float32 [4544], replicated
- qkv_grad: float32 [4544, 4672], P('ctx', 'fsdp')
- up_grad: float32 [4544, 18176], P('ctx', 'fsdp')
- dense_grad: float32 [4544, 4544], P('ctx', 'fsdp')
- down_grad: float32 [4544, 18176], P('ctx', 'fsdp')
The draws below stay inside these ranges and needn't reach their ends.
All inputs are finite; a program needn't handle non-finite values.
Results may differ from the reference program's by a relative error of at most 0.04.
Values may be sent and summed in bfloat16 or wider, within the bound.
A program may use at most 1.625 GiB of HBM per device.

```python
import math
import jax
import jax.numpy as jnp
from jax import lax

D = 4544
HEADS = 71
HEAD = 64
FF = 18176
QKV = 4672
LENGTH = 2048
SEQS = 2


def draw_qkv_weight(key, part):
    entries = jax.random.truncated_normal(key, -4.0, 4.0, (D, QKV), jnp.float32) / math.sqrt(D)
    return jnp.clip(entries, -1.0, 1.0).astype(jnp.bfloat16)


def block_levels(stream_key, extent, shards, smallest, top_value):
    level = 1.0
    for position, parts in shards:
        steps = jax.random.uniform(jax.random.fold_in(jax.random.fold_in(stream_key, 6), position), (parts,), jnp.float32, smallest / len(shards), top_value / len(shards))
        level = level * jnp.repeat(jnp.exp(steps), extent[position] // parts).reshape((-1,) + (1,) * (len(extent) - 1 - position))
    return level


def centred(stream_key, shape, width, most, split=(), kind=jnp.bfloat16):
    values = jax.random.normal(stream_key, shape, jnp.float32) * width
    if len(split) > 0:
        values = block_levels(stream_key, shape, split, -0.22, 0.18) * values
    return jnp.clip(values, min=-most, max=most).astype(kind)


def setup_inputs(seed: int = 0) -> dict:
    seeds = jax.random.split(jax.random.key(seed), 9)
    layer_input = centred(seeds[0], (SEQS, LENGTH, D), 1.0, 6.0, ((0, 2), (1, 16)))
    cotangent = centred(seeds[1], (SEQS, LENGTH, D), 1.0, 6.0, ((0, 2), (1, 16)))
    norm_gain = jnp.clip(1.0 + 0.1 * jax.random.normal(seeds[2], (D,), jnp.float32), 0.5, 1.5)
    norm_bias = centred(seeds[3], (D,), 0.5, 3.0, (), jnp.float32)
    qkv_weight = draw_qkv_weight(jax.random.fold_in(seeds[8], 71), 0)
    up_weight = centred(seeds[5], (D, FF), D ** -0.5, 0.09375, ((0, 16), (1, 2)))
    dense_weight = centred(seeds[6], (D, D), (D // 64) ** -0.5, 0.75, ((0, 16), (1, 2)))
    down_weight = centred(seeds[7], (D, FF), FF ** -0.5, 0.046875, ((0, 16), (1, 2)))
    return dict(layer_input=layer_input, cotangent=cotangent, norm_gain=norm_gain, norm_bias=norm_bias, qkv_weight=qkv_weight, up_weight=up_weight, dense_weight=dense_weight, down_weight=down_weight)


@jax.custom_vjp
def low(v):
    return lax.optimization_barrier(v.astype(jnp.bfloat16)).astype(jnp.float32)

@jax.custom_vjp
def low_back(v):
    return v

def low_keep(v):
    return (low(v), None)

def low_pass(kept, grad):
    return (grad,)

def back_keep(v):
    return (v, None)

def back_low(kept, grad):
    return (low(grad),)
low.defvjp(low_keep, low_pass)
low_back.defvjp(back_keep, back_low)
epsilon = 1e-05
rope_base = 10000.0
masked_score = -1e+30
highest = lax.Precision.HIGHEST

def layer_norm(values, gain_vec, bias_vec):
    center = values - lax.optimization_barrier(jnp.mean(values, -1, keepdims=True))
    spread = lax.optimization_barrier(jnp.mean(center * center, -1, keepdims=True))
    return center * lax.rsqrt(spread + epsilon) * gain_vec + bias_vec

def rotate(values, cosines, sines):
    middle = values.shape[-1] // 2
    turned = jnp.concatenate([-values[..., middle:], values[..., :middle]], -1)
    return values * cosines + turned * sines

def angles(positions, head_size):
    inverse_freq = rope_base ** (-jnp.arange(0, head_size, 2).astype(jnp.float32) / head_size)
    phases = positions.astype(jnp.float32)[:, None] * inverse_freq[None, :]
    phases = jnp.concatenate([phases, phases], -1)
    return (jnp.cos(phases), jnp.sin(phases))

def attention(queries, key_rot, values):
    length = key_rot.shape[0]
    query_tokens = math.gcd(32, length)
    blocks = queries.reshape(length // query_tokens, query_tokens, HEADS, HEAD)
    starts = jnp.arange(length // query_tokens, dtype=jnp.int32) * query_tokens
    key_pos = jnp.arange(length, dtype=jnp.int32)

    def one_block(operands):
        query_block, first_pos = operands
        raw_scores = jnp.einsum('qhd,kd->qhk', query_block, key_rot, precision=highest) * HEAD ** (-0.5)
        raw_scores = low_back(raw_scores)
        query_pos = first_pos + jnp.arange(query_tokens, dtype=jnp.int32)
        scores = jnp.where(key_pos[None, None, :] <= query_pos[:, None, None], raw_scores, masked_score)
        row_max = lax.optimization_barrier(jnp.max(scores, -1, keepdims=True))
        exp_scores = jnp.exp(scores - row_max)
        probabilities = low(exp_scores / lax.optimization_barrier(jnp.sum(exp_scores, -1, keepdims=True)))
        return jnp.einsum('qhk,kd->qhd', probabilities, values, precision=highest)
    outputs = lax.map(jax.checkpoint(one_block), (blocks, starts))
    return outputs.reshape(length, HEADS * HEAD)

def sequence(stream, gain_vec, bias_vec, w_joined, w_up, w_dense, w_down):
    length = stream.shape[0]
    features = HEADS * HEAD
    normed = low(layer_norm(stream, gain_vec, bias_vec))
    joined_out = low_back(jnp.dot(normed, w_joined, precision=highest))
    up_raw = low_back(jnp.dot(normed, w_up, precision=highest))
    cosines, sines = angles(jnp.arange(length, dtype=jnp.int32), HEAD)
    queries = low(rotate(joined_out[:, :features].reshape(length, HEADS, HEAD), cosines[:, None, :], sines[:, None, :]))
    key_rot = low(rotate(joined_out[:, features:features + HEAD], cosines, sines))
    values = low(joined_out[:, features + HEAD:])
    attended = low_back(low(attention(queries, key_rot, values)))
    hidden = low(jax.nn.gelu(up_raw, approximate=False))
    branch = jnp.dot(attended, w_dense.T, precision=highest) + jnp.dot(hidden, w_down.T, precision=highest)
    return stream + branch

def reference(layer_input, cotangent, norm_gain, norm_bias, qkv_weight, up_weight, dense_weight, down_weight):

    def forward(stream, gain_vec, bias_vec, w_joined, w_up, w_dense, w_down):
        checked = jax.checkpoint(sequence)

        def single(piece):
            return checked(piece, gain_vec, bias_vec, w_joined, w_up, w_dense, w_down)
        return lax.map(single, stream)
    output, pullback = jax.vjp(forward, layer_input.astype(jnp.float32), norm_gain.astype(jnp.float32), norm_bias.astype(jnp.float32), qkv_weight.astype(jnp.float32), up_weight.astype(jnp.float32), dense_weight.astype(jnp.float32), down_weight.astype(jnp.float32))
    gradients = pullback(cotangent.astype(jnp.float32))
    return (output.astype(jnp.bfloat16), gradients[0], gradients[1], gradients[2], gradients[3], gradients[4], gradients[5], gradients[6])
```

```python
import functools

import jax
import jax.numpy as jnp
from jax import lax
from jax.experimental import pallas as pl
from jax.experimental.pallas import tpu as pltpu
from jax.sharding import PartitionSpec as P

HEADS = 71
HEAD = 64
EPS = 1e-05
ROPE_BASE = 10000.0
MASKED = -1e30
F32 = jnp.float32
BF16 = jnp.bfloat16
ROWS_COLS = (((1,), (1,)), ((), ()))
ROWS_ROWS = (((0,), (0,)), ((), ()))


def dot(a, b, dims=None):
    if dims is None:
        return jnp.dot(a, b, preferred_element_type=F32)
    return lax.dot_general(a, b, dims, preferred_element_type=F32)


def attend_forward_kernel(q_ref, k_ref, v_ref, o_ref, lse_ref, acc, top):
    index = pl.program_id(1)
    rows = q_ref.shape[1]
    q = q_ref[0]
    acc[...] = jnp.zeros_like(acc)
    top[...] = jnp.full_like(top, MASKED)

    def block(start, masked):
        s = dot(q, k_ref[pl.ds(start, rows), :], ROWS_COLS)
        if masked:
            key = lax.broadcasted_iota(jnp.int32, s.shape, 1)
            query = lax.broadcasted_iota(jnp.int32, s.shape, 0)
            s = jnp.where(key <= query, s, MASKED)
        old = top[...]
        new = jnp.maximum(old, jnp.max(s, 1, keepdims=True))
        p = jnp.exp(s - new).astype(BF16)
        acc[...] = acc[...] * jnp.exp(old - new) + dot(p, v_ref[pl.ds(start, rows), :])
        top[...] = new

    def full(i, carry):
        block(pl.multiple_of(i * rows, rows), False)
        return carry

    lax.fori_loop(0, index, full, 0)
    block(pl.multiple_of(index * rows, rows), True)
    total = acc[...]
    norm = total[:, HEAD : HEAD + 1]
    o_ref[0] = total[:, :HEAD] / norm
    lse_ref[0] = top[...] + jnp.log(norm)


def attend_forward(q, k, v):
    heads, length, _ = q.shape
    rows = min(512, length)
    wide = jnp.concatenate([v, jnp.ones_like(v)], 1)
    return pl.pallas_call(
        attend_forward_kernel,
        grid=(heads, length // rows),
        in_specs=[
            pl.BlockSpec((1, rows, HEAD), lambda h, i: (h, i, 0)),
            pl.BlockSpec((length, HEAD), lambda h, i: (0, 0)),
            pl.BlockSpec((length, 2 * HEAD), lambda h, i: (0, 0)),
        ],
        out_specs=[
            pl.BlockSpec((1, rows, HEAD), lambda h, i: (h, i, 0)),
            pl.BlockSpec((1, rows, 1), lambda h, i: (h, i, 0)),
        ],
        out_shape=[
            jax.ShapeDtypeStruct((heads, length, HEAD), F32),
            jax.ShapeDtypeStruct((heads, length, 1), F32),
        ],
        scratch_shapes=[pltpu.VMEM((rows, 2 * HEAD), F32), pltpu.VMEM((rows, 1), F32)],
        compiler_params=pltpu.CompilerParams(vmem_limit_bytes=40 << 20),
        cost_estimate=pl.CostEstimate(
            flops=2 * heads * length * length * HEAD,
            transcendentals=heads * length * length // 2,
            bytes_accessed=8 * heads * length * HEAD,
        ),
        name="attend_forward",
    )(q, k, wide)


def attend_backward_kernel(q_ref, k_ref, v_ref, g_ref, lse_ref, delta_ref, dq_ref, dk_ref, dv_ref, acc):
    index = pl.program_id(1)
    rows = q_ref.shape[1]

    @pl.when((pl.program_id(0) == 0) & (index == 0))
    def _():
        dk_ref[...] = jnp.zeros_like(dk_ref)
        dv_ref[...] = jnp.zeros_like(dv_ref)

    q = q_ref[0]
    g = g_ref[0]
    lse = lse_ref[0]
    delta = delta_ref[0]
    acc[...] = jnp.zeros_like(acc)

    def block(start, masked):
        at = pl.ds(start, rows)
        k = k_ref[at, :]
        s = dot(k, q, ROWS_COLS)
        p = jnp.exp(s - lse)
        if masked:
            key = lax.broadcasted_iota(jnp.int32, s.shape, 0)
            query = lax.broadcasted_iota(jnp.int32, s.shape, 1)
            p = jnp.where(key <= query, p, 0.0)
        dp = dot(v_ref[at, :], g, ROWS_COLS)
        ds = (p * (dp - delta)).astype(BF16)
        dv_ref[at, :] += dot(p.astype(BF16), g)
        dk_ref[at, :] += dot(ds, q)
        acc[...] += dot(ds, k, ROWS_ROWS)

    def full(i, carry):
        block(pl.multiple_of(i * rows, rows), False)
        return carry

    lax.fori_loop(0, index, full, 0)
    block(pl.multiple_of(index * rows, rows), True)
    dq_ref[0] = acc[...]


def attend_backward(q, k, v, g, lse, delta):
    heads, length, _ = q.shape
    rows = min(512, length)
    per_query = pl.BlockSpec((1, rows, HEAD), lambda h, i: (h, i, 0))
    per_row = pl.BlockSpec((1, 1, rows), lambda h, i: (h, 0, i))
    whole = pl.BlockSpec((length, HEAD), lambda h, i: (0, 0))
    return pl.pallas_call(
        attend_backward_kernel,
        grid=(heads, length // rows),
        in_specs=[per_query, whole, whole, per_query, per_row, per_row],
        out_specs=[per_query, whole, whole],
        out_shape=[
            jax.ShapeDtypeStruct((heads, length, HEAD), F32),
            jax.ShapeDtypeStruct((length, HEAD), F32),
            jax.ShapeDtypeStruct((length, HEAD), F32),
        ],
        scratch_shapes=[pltpu.VMEM((rows, HEAD), F32)],
        compiler_params=pltpu.CompilerParams(vmem_limit_bytes=48 << 20),
        cost_estimate=pl.CostEstimate(
            flops=5 * heads * length * length * HEAD,
            transcendentals=heads * length * length // 2,
            bytes_accessed=12 * heads * length * HEAD,
        ),
        name="attend_backward",
    )(q, k, v, g, lse, delta)


def share_heads(columns, chips):
    rows, width = columns.shape
    heads = width // HEAD
    most = -(-heads // chips)
    richer = heads - chips * (most - 1)
    cut = richer * most * HEAD
    first = jnp.moveaxis(columns[:, :cut].reshape(rows, richer, most * HEAD), 1, 0)
    if richer == chips:
        return first
    rest = jnp.moveaxis(columns[:, cut:].reshape(rows, chips - richer, (most - 1) * HEAD), 1, 0)
    return jnp.concatenate([first, jnp.pad(rest, ((0, 0), (0, 0), (0, HEAD)))], 0)


def join_heads(parts, heads):
    chips, rows, width = parts.shape
    most = width // HEAD
    richer = heads - chips * (most - 1)
    first = jnp.moveaxis(parts[:richer], 0, 1).reshape(rows, -1)
    if richer == chips:
        return first
    rest = jnp.moveaxis(parts[richer:, :, : width - HEAD], 0, 1).reshape(rows, -1)
    return jnp.concatenate([first, rest], 1)


def swap(values):
    return lax.ppermute(values, "fsdp", [(0, 1), (1, 0)])


def in_order(mine, other, core, axis):
    return jnp.where(
        core == 0,
        jnp.concatenate([mine, other], axis),
        jnp.concatenate([other, mine], axis),
    )


def half_of(values, core, axis):
    first, second = jnp.split(values, 2, axis)
    return jnp.where(core == 0, first, second), jnp.where(core == 0, second, first)


def to_columns(shard, chips):
    rows, columns = shard.shape
    blocks = jnp.moveaxis(shard.reshape(rows, chips, columns // chips), 1, 0)
    blocks = lax.all_to_all(blocks, "ctx", 0, 0, tiled=True)
    return blocks.reshape(chips * rows, columns // chips)


def to_rows(shard, chips):
    rows, columns = shard.shape
    blocks = lax.all_to_all(shard.reshape(chips, rows // chips, columns), "ctx", 0, 0, tiled=True)
    return jnp.moveaxis(blocks, 0, 1).reshape(rows // chips, chips * columns)


def rotate(values, cosines, sines):
    middle = values.shape[-1] // 2
    turned = jnp.concatenate([-values[..., middle:], values[..., :middle]], -1)
    return values * cosines + turned * sines


def rotate_back(values, cosines, sines):
    middle = values.shape[-1] // 2
    turned = jnp.concatenate([values[..., middle:], -values[..., :middle]], -1)
    return values * cosines + turned * sines


def angles(length):
    inverse_freq = ROPE_BASE ** (-jnp.arange(0, HEAD, 2).astype(F32) / HEAD)
    phases = jnp.arange(length, dtype=jnp.int32).astype(F32)[:, None] * inverse_freq[None, :]
    phases = jnp.concatenate([phases, phases], -1)
    return jnp.cos(phases), jnp.sin(phases)


def gelu(values):
    return jax.nn.gelu(values, approximate=False)


def body(layer_input, cotangent, norm_gain, norm_bias, qkv_weight, up_weight, dense_weight, down_weight):
    chips = lax.axis_size("ctx")
    core = lax.axis_index("fsdp")
    inputs = layer_input[0].astype(F32)
    tokens, features = inputs.shape
    length = tokens * chips
    heads = features // HEAD
    most = -(-heads // chips)
    qwide = most * HEAD
    shard_rows = qkv_weight.shape[0]
    half_rows = -(-shard_rows // 2)

    center = inputs - jnp.mean(inputs, -1, keepdims=True)
    inverse = lax.rsqrt(jnp.mean(center * center, -1, keepdims=True) + EPS)
    xhat = center * inverse
    normed_low = (xhat * norm_gain + norm_bias).astype(BF16)
    grad_low = cotangent[0]

    qkv_rows = in_order(qkv_weight, swap(qkv_weight), core, 1)
    dense_rows = in_order(dense_weight, swap(dense_weight), core, 1)
    joint = jnp.concatenate([qkv_rows, dense_rows], 1)
    joint = jnp.pad(joint, ((0, 2 * half_rows - shard_rows), (0, 0)))
    joint, _ = half_of(joint, core, 0)
    query_cols, kv_cols, dense_cols = jnp.split(joint, [features, features + 2 * HEAD], 1)
    blocks = jnp.concatenate(
        [
            share_heads(query_cols, chips),
            jnp.broadcast_to(kv_cols, (chips, half_rows, 2 * HEAD)),
            share_heads(dense_cols, chips),
        ],
        2,
    )
    blocks = lax.all_to_all(blocks, "ctx", 0, 0, tiled=True)
    small = in_order(blocks, swap(blocks), core, 1)[:, :shard_rows].reshape(features, -1)
    qkv_cols, dense_cols = small[:, : qwide + 2 * HEAD], small[:, qwide + 2 * HEAD :]
    up_mine = to_columns(up_weight, chips)
    up_cols = jnp.concatenate([up_mine, swap(up_mine)], 1)
    down_mine = to_columns(down_weight, chips)
    down_cols = jnp.concatenate([down_mine, swap(down_mine)], 1)

    normed_all = lax.all_gather(normed_low, "ctx", axis=0, tiled=True)
    grad_all = lax.all_gather(grad_low, "ctx", axis=0, tiled=True)
    joined = dot(normed_all, qkv_cols)
    up_raw = dot(normed_all, up_cols)
    cosines, sines = angles(length)
    scale = HEAD ** (-0.5)
    query_raw = jnp.moveaxis(joined[:, :qwide].reshape(length, most, HEAD), 1, 0)
    queries = (rotate(query_raw, cosines, sines).astype(BF16) * scale).astype(BF16)
    keys = rotate(joined[:, qwide : qwide + HEAD], cosines, sines).astype(BF16)
    values = joined[:, qwide + HEAD :].astype(BF16)
    attention, log_sum = attend_forward(queries, keys, values)
    attended_low = jnp.moveaxis(attention.astype(BF16), 0, 1).reshape(length, qwide)
    hidden_low = gelu(up_raw).astype(BF16)
    branch = dot(attended_low, dense_cols, ROWS_COLS) + dot(hidden_low, down_cols, ROWS_COLS)
    branch = lax.psum_scatter(branch.astype(BF16), "ctx", scatter_dimension=0, tiled=True)
    layer_output = (inputs + branch.astype(F32)).astype(BF16)

    grad_heads = dot(grad_all, dense_cols).astype(BF16)
    grad_heads = jnp.moveaxis(grad_heads.reshape(length, most, HEAD), 1, 0)
    grad_hidden = dot(grad_all, down_cols)
    dense_part = dot(grad_all, attended_low, ROWS_ROWS)
    down_part = dot(grad_all, hidden_low, ROWS_ROWS)
    delta = jnp.sum(grad_heads.astype(F32) * attention, 2)
    query_grad, key_grad, value_grad = attend_backward(
        queries, keys, values, grad_heads, log_sum.reshape(most, 1, length), delta.reshape(most, 1, length)
    )
    query_grad = rotate_back(query_grad * scale, cosines, sines).astype(BF16)
    grad_joined = jnp.concatenate(
        [
            jnp.moveaxis(query_grad, 0, 1).reshape(length, qwide),
            rotate_back(key_grad, cosines, sines).astype(BF16),
            value_grad.astype(BF16),
        ],
        1,
    )
    _, gelu_back = jax.vjp(gelu, up_raw)
    grad_up = gelu_back(grad_hidden)[0].astype(BF16)
    grad_normed = dot(grad_joined, qkv_cols, ROWS_COLS) + dot(grad_up, up_cols, ROWS_COLS)
    grad_normed = lax.psum_scatter(
        grad_normed.astype(BF16), "ctx", scatter_dimension=0, tiled=True
    ).astype(F32)
    qkv_part = dot(normed_all, grad_joined, ROWS_ROWS)
    up_part = dot(normed_all, grad_up, ROWS_ROWS)

    def wide_grad(part):
        mine, other = jnp.split(part, 2, 1)
        total = mine + swap(other.astype(BF16)).astype(F32)
        return to_rows(total.astype(BF16), chips).astype(F32)

    down_grad = wide_grad(down_part)
    up_grad = wide_grad(up_part)
    small_part = jnp.concatenate([qkv_part, dense_part], 1).reshape(chips, shard_rows, -1)
    small_part = jnp.pad(small_part, ((0, 0), (0, 2 * half_rows - shard_rows), (0, 0)))
    mine, other = half_of(small_part, core, 1)
    total = (mine + swap(other.astype(BF16)).astype(F32)).astype(BF16)
    total = lax.all_to_all(total, "ctx", 0, 0, tiled=True)
    qkv_rows = jnp.concatenate(
        [
            join_heads(total[:, :, :qwide], heads),
            jnp.sum(total[:, :, qwide : qwide + 2 * HEAD].astype(F32), 0).astype(BF16),
        ],
        1,
    )
    dense_rows = join_heads(total[:, :, qwide + 2 * HEAD :], heads)

    def own_columns(rows):
        mine, other = half_of(rows, core, 1)
        return in_order(mine, swap(other), core, 0)[:shard_rows].astype(F32)

    qkv_grad = own_columns(qkv_rows)
    dense_grad = own_columns(dense_rows)

    gain_part = jnp.sum(grad_normed * xhat, 0)
    bias_part = jnp.sum(grad_normed, 0)
    gain_grad, bias_grad = lax.psum((gain_part, bias_part), ("ctx", "fsdp"))
    scaled = grad_normed * norm_gain
    input_part = (
        scaled
        - jnp.mean(scaled, -1, keepdims=True)
        - xhat * jnp.mean(scaled * xhat, -1, keepdims=True)
    ) * inverse
    input_grad = grad_low.astype(F32) + input_part
    return (
        layer_output[None],
        input_grad[None],
        gain_grad,
        bias_grad,
        qkv_grad,
        up_grad,
        dense_grad,
        down_grad,
    )


def solution(mesh):
    split = P("ctx", "fsdp")
    stream = P("fsdp", "ctx", None)
    return jax.shard_map(
        body,
        mesh=mesh,
        in_specs=(stream, stream, P(), P(), split, split, split, split),
        out_specs=(stream, stream, P(), P(), split, split, split, split),
        check_vma=False,
    )
```

```python
import functools

import jax
import jax.numpy as jnp
from jax import lax
from jax.experimental import pallas as pl
from jax.experimental.pallas import tpu as pltpu
from jax.sharding import PartitionSpec as P

HEADS = 71
HEAD = 64
EPS = 1e-05
ROPE_BASE = 10000.0
MASKED = -1e30
LANES = 128
F32 = jnp.float32
BF16 = jnp.bfloat16
ROWS_COLS = (((1,), (1,)), ((), ()))
ROWS_ROWS = (((0,), (0,)), ((), ()))
MESH = pl.DeviceIdType.MESH
ANY = pl.BlockSpec(memory_space=pl.ANY)
WHOLE = pl.BlockSpec(memory_space=pltpu.VMEM)
DMA = pltpu.SemaphoreType.DMA


def dot(a, b, dims=None):
    if dims is None:
        return jnp.dot(a, b, preferred_element_type=F32)
    return lax.dot_general(a, b, dims, preferred_element_type=F32)


def grid_of(chips):
    return (4, 4, 4) if chips == 64 else (chips // 4, 2, 2)


def padded_rows(rows):
    return -(-rows // 16) * 16


def tile_share(tiles, chips):
    return tiles // chips, tiles % chips


class Place:
    def __init__(self, chips):
        self.chips = chips
        self.nz, self.ny, self.nx = grid_of(chips)
        self.me = lax.axis_index("ctx")
        self.core = lax.axis_index("fsdp")
        self.z = self.me // (self.ny * self.nx)
        self.y = lax.rem(self.me // self.nx, self.ny)
        self.x = lax.rem(self.me, self.nx)

    def at(self, dz, dy, dx):
        z = lax.rem(self.z + dz + self.nz, self.nz)
        y = lax.rem(self.y + dy + self.ny, self.ny)
        x = lax.rem(self.x + dx + self.nx, self.nx)
        return (z * self.ny + y) * self.nx + x

    def pair(self, i):
        return self.me ^ i


def enter(place):
    barrier = pltpu.get_barrier_semaphore()

    def greet(i):
        pl.semaphore_signal(barrier, 1, device_id=(place.pair(i), place.core), device_id_type=MESH)

    each(1, place.chips, greet)
    pl.semaphore_signal(barrier, 1, device_id=(place.me, 1 - place.core), device_id_type=MESH)
    pl.semaphore_wait(barrier, place.chips)


def remote(src, dst, send, recv, chip, core):
    return pltpu.make_async_remote_copy(
        src_ref=src, dst_ref=dst, send_sem=send, recv_sem=recv, device_id=(chip, core), device_id_type=MESH
    )


def each(first, last, do):
    def step(i, carry):
        do(i)
        return carry

    lax.fori_loop(first, last, step, 0)


def when(condition, do):
    if condition is None:
        do()
    else:
        pl.when(condition)(do)


def rows_at(start, count):
    return pl.ds(pl.multiple_of(start, 8), count)


def lanes_at(tile, count):
    return pl.ds(pl.multiple_of(tile * LANES, LANES), count * LANES)


def move(src, dst, sem):
    copy = pltpu.make_async_copy(src, dst, sem)
    copy.start()
    copy.wait()


class Tiles:
    def __init__(self, columns, chips):
        self.chips = chips
        self.least, self.richer = tile_share(columns // LANES, chips)
        assert 0 < self.least and 2 * self.richer <= chips

    def more(self, chip, core):
        return jnp.where(core == 0, chip < self.richer, chip >= self.chips - self.richer)

    def first(self, chip, core):
        late = jnp.maximum(chip - (self.chips - self.richer), 0)
        return self.least * chip + jnp.where(core == 0, jnp.minimum(chip, self.richer), late)

    def cut(self, ref, chip, core):
        start = self.first(chip, core)
        return (
            ref.at[:, lanes_at(start, self.least)],
            ref.at[:, lanes_at(jnp.minimum(start + self.least, self.first(self.chips, core) - 1), 1)],
        )


class Gather:
    @staticmethod
    def shape(chips, a):
        return (chips, *a.shape)

    @staticmethod
    def scratch(chips, a):
        nz, ny, nx = grid_of(chips)
        return [DMA((nz,))] * 2 + [DMA((nz, nx))] * 2 + [DMA((nz, ny))] * 2 + [DMA((nz, nx, ny))] * 4 + [DMA]

    def __init__(self, place, mine, out, sems):
        self.p, self.mine, self.out = place, mine, out
        (self.sl, self.rl, self.sx, self.rx, self.sy, self.ry, self.s1, self.r1, self.s2, self.r2, self.own) = sems
        self.half = mine.shape[0] // 2

    def line(self, k):
        p = self.p
        return remote(self.mine, self.out.at[p.me], self.sl.at[k], self.rl.at[k], p.at(k, 0, 0), p.core)

    def across(self, k, i):
        p = self.p
        b = p.at(-k, 0, 0)
        src = self.mine if k == 0 else self.out.at[b]
        return remote(src, self.out.at[b], self.sx.at[k, i], self.rx.at[k, i], p.at(0, 0, i), p.core)

    def along(self, k, j):
        p = self.p
        b = p.at(-k, 0, 0)
        src = self.mine if k == 0 else self.out.at[b]
        return remote(src, self.out.at[b], self.sy.at[k, j], self.ry.at[k, j], p.at(0, j, 0), p.core)

    def corner1(self, k, i, j):
        p = self.p
        part = self.out.at[p.at(-k, 0, -i), pl.ds(0, self.half)]
        return remote(part, part, self.s1.at[k, i, j], self.r1.at[k, i, j], p.at(0, j, 0), p.core)

    def corner2(self, k, i, j):
        p = self.p
        part = self.out.at[p.at(-k, -j, 0), pl.ds(self.half, self.half)]
        return remote(part, part, self.s2.at[k, i, j], self.r2.at[k, i, j], p.at(0, 0, i), p.core)

    def spread(self, k):
        for i in range(1, self.p.nx):
            self.across(k, i).start()
        for j in range(1, self.p.ny):
            self.along(k, j).start()

    def begin(self):
        for k in range(1, self.p.nz):
            self.line(k).start()
        self.spread(0)
        pltpu.make_async_copy(self.mine, self.out.at[self.p.me], self.own).start()

    def turn(self, k):
        p = self.p
        for i in range(1, p.nx):
            self.across(k, i).wait_recv()
            for j in range(1, p.ny):
                self.corner1(k, i, j).start()
        for j in range(1, p.ny):
            self.along(k, j).wait_recv()
            for i in range(1, p.nx):
                self.corner2(k, i, j).start()

    def steps(self):
        nz = self.p.nz
        order = [1, nz - 1] + list(range(2, nz - 1))

        def come(k):
            self.line(k).wait_recv()
            self.spread(k)

        return (
            [functools.partial(self.turn, 0)]
            + [functools.partial(come, k) for k in order]
            + [functools.partial(self.turn, k) for k in order]
        )

    def end(self):
        p = self.p
        pltpu.make_async_copy(self.mine, self.out.at[p.me], self.own).wait()
        for k in range(p.nz):
            if k:
                self.line(k).wait_send()
            for i in range(1, p.nx):
                self.across(k, i).wait_send()
            for j in range(1, p.ny):
                self.along(k, j).wait_send()
            for i in range(1, p.nx):
                for j in range(1, p.ny):
                    self.corner1(k, i, j).wait()
                    self.corner2(k, i, j).wait()


class Columns:
    @staticmethod
    def shape(chips, a):
        least, _ = tile_share(a.shape[1] // LANES, chips)
        return (chips * a.shape[0], (2 * least + 1) * LANES)

    @staticmethod
    def scratch(chips, a):
        return [DMA((chips,))] * 8 + [pltpu.VMEM((a.shape[0], LANES), a.dtype)]

    def __init__(self, place, weight, out, sems):
        self.p, self.w, self.out = place, weight, out
        self.ms, self.mr, self.es, self.er, self.fs, self.fr, self.gs, self.gr, self.nought = sems
        self.tiles = Tiles(weight.shape[1], place.chips)
        self.rows = weight.shape[0]

    def slots(self, chip, own):
        rows = rows_at(chip * self.rows, self.rows)
        least = self.tiles.least
        return self.out.at[rows, lanes_at(0 if own else least + 1, least)], self.out.at[rows, lanes_at(least, 1)]

    def sends(self, i):
        p = self.p
        chip = p.pair(i)
        (a, b), (c, d) = self.tiles.cut(self.w, chip, p.core), self.slots(p.me, True)
        return (
            remote(a, c, self.ms.at[i], self.mr.at[i], chip, p.core),
            remote(b, d, self.es.at[i], self.er.at[i], chip, p.core),
            self.tiles.more(chip, p.core),
        )

    def gets(self, i):
        p = self.p
        chip = p.pair(i)
        (a, b), (c, d) = self.tiles.cut(self.w, chip, p.core), self.slots(chip, True)
        return (
            remote(a, c, self.ms.at[i], self.mr.at[i], chip, p.core),
            remote(b, d, self.es.at[i], self.er.at[i], chip, p.core),
        )

    def passes(self, i):
        p = self.p
        chip = p.pair(i)
        a, b = self.slots(chip, True)
        if isinstance(i, int) and i == 0:
            a, b = self.tiles.cut(self.w, p.me, p.core)
        c, d = self.slots(chip, False)
        return (
            remote(a, c, self.fs.at[i], self.fr.at[i], p.me, 1 - p.core),
            remote(b, d, self.gs.at[i], self.gr.at[i], p.me, 1 - p.core),
        )

    def here(self):
        p = self.p
        (a, b), (c, d) = self.tiles.cut(self.w, p.me, p.core), self.slots(p.me, True)
        return pltpu.make_async_copy(a, c, self.ms.at[0]), pltpu.make_async_copy(b, d, self.es.at[0])

    def begin(self):
        p = self.p

        def send(i):
            main, extra, more = self.sends(i)
            main.start()
            pl.when(more)(extra.start)

        each(1, p.chips, send)
        own, pass_on = self.here(), self.passes(0)
        own[0].start()
        pass_on[0].start()

        @pl.when(self.tiles.more(p.me, p.core))
        def _():
            own[1].start()
            pass_on[1].start()

    def steps(self):
        return [self.hand_on]

    def hand_on(self):
        p = self.p
        mine = self.tiles.more(p.me, p.core)

        def hand(i):
            main, extra = self.gets(i)
            to_main, to_extra = self.passes(i)
            main.wait_recv()
            to_main.start()

            @pl.when(mine)
            def _():
                extra.wait_recv()
                to_extra.start()

        each(1, p.chips, hand)

    def end(self):
        p = self.p
        mine = self.tiles.more(p.me, p.core)
        theirs = self.tiles.more(p.me, 1 - p.core)
        own = self.here()
        own[0].wait()
        pl.when(mine)(own[1].wait)

        @pl.when(jnp.logical_not(mine | theirs))
        def _():
            self.nought[...] = jnp.zeros_like(self.nought)
            each(0, p.chips, lambda c: move(self.nought, self.slots(c, True)[1], self.es.at[0]))

        def sent(i):
            main, extra, more = self.sends(i)
            main.wait_send()
            pl.when(more)(extra.wait_send)

        each(1, p.chips, sent)

        def handed(i):
            main, extra = self.passes(i)
            main.wait()
            pl.when(mine)(extra.wait_send)
            pl.when(theirs)(extra.wait_recv)

        handed(0)
        each(1, p.chips, handed)


class Blocks:
    @staticmethod
    def shape(chips, a):
        return (chips * 2 * a.shape[1], a.shape[2])

    @staticmethod
    def scratch(chips, a):
        return [DMA((chips,))] * 4

    def __init__(self, place, blocks, out, sems):
        self.p, self.b, self.out = place, blocks, out
        self.s, self.r, self.fs, self.fr = sems
        self.rows = blocks.shape[1]

    def slot(self, chip, core):
        return self.out.at[rows_at((2 * chip + core) * self.rows, self.rows)]

    def sends(self, i):
        p = self.p
        chip = p.pair(i)
        return remote(self.b.at[chip], self.slot(p.me, p.core), self.s.at[i], self.r.at[i], chip, p.core)

    def passes(self, i):
        p = self.p
        part = self.slot(p.pair(i), p.core)
        mine = self.b.at[p.me] if isinstance(i, int) and i == 0 else part
        return remote(mine, part, self.fs.at[i], self.fr.at[i], p.me, 1 - p.core)

    def here(self):
        p = self.p
        return pltpu.make_async_copy(self.b.at[p.me], self.slot(p.me, p.core), self.s.at[0])

    def begin(self):
        each(1, self.p.chips, lambda i: self.sends(i).start())
        self.here().start()
        self.passes(0).start()

    def steps(self):
        return [self.hand_on]

    def hand_on(self):
        def hand(i):
            self.sends(i).wait_recv()
            self.passes(i).start()

        each(1, self.p.chips, hand)

    def end(self):
        p = self.p
        self.here().wait()
        each(1, p.chips, lambda i: self.sends(i).wait_send())
        self.passes(0).wait()
        each(1, p.chips, lambda i: self.passes(i).wait())


def drive(parts):
    for part in parts:
        part.begin()
    todo = [part.steps() for part in parts]
    total = max(len(steps) for steps in todo)
    for at in range(total):
        for steps in todo:
            index = at - (total - len(steps))
            if index >= 0:
                steps[index]()
    for part in parts:
        part.end()


def take(refs, counts):
    out, at = [], 0
    for count in counts:
        out.append(refs[at : at + count])
        at += count
    return out


def bring_kernel(chips, plan, *refs):
    n = len(plan)
    ins, outs, held = refs[:n], refs[n : 2 * n], refs[2 * n :]
    place = Place(chips)
    enter(place)
    held = take(held, [count for _, count in plan])
    drive([kind(place, a, o, h) for (kind, _), a, o, h in zip(plan, ins, outs, held)])


def bring(chips, number, name, *jobs):
    held = [kind.scratch(chips, a) for kind, a in jobs]
    return pl.pallas_call(
        functools.partial(bring_kernel, chips, [(kind, len(h)) for (kind, _), h in zip(jobs, held)]),
        in_specs=[ANY] * len(jobs),
        out_specs=[ANY] * len(jobs),
        out_shape=[jax.ShapeDtypeStruct(kind.shape(chips, a), a.dtype) for kind, a in jobs],
        scratch_shapes=[s for h in held for s in h],
        compiler_params=pltpu.CompilerParams(collective_id=number, has_side_effects=True, vmem_limit_bytes=16 << 20),
        name=name,
    )(*[a for _, a in jobs])


class Paired:
    @staticmethod
    def scratch(chips, shape, dtype):
        return [DMA((chips,))] * 5 + [pltpu.VMEM((chips, *shape), dtype)] * 2

    def __init__(self, place, held, views, gives=None, sums=None, comes=lambda j: None):
        self.p = place
        self.cs, self.cr, self.s, self.r, self.load, self.total, self.stage = held
        self.mine, self.theirs, self.target, self.source = views
        self.gives, self.sums, self.comes = gives, sums, comes

    def across(self, i):
        p = self.p
        return remote(self.theirs(p.pair(i)), self.stage.at[i], self.cs.at[i], self.cr.at[i], p.me, 1 - p.core)

    def fetch(self, i):
        return pltpu.make_async_copy(self.mine(self.p.pair(i)), self.total.at[i], self.load.at[i])

    def sends(self, i):
        p = self.p
        j = p.pair(i)
        return remote(self.total.at[i], self.target(j), self.s.at[i], self.r.at[i], j, p.core)

    def gets(self, i):
        p = self.p
        j = p.pair(i)
        return remote(self.total.at[i], self.source(j), self.s.at[i], self.r.at[i], j, p.core)

    def here(self):
        return pltpu.make_async_copy(self.total.at[0], self.source(self.p.me), self.s.at[0])

    def begin(self):
        chips = self.p.chips
        when(self.gives, lambda: each(0, chips, lambda i: self.across(i).start()))
        when(self.sums, lambda: each(0, chips, lambda i: self.fetch(i).start()))

    def add(self, i):
        self.fetch(i).wait()
        self.across(i).wait_recv()
        self.total[i] = (self.total[i].astype(F32) + self.stage[i].astype(F32)).astype(self.total.dtype)

    def some(self, first, last):
        def do(i):
            self.add(i)
            self.sends(i).start()

        when(self.sums, lambda: each(first, last, do))

    def own(self):
        def do():
            self.add(0)
            self.here().start()

        when(self.sums, do)

    def end(self):
        chips = self.p.chips
        when(self.gives, lambda: each(0, chips, lambda i: self.across(i).wait_send()))

        def sent():
            self.here().wait()
            each(1, chips, lambda i: self.sends(i).wait_send())

        when(self.sums, sent)

        def came(i):
            when(self.comes(self.p.pair(i)), lambda: self.gets(i).wait_recv())

        each(1, chips, came)

    def steps(self):
        chips = self.p.chips
        return [functools.partial(self.some, 1, chips), self.own]


class Scatter:
    @staticmethod
    def stages(chips, a):
        nz, _, n = grid_of(chips)
        _, t, d = a.shape
        h = t // 2
        return [(2, nz, n, n, h, d), (2, nz, n, h, d), (2, nz, n, h, d), (nz, t, d), (nz, t, d)]

    @staticmethod
    def scratch(chips, a):
        nz, _, n = grid_of(chips)
        _, t, d = a.shape
        h = t // 2
        most = max(n, nz)
        sems = [DMA((2, nz, n, n))] * 2 + [DMA((2, nz, n))] * 2 + [DMA((nz,))] * 2 + [DMA((most,)), DMA]
        return sems + [pltpu.VMEM((most, h, d), a.dtype), pltpu.VMEM((h, d), a.dtype)]

    def __init__(self, place, blocks, stages, held):
        self.p, self.b = place, blocks
        self.got1, self.sum1, self.got2, self.sum2, self.got3 = stages
        (self.s1, self.r1, self.s2, self.r2, self.s3, self.r3, self.load, self.store, self.parts, self.low) = held
        self.h = blocks.shape[1] // 2
        self.n = place.nx

    def chip(self, half, dz, du, dv):
        return self.p.at(dz, dv, du) if half == 0 else self.p.at(dz, du, dv)

    def rows(self, half):
        return pl.ds(half * self.h, self.h)

    def send1(self, half, dz, v, i):
        return remote(
            self.b.at[self.chip(half, dz, i, v), self.rows(half)],
            self.got1.at[half, dz, v, i],
            self.s1.at[half, dz, v, i],
            self.r1.at[half, dz, v, i],
            self.chip(half, 0, i, 0),
            self.p.core,
        )

    def send2(self, half, dz, v):
        return remote(
            self.sum1.at[half, dz, v],
            self.got2.at[half, dz, v],
            self.s2.at[half, dz, v],
            self.r2.at[half, dz, v],
            self.chip(half, 0, 0, v),
            self.p.core,
        )

    def send3(self, dz):
        return remote(
            self.sum2.at[dz], self.got3.at[dz], self.s3.at[dz], self.r3.at[dz], self.p.at(dz, 0, 0), self.p.core
        )

    def fetch(self, refs):
        loads = [pltpu.make_async_copy(r, self.parts.at[i], self.load.at[i]) for i, r in enumerate(refs)]
        for copy in loads:
            copy.start()
        for copy in loads:
            copy.wait()

    def add(self, refs, to):
        self.fetch(refs)
        total = self.parts[0].astype(F32)
        for i in range(1, len(refs)):
            total = total + self.parts[i].astype(F32)
        self.low[...] = total.astype(self.low.dtype)
        move(self.low, to, self.store)

    def order(self):
        nz = self.p.nz
        return [nz // 2] + [k for k in range(1, nz) if k != nz // 2] + [0]

    def begin(self):
        for dz in self.order():
            for half in (0, 1):
                for v in list(range(1, self.n)) + [0]:
                    for i in range(1, self.n):
                        self.send1(half, dz, v, i).start()

    def first(self, dz):
        for half in (0, 1):
            for v in list(range(1, self.n)) + [0]:
                for i in range(1, self.n):
                    self.send1(half, dz, v, i).wait_recv()
                mine = self.b.at[self.chip(half, dz, 0, v), self.rows(half)]
                self.add([mine] + [self.got1.at[half, dz, v, i] for i in range(1, self.n)], self.sum1.at[half, dz, v])
                if v:
                    self.send2(half, dz, v).start()

    def second(self, dz):
        for half in (0, 1):
            for v in range(1, self.n):
                self.send2(half, dz, v).wait_recv()
            parts = [self.sum1.at[half, dz, 0]] + [self.got2.at[half, dz, v] for v in range(1, self.n)]
            self.add(parts, self.sum2.at[dz, self.rows(half)])
        if dz:
            self.send3(dz).start()

    def last(self):
        for dz in range(1, self.p.nz):
            self.send3(dz).wait_recv()
        for half in (0, 1):
            rows = self.rows(half)
            self.fetch([self.sum2.at[0, rows]] + [self.got3.at[dz, rows] for dz in range(1, self.p.nz)])
            self.finish(half)

    def steps(self):
        order = self.order()
        steps = [functools.partial(self.first, order[0])]
        for old, new in zip(order[:-1], order[1:]):
            steps += [functools.partial(self.first, new), functools.partial(self.second, old)]
        return steps + [functools.partial(self.second, order[-1]), self.last]

    def end(self):
        for dz in range(self.p.nz):
            for half in (0, 1):
                for v in range(self.n):
                    for i in range(1, self.n):
                        self.send1(half, dz, v, i).wait_send()
                    if v:
                        self.send2(half, dz, v).wait_send()
            if dz:
                self.send3(dz).wait_send()


class NormBack(Scatter):
    @staticmethod
    def scratch(chips, a):
        d = a.shape[2]
        more = [pltpu.VMEM((2, 8, d), F32), pltpu.VMEM((2, d), F32), pltpu.VMEM((2, d), F32), pltpu.VMEM((chips, 2, d), F32)]
        return Scatter.scratch(chips, a) + more + [DMA((chips,))] * 2 + [DMA((3,))]

    def __init__(self, place, blocks, stages, held, operands, results, features):
        super().__init__(place, blocks, stages, held[:10])
        self.sums, self.mine, self.other, self.slots, self.ss, self.sr, self.pairs = held[10:]
        self.xhat, self.grad, self.gain, self.inverse = operands
        self.input_grad, self.stats = results
        self.features = features

    def begin(self):
        super().begin()
        self.sums[...] = jnp.zeros_like(self.sums)

    def finish(self, half):
        d = self.xhat.shape[1]

        def some(c):
            at = pl.multiple_of(c * 16, 16)
            total = self.parts[0, pl.ds(at, 16)].astype(F32)
            for i in range(1, self.p.nz):
                total = total + self.parts[i, pl.ds(at, 16)].astype(F32)
            rows = pl.ds(pl.multiple_of(half * self.h + c * 16, 16), 16)
            xhat = self.xhat[rows]
            both = total * xhat
            self.sums[0] += both[:8] + both[8:]
            self.sums[1] += total[:8] + total[8:]
            scaled = total * self.gain[...]
            mean = jnp.sum(scaled, 1, keepdims=True) / self.features
            slope = jnp.sum(scaled * xhat, 1, keepdims=True) / self.features
            change = (scaled - mean - xhat * slope) * self.inverse[rows]
            self.input_grad[rows] = self.grad[rows].astype(F32) + change

        each(0, self.h // 16, some)

    def swap_stats(self):
        p = self.p
        return remote(self.mine, self.other, self.pairs.at[0], self.pairs.at[1], p.me, 1 - p.core)

    def share_stats(self, i):
        p = self.p
        return remote(self.mine, self.slots.at[p.me], self.ss.at[i], self.sr.at[i], p.pair(i), p.core)

    def get_stats(self, i):
        p = self.p
        return remote(self.mine, self.slots.at[p.pair(i)], self.ss.at[i], self.sr.at[i], p.pair(i), p.core)

    def stats_out(self):
        self.mine[0:1] = jnp.sum(self.sums[0], 0, keepdims=True)
        self.mine[1:2] = jnp.sum(self.sums[1], 0, keepdims=True)
        self.swap_stats().start()
        self.swap_stats().wait()
        self.mine[...] += self.other[...]
        self.slots[self.p.me] = self.mine[...]
        each(1, self.p.chips, lambda i: self.share_stats(i).start())

    def steps(self):
        return super().steps() + [self.stats_out]

    def end(self):
        super().end()

        def done(i):
            self.share_stats(i).wait_send()
            self.get_stats(i).wait_recv()

        each(1, self.p.chips, done)
        self.stats[...] = self.slots[0]

        def more(c):
            self.stats[...] += self.slots[c]

        each(1, self.p.chips, more)


def return_parts(place, part, out, held):
    tiles = Tiles(out.shape[1], place.chips)
    least, rows, core, me = tiles.least, out.shape[0], place.core, place.me
    n = len(held) // 2

    def at(j, tile, count):
        return part.at[rows_at(j * rows, rows), lanes_at(tile, count)]

    main = Paired(
        place,
        held[:n],
        (
            lambda j: at(j, 0, least),
            lambda j: at(j, least + 1, least),
            lambda j: tiles.cut(out, me, core)[0],
            lambda j: tiles.cut(out, j, core)[0],
        ),
    )
    extra = Paired(
        place,
        held[n:],
        (
            lambda j: at(j, least, 1),
            lambda j: at(j, least, 1),
            lambda j: tiles.cut(out, me, core)[1],
            lambda j: tiles.cut(out, j, core)[1],
        ),
        tiles.more(me, 1 - core),
        tiles.more(me, core),
        lambda j: tiles.more(j, core),
    )
    return [main, extra]


def trade_parts(place, part, out, held):
    rows = out.shape[1]

    def at(j, core):
        return part.at[rows_at((2 * j + core) * rows, rows)]

    views = (
        lambda j: at(j, place.core),
        lambda j: at(j, 1 - place.core),
        lambda j: out.at[place.me],
        lambda j: out.at[j],
    )
    return [Paired(place, held, views)]


def send_kernel(chips, features, counts, *refs):
    blocks, wide, small, xhat, grad, gain, inverse = refs[:7]
    input_grad, stats, wide_out, small_out = refs[7:11]
    stages = refs[11:16]
    norm_held, wide_held, small_held = take(refs[16:], counts)
    place = Place(chips)
    enter(place)
    norm = NormBack(place, blocks, stages, norm_held, (xhat, grad, gain, inverse), (input_grad, stats), features)
    parts = return_parts(place, wide, wide_out, wide_held)
    parts += trade_parts(place, small, small_out, small_held)
    for part in [norm] + parts:
        part.begin()
    for part in parts + [norm]:
        for step in part.steps():
            step()
    for part in [norm] + parts:
        part.end()


def send(chips, number, features, blocks, wide, columns, small, xhat, grad, gain, inverse):
    _, tokens, d = blocks.shape
    rows = d // chips
    least, _ = tile_share(columns // LANES, chips)
    width = small.shape[1]
    held = [
        NormBack.scratch(chips, blocks),
        Paired.scratch(chips, (rows, least * LANES), BF16) + Paired.scratch(chips, (rows, LANES), BF16),
        Paired.scratch(chips, (rows // 2, width), BF16),
    ]
    low = lambda *shape: jax.ShapeDtypeStruct(shape, BF16)
    results = pl.pallas_call(
        functools.partial(send_kernel, chips, features, [len(h) for h in held]),
        in_specs=[ANY] * 3 + [WHOLE] * 4,
        out_specs=[WHOLE] * 2 + [ANY] * 7,
        out_shape=[
            jax.ShapeDtypeStruct((tokens, d), F32),
            jax.ShapeDtypeStruct((2, d), F32),
            low(rows, columns),
            low(chips, rows // 2, width),
        ]
        + [low(*s) for s in Scatter.stages(chips, blocks)],
        scratch_shapes=[s for h in held for s in h],
        compiler_params=pltpu.CompilerParams(collective_id=number, has_side_effects=True, vmem_limit_bytes=48 << 20),
        name="send",
    )(blocks, wide, small, xhat, grad, gain, inverse)
    return results[:4]


def untile_kernel(parts_ref, out_ref, low, high, load, main_sem, extra_sem):
    chips = parts_ref.shape[0]
    rows = out_ref.shape[0]
    core = lax.axis_index("fsdp")
    tiles = Tiles(out_ref.shape[1], chips)
    least = tiles.least

    def bring_in(chip, slot):
        return pltpu.make_async_copy(parts_ref.at[chip], low.at[slot], load.at[slot])

    def stores(chip, slot):
        main, extra = tiles.cut(out_ref, chip, core)
        return (
            pltpu.make_async_copy(high.at[slot, :, lanes_at(0, least)], main, main_sem.at[slot]),
            pltpu.make_async_copy(high.at[slot, :, lanes_at(least, 1)], extra, extra_sem.at[slot]),
        )

    def finish(chip, slot):
        main, extra = stores(chip, slot)
        main.wait()
        pl.when(tiles.more(chip, core))(extra.wait)

    bring_in(0, 0).start()

    def step(chip):
        slot = lax.rem(chip, 2)
        pl.when(chip + 1 < chips)(lambda: bring_in(chip + 1, 1 - slot).start())
        bring_in(chip, slot).wait()
        pl.when(chip >= 2)(lambda: finish(chip - 2, slot))
        high[slot] = low[slot, :rows].astype(F32)
        main, extra = stores(chip, slot)
        main.start()
        pl.when(tiles.more(chip, core))(extra.start)

    each(0, chips, step)
    finish(chips - 2, chips % 2)
    finish(chips - 1, 1 - chips % 2)


def untile(parts, rows, columns):
    _, high, width = parts.shape
    return pl.pallas_call(
        untile_kernel,
        in_specs=[ANY],
        out_specs=ANY,
        out_shape=jax.ShapeDtypeStruct((rows, columns), F32),
        scratch_shapes=[pltpu.VMEM((2, high, width), BF16), pltpu.VMEM((2, rows, width), F32)] + [DMA((2,))] * 3,
        compiler_params=pltpu.CompilerParams(vmem_limit_bytes=24 << 20),
        cost_estimate=pl.CostEstimate(flops=0, transcendentals=0, bytes_accessed=6 * rows * columns),
        name="untile",
    )(parts)


def rotate(values, cosines, sines):
    middle = values.shape[-1] // 2
    turned = jnp.concatenate([-values[..., middle:], values[..., :middle]], -1)
    return values * cosines + turned * sines


def rotate_back(values, cosines, sines):
    middle = values.shape[-1] // 2
    turned = jnp.concatenate([values[..., middle:], -values[..., :middle]], -1)
    return values * cosines + turned * sines


def attend_forward_kernel(lead, q_ref, k_ref, v_ref, low_ref, o_ref, lse_ref, acc, top):
    index = pl.program_id(0)
    heads, rows, _ = q_ref.shape
    outs = []
    for h in range(heads):
        q = q_ref[h]
        acc[...] = jnp.zeros_like(acc)
        top[...] = jnp.full_like(top, MASKED)

        def block(start, masked):
            s = dot(q, k_ref[pl.ds(start, rows), :], ROWS_COLS)
            if masked:
                key = lax.broadcasted_iota(jnp.int32, s.shape, 1)
                query = lax.broadcasted_iota(jnp.int32, s.shape, 0)
                s = jnp.where(key <= query, s, MASKED)
            old = top[...]
            new = jnp.maximum(old, jnp.max(s, 1, keepdims=True))
            p = jnp.exp(s - new).astype(BF16)
            acc[...] = acc[...] * jnp.exp(old - new) + dot(p, v_ref[pl.ds(start, rows), :])
            top[...] = new

        each(0, index, lambda i: block(pl.multiple_of(i * rows, rows), False))
        block(pl.multiple_of(index * rows, rows), True)
        total = acc[...]
        norm = total[:, HEAD : HEAD + 1]
        out = total[:, :HEAD] / norm
        o_ref[h] = out
        outs.append(out.astype(BF16))
        lse = jnp.broadcast_to(top[...] + jnp.log(norm), (rows, LANES))
        lse_ref[h] = lse.T[:1]
    if lead:
        outs = [jnp.zeros((rows, lead), BF16)] + outs
    low_ref[...] = jnp.concatenate(outs, 1)


def attend_forward(q, k, v, lead):
    heads, length, _ = q.shape
    rows = min(512, length)
    width = lead + heads * HEAD
    wide = jnp.concatenate([v, jnp.ones_like(v)], 1)
    return pl.pallas_call(
        functools.partial(attend_forward_kernel, lead),
        grid=(length // rows,),
        in_specs=[
            pl.BlockSpec((heads, rows, HEAD), lambda i: (0, i, 0)),
            pl.BlockSpec((length, HEAD), lambda i: (0, 0)),
            pl.BlockSpec((length, 2 * HEAD), lambda i: (0, 0)),
        ],
        out_specs=[
            pl.BlockSpec((rows, width), lambda i: (i, 0)),
            pl.BlockSpec((heads, rows, HEAD), lambda i: (0, i, 0)),
            pl.BlockSpec((heads, 1, rows), lambda i: (0, 0, i)),
        ],
        out_shape=[
            jax.ShapeDtypeStruct((length, width), BF16),
            jax.ShapeDtypeStruct((heads, length, HEAD), F32),
            jax.ShapeDtypeStruct((heads, 1, length), F32),
        ],
        scratch_shapes=[pltpu.VMEM((rows, 2 * HEAD), F32), pltpu.VMEM((rows, 1), F32)],
        compiler_params=pltpu.CompilerParams(vmem_limit_bytes=40 << 20),
        cost_estimate=pl.CostEstimate(
            flops=2 * heads * length * length * HEAD,
            transcendentals=heads * length * length // 2,
            bytes_accessed=8 * heads * length * HEAD,
        ),
        name="attend_forward",
    )(q, k, wide)


def attend_backward_kernel(q_ref, k_ref, v_ref, g_ref, o_ref, lse_ref, cos_ref, sin_ref, out_ref, acc, dk, dv):
    index = pl.program_id(0)
    heads, rows, _ = q_ref.shape
    scale = HEAD ** (-0.5)

    @pl.when(index == 0)
    def _():
        dk[...] = jnp.zeros_like(dk)
        dv[...] = jnp.zeros_like(dv)
        out_ref[...] = jnp.zeros_like(out_ref)

    here = pl.ds(pl.multiple_of(index * rows, rows), rows)
    cosines, sines = cos_ref[here], sin_ref[here]
    grads = []
    for h in range(heads):
        q = q_ref[h]
        g = g_ref[h]
        lse = lse_ref[h]
        delta = jnp.sum((g.astype(F32) * o_ref[h]).T, 0, keepdims=True)
        acc[...] = jnp.zeros_like(acc)

        def block(start, masked):
            at = pl.ds(start, rows)
            k = k_ref[at, :]
            p = jnp.exp(dot(k, q, ROWS_COLS) - lse)
            if masked:
                key = lax.broadcasted_iota(jnp.int32, p.shape, 0)
                query = lax.broadcasted_iota(jnp.int32, p.shape, 1)
                p = jnp.where(key <= query, p, 0.0)
            dp = dot(v_ref[at, :], g, ROWS_COLS)
            ds = (p * (dp - delta)).astype(BF16)
            dv[at, :] += dot(p.astype(BF16), g)
            dk[at, :] += dot(ds, q)
            acc[...] += dot(ds, k, ROWS_ROWS)

        each(0, index, lambda i: block(pl.multiple_of(i * rows, rows), False))
        block(pl.multiple_of(index * rows, rows), True)
        grads.append(rotate_back(acc[...] * scale, cosines, sines).astype(BF16))
    out_ref[here, : heads * HEAD] = jnp.concatenate(grads, 1)

    @pl.when(index == pl.num_programs(0) - 1)
    def _():
        keys = rotate_back(dk[...], cos_ref[...], sin_ref[...]).astype(BF16)
        both = jnp.concatenate([keys, dv[...].astype(BF16)], 1)
        out_ref[:, heads * HEAD : (heads + 2) * HEAD] = both


def attend_backward(q, k, v, g, o, lse, cosines, sines):
    heads, length, _ = q.shape
    rows = min(512, length)
    width = -(-(heads + 2) * HEAD // LANES) * LANES
    per_query = pl.BlockSpec((heads, rows, HEAD), lambda i: (0, i, 0))
    whole = pl.BlockSpec((length, HEAD), lambda i: (0, 0))
    return pl.pallas_call(
        attend_backward_kernel,
        grid=(length // rows,),
        in_specs=[
            per_query,
            whole,
            whole,
            per_query,
            per_query,
            pl.BlockSpec((heads, 1, rows), lambda i: (0, 0, i)),
            whole,
            whole,
        ],
        out_specs=pl.BlockSpec((length, width), lambda i: (0, 0)),
        out_shape=jax.ShapeDtypeStruct((length, width), BF16),
        scratch_shapes=[pltpu.VMEM((rows, HEAD), F32), pltpu.VMEM((length, HEAD), F32), pltpu.VMEM((length, HEAD), F32)],
        compiler_params=pltpu.CompilerParams(vmem_limit_bytes=56 << 20),
        cost_estimate=pl.CostEstimate(
            flops=5 * heads * length * length * HEAD,
            transcendentals=heads * length * length // 2,
            bytes_accessed=12 * heads * length * HEAD,
        ),
        name="attend_backward",
    )(q, k, v, g, o, lse, cosines, sines)


def flat(ref):
    return ref[...].reshape(ref.shape[0] * ref.shape[1], ref.shape[2])


def chunks(width, most):
    return [(at, min(most, width - at)) for at in range(0, width, most)]


def resident(shape, column=0):
    return pl.BlockSpec(shape, lambda i: (0, column), pipeline_mode=pl.Buffered(1))


def per_row(rows, width):
    return pl.BlockSpec((rows, width), lambda i: (i, 0))


def forward_in_kernel(x_ref, small_ref, wide_ref, cos_ref, sin_ref, q_ref, k_ref, v_ref, hidden_ref, slope_ref):
    x = flat(x_ref)
    cosines, sines = cos_ref[...], sin_ref[...]
    joined = dot(x, small_ref[...])
    heads = q_ref.shape[0]
    for h in range(heads):
        q = rotate(joined[:, h * HEAD : (h + 1) * HEAD], cosines, sines).astype(BF16)
        q_ref[h] = q * HEAD ** (-0.5)
    at = heads * HEAD
    k_ref[...] = rotate(joined[:, at : at + HEAD], cosines, sines).astype(BF16)
    v_ref[...] = joined[:, at + HEAD : at + 2 * HEAD].astype(BF16)
    for at, width in chunks(wide_ref.shape[1], 384):
        up = dot(x, wide_ref[:, at : at + width])
        bell = 0.5 + 0.5 * lax.erf(up * 0.5**0.5)
        hidden_ref[:, at : at + width] = (up * bell).astype(BF16)
        slope = bell + up * jnp.exp(up * up * -0.5) * (2 * jnp.pi) ** (-0.5)
        slope_ref[:, at : at + width] = slope.astype(BF16)


def forward_in(x, small, wide, cosines, sines, heads):
    chips, tokens, d = x.shape
    length = chips * tokens
    step = max(1, 512 // tokens)
    rows = step * tokens
    width = -(-(heads + 2) * HEAD // LANES) * LANES
    n = wide.shape[1]
    return pl.pallas_call(
        forward_in_kernel,
        grid=(chips // step,),
        in_specs=[
            pl.BlockSpec((step, tokens, d), lambda i: (i, 0, 0)),
            resident((d, width)),
            resident((d, n)),
            per_row(rows, HEAD),
            per_row(rows, HEAD),
        ],
        out_specs=[
            pl.BlockSpec((heads, rows, HEAD), lambda i: (0, i, 0)),
            per_row(rows, HEAD),
            per_row(rows, HEAD),
            per_row(rows, n),
            per_row(rows, n),
        ],
        out_shape=[
            jax.ShapeDtypeStruct((heads, length, HEAD), BF16),
            jax.ShapeDtypeStruct((length, HEAD), BF16),
            jax.ShapeDtypeStruct((length, HEAD), BF16),
            jax.ShapeDtypeStruct((length, n), BF16),
            jax.ShapeDtypeStruct((length, n), BF16),
        ],
        compiler_params=pltpu.CompilerParams(vmem_limit_bytes=56 << 20),
        cost_estimate=pl.CostEstimate(
            flops=2 * length * d * (n + width), transcendentals=2 * length * n, bytes_accessed=2 * length * d
        ),
        name="forward_in",
    )(x, small, wide, cosines, sines)


def back_in_kernel(lead, g_ref, dense_ref, down_ref, slope_ref, heads_ref, grad_ref):
    g = flat(g_ref)
    grad = dot(g, dense_ref[...]).astype(BF16)
    for h in range(heads_ref.shape[0]):
        heads_ref[h] = grad[:, lead + h * HEAD : lead + (h + 1) * HEAD]
    for at, width in chunks(down_ref.shape[1], 384):
        part = dot(g, down_ref[:, at : at + width])
        grad_ref[:, at : at + width] = (part * slope_ref[:, at : at + width].astype(F32)).astype(BF16)


def back_in(g, small, lead, heads, down, slope):
    chips, tokens, d = g.shape
    length = chips * tokens
    step = max(1, 512 // tokens)
    rows = step * tokens
    width = lead + heads * HEAD
    n = down.shape[1]
    return pl.pallas_call(
        functools.partial(back_in_kernel, lead),
        grid=(chips // step,),
        in_specs=[
            pl.BlockSpec((step, tokens, d), lambda i: (i, 0, 0)),
            resident((d, width), small.shape[1] // width - 1),
            resident((d, n)),
            per_row(rows, n),
        ],
        out_specs=[pl.BlockSpec((heads, rows, HEAD), lambda i: (0, i, 0)), per_row(rows, n)],
        out_shape=[jax.ShapeDtypeStruct((heads, length, HEAD), BF16), jax.ShapeDtypeStruct((length, n), BF16)],
        compiler_params=pltpu.CompilerParams(vmem_limit_bytes=56 << 20),
        cost_estimate=pl.CostEstimate(
            flops=2 * length * d * (n + width), transcendentals=0, bytes_accessed=2 * length * d
        ),
        name="back_in",
    )(g, small, down, slope)


def out_kernel(a_ref, b_ref, small_ref, wide_ref, out_ref):
    step, tokens, d = out_ref.shape
    a, b = a_ref[...], b_ref[...]
    for at, width in chunks(d, 512):
        part = dot(a, small_ref[at : at + width], ROWS_COLS) + dot(b, wide_ref[at : at + width], ROWS_COLS)
        out_ref[:, :, at : at + width] = part.astype(BF16).reshape(step, tokens, width)


def out_product(a, b, small, column, wide, chips, name):
    length, width = a.shape
    tokens, d = length // chips, small.shape[0]
    step = max(1, 512 // tokens)
    rows = step * tokens
    n = wide.shape[1]
    return pl.pallas_call(
        out_kernel,
        grid=(chips // step,),
        in_specs=[per_row(rows, width), per_row(rows, n), resident((d, width), column), resident((d, n))],
        out_specs=pl.BlockSpec((step, tokens, d), lambda i: (i, 0, 0)),
        out_shape=jax.ShapeDtypeStruct((chips, tokens, d), BF16),
        compiler_params=pltpu.CompilerParams(vmem_limit_bytes=56 << 20),
        cost_estimate=pl.CostEstimate(
            flops=2 * length * d * (n + width), transcendentals=0, bytes_accessed=2 * length * d
        ),
        name=name,
    )(a, b, small, wide)


def weight_kernel(x_ref, a_ref, b_ref, small_ref, wide_ref):
    chips, tokens, width = x_ref.shape
    x = x_ref[...].reshape(chips * tokens, width)
    small_ref[...] = dot(x, a_ref[...], ROWS_ROWS).astype(BF16)
    for at, n in chunks(wide_ref.shape[1], 384):
        wide_ref[:, at : at + n] = dot(x, b_ref[:, at : at + n], ROWS_ROWS).astype(BF16)


def weight_product(x, a, b, name):
    chips, tokens, d = x.shape
    length = chips * tokens
    width = 768 if d % 768 == 0 else 512
    return pl.pallas_call(
        weight_kernel,
        grid=(d // width,),
        in_specs=[pl.BlockSpec((chips, tokens, width), lambda i: (0, 0, i)), resident(a.shape), resident(b.shape)],
        out_specs=[per_row(width, a.shape[1]), per_row(width, b.shape[1])],
        out_shape=[jax.ShapeDtypeStruct((d, a.shape[1]), BF16), jax.ShapeDtypeStruct((d, b.shape[1]), BF16)],
        compiler_params=pltpu.CompilerParams(vmem_limit_bytes=56 << 20),
        cost_estimate=pl.CostEstimate(
            flops=2 * length * d * (a.shape[1] + b.shape[1]), transcendentals=0, bytes_accessed=2 * length * d
        ),
        name=name,
    )(x, a, b)


def share_heads(columns, chips):
    rows, width = columns.shape
    heads = width // HEAD
    most = -(-heads // chips)
    richer = heads - chips * (most - 1)
    cut = richer * most * HEAD
    first = jnp.moveaxis(columns[:, :cut].reshape(rows, richer, most * HEAD), 1, 0)
    if richer == chips:
        return first
    rest = jnp.moveaxis(columns[:, cut:].reshape(rows, chips - richer, (most - 1) * HEAD), 1, 0)
    return jnp.concatenate([first, jnp.pad(rest, ((0, 0), (0, 0), (0, HEAD)))], 0)


def join_heads(parts, heads):
    chips, rows, width = parts.shape
    most = width // HEAD
    richer = heads - chips * (most - 1)
    first = jnp.moveaxis(parts[:richer], 0, 1).reshape(rows, -1)
    if richer == chips:
        return first
    rest = jnp.moveaxis(parts[richer:, :, : width - HEAD], 0, 1).reshape(rows, -1)
    return jnp.concatenate([first, rest], 1)


def swap(values):
    return lax.ppermute(values, "fsdp", [(0, 1), (1, 0)])


def in_order(mine, other, core, axis):
    return jnp.where(
        core == 0,
        jnp.concatenate([mine, other], axis),
        jnp.concatenate([other, mine], axis),
    )


def half_of(values, core, axis):
    first, second = jnp.split(values, 2, axis)
    return jnp.where(core == 0, first, second), jnp.where(core == 0, second, first)


def angles(length):
    inverse_freq = ROPE_BASE ** (-jnp.arange(0, HEAD, 2).astype(F32) / HEAD)
    phases = jnp.arange(length, dtype=jnp.int32).astype(F32)[:, None] * inverse_freq[None, :]
    phases = jnp.concatenate([phases, phases], -1)
    return jnp.cos(phases), jnp.sin(phases)


def body(layer_input, cotangent, norm_gain, norm_bias, qkv_weight, up_weight, dense_weight, down_weight):
    chips = lax.axis_size("ctx")
    core = lax.axis_index("fsdp")
    inputs = layer_input[0].astype(F32)
    tokens, features = inputs.shape
    length = tokens * chips
    heads = features // HEAD
    most = -(-heads // chips)
    qwide = most * HEAD
    rows = qkv_weight.shape[0]
    high = padded_rows(rows)
    wide_columns = up_weight.shape[1]
    lead = (qwide + 2 * HEAD) % LANES

    def pad(values):
        apart = values.reshape(*values.shape[:-1], chips, rows)
        apart = jnp.pad(apart, [(0, 0)] * (apart.ndim - 1) + [(0, high - rows)])
        return apart.reshape(*values.shape[:-1], chips * high)

    def unpad(values):
        apart = values.reshape(*values.shape[:-1], chips, high)[..., :rows]
        return apart.reshape(*values.shape[:-1], features)

    def pad_rows(weight):
        return jnp.pad(weight, ((0, high - rows), (0, 0)))

    center = inputs - jnp.mean(inputs, -1, keepdims=True)
    inverse = lax.rsqrt(jnp.mean(center * center, -1, keepdims=True) + EPS)
    xhat = center * inverse
    normed_low = pad((xhat * norm_gain + norm_bias).astype(BF16))
    grad_low = pad(cotangent[0])

    mine, other = half_of(pad_rows(jnp.concatenate([qkv_weight, dense_weight], 1)), core, 0)
    other = swap(other)
    qkv_columns = qkv_weight.shape[1]
    qkv_rows = in_order(mine[:, :qkv_columns], other[:, :qkv_columns], core, 1)
    dense_rows = in_order(mine[:, qkv_columns:], other[:, qkv_columns:], core, 1)
    blocks = jnp.concatenate(
        [
            share_heads(qkv_rows[:, :features], chips),
            jnp.broadcast_to(qkv_rows[:, features:], (chips, high // 2, 2 * HEAD)),
            share_heads(dense_rows, chips),
        ],
        2,
    )
    normed_all, grad_all, up_cols, down_cols, small = bring(
        chips,
        0,
        "bring",
        (Gather, normed_low),
        (Gather, grad_low),
        (Columns, pad_rows(up_weight)),
        (Columns, pad_rows(down_weight)),
        (Blocks, blocks),
    )

    cosines, sines = angles(length)
    dense_block = small.shape[1] // (lead + qwide) - 1
    queries, keys, values, hidden_low, slope = forward_in(normed_all, small, up_cols, cosines, sines, most)
    attended_low, attention, log_sum = attend_forward(queries, keys, values, lead)
    branch = out_product(attended_low, hidden_low, small, dense_block, down_cols, chips, "forward_out")
    branch, grad_all = lax.optimization_barrier((branch, grad_all))
    branch = unpad(lax.psum_scatter(branch, "ctx", scatter_dimension=0, tiled=False))
    layer_output = (inputs + branch.astype(F32)).astype(BF16)

    least, _ = tile_share(wide_columns // LANES, chips)
    own_wide, one_wide = (least + 1) * LANES, least * LANES
    dense_part, down_part = weight_product(grad_all, attended_low, hidden_low, "late_weights")
    down_part, grad_all = lax.optimization_barrier((down_part, grad_all))
    other = jnp.concatenate([down_part[:, own_wide:], down_part[:, one_wide:own_wide]], 1)
    down_total = (down_part[:, :own_wide] + swap(other)).reshape(chips, high, own_wide)
    down_total = lax.all_to_all(down_total, "ctx", 0, 0, tiled=True)
    down_grad = untile(down_total, rows, wide_columns)
    grad_heads, grad_up = back_in(grad_all, small, lead, most, down_cols, slope)
    grad_joined = attend_backward(queries, keys, values, grad_heads, attention, log_sum, cosines, sines)
    qkv_part, up_part = weight_product(normed_all, grad_joined, grad_up, "early_weights")
    grad_normed = out_product(grad_joined, grad_up, small, 0, up_cols, chips, "back_out")

    small_part = jnp.concatenate([qkv_part[:, : qwide + 2 * HEAD], dense_part[:, lead:]], 1)
    input_grad, stats, up_grad, total = send(
        chips,
        1,
        features,
        grad_normed,
        up_part,
        wide_columns,
        small_part,
        pad(xhat),
        grad_low,
        pad(norm_gain[None]),
        inverse,
    )
    up_grad = up_grad[:rows].astype(F32)
    qkv_rows = jnp.concatenate(
        [
            join_heads(total[:, :, :qwide], heads),
            jnp.sum(total[:, :, qwide : qwide + 2 * HEAD].astype(F32), 0).astype(BF16),
        ],
        1,
    )
    dense_rows = join_heads(total[:, :, qwide + 2 * HEAD :], heads)

    def own_columns(values):
        mine, other = half_of(values, core, 1)
        return in_order(mine, swap(other), core, 0)[:rows].astype(F32)

    stats = unpad(stats)
    return (
        layer_output[None],
        unpad(input_grad)[None],
        stats[0],
        stats[1],
        own_columns(qkv_rows),
        up_grad,
        own_columns(dense_rows),
        down_grad,
    )


def solution(mesh):
    split = P("ctx", "fsdp")
    stream = P("fsdp", "ctx", None)
    return jax.shard_map(
        body,
        mesh=mesh,
        in_specs=(stream, stream, P(), P(), split, split, split, split),
        out_specs=(stream, stream, P(), P(), split, split, split, split),
        check_vma=False,
    )
```

```python
import functools

import jax
import jax.numpy as jnp
from jax import lax
from jax.experimental import pallas as pl
from jax.experimental.pallas import tpu as pltpu
from jax.sharding import PartitionSpec as P

HEADS = 71
HEAD = 64
EPS = 1e-05
ROPE_BASE = 10000.0
MASKED = -1e30
LANES = 128
F32 = jnp.float32
BF16 = jnp.bfloat16
ROWS_COLS = (((1,), (1,)), ((), ()))
ROWS_ROWS = (((0,), (0,)), ((), ()))
MESH = pl.DeviceIdType.MESH
ANY = pl.BlockSpec(memory_space=pl.ANY)
WHOLE = pl.BlockSpec(memory_space=pltpu.VMEM)
DMA = pltpu.SemaphoreType.DMA


def dot(a, b, dims=None):
    if dims is None:
        return jnp.dot(a, b, preferred_element_type=F32)
    return lax.dot_general(a, b, dims, preferred_element_type=F32)


def grid_of(chips):
    return (4, 4, 4) if chips == 64 else (chips // 4, 2, 2)


def padded_rows(rows):
    return -(-rows // 16) * 16


def tile_share(tiles, chips):
    return tiles // chips, tiles % chips


class Place:
    def __init__(self, chips):
        self.chips = chips
        self.nz, self.ny, self.nx = grid_of(chips)
        self.me = lax.axis_index("ctx")
        self.core = lax.axis_index("fsdp")
        self.z = self.me // (self.ny * self.nx)
        self.y = lax.rem(self.me // self.nx, self.ny)
        self.x = lax.rem(self.me, self.nx)

    def at(self, dz, dy, dx):
        z = lax.rem(self.z + dz + self.nz, self.nz)
        y = lax.rem(self.y + dy + self.ny, self.ny)
        x = lax.rem(self.x + dx + self.nx, self.nx)
        return (z * self.ny + y) * self.nx + x

    def pair(self, i):
        return self.me ^ i


def enter(place):
    barrier = pltpu.get_barrier_semaphore()

    def greet(i):
        pl.semaphore_signal(barrier, 1, device_id=(place.pair(i), place.core), device_id_type=MESH)

    each(1, place.chips, greet)
    pl.semaphore_signal(barrier, 1, device_id=(place.me, 1 - place.core), device_id_type=MESH)
    pl.semaphore_wait(barrier, place.chips)


def remote(src, dst, send, recv, chip, core):
    return pltpu.make_async_remote_copy(
        src_ref=src, dst_ref=dst, send_sem=send, recv_sem=recv, device_id=(chip, core), device_id_type=MESH
    )


def each(first, last, do):
    def step(i, carry):
        do(i)
        return carry

    lax.fori_loop(first, last, step, 0)


def when(condition, do):
    if condition is None:
        do()
    else:
        pl.when(condition)(do)


def rows_at(start, count):
    return pl.ds(pl.multiple_of(start, 8), count)


def lanes_at(tile, count):
    return pl.ds(pl.multiple_of(tile * LANES, LANES), count * LANES)


def move(src, dst, sem):
    copy = pltpu.make_async_copy(src, dst, sem)
    copy.start()
    copy.wait()


class Tiles:
    def __init__(self, columns, chips):
        self.chips = chips
        self.least, self.richer = tile_share(columns // LANES, chips)
        assert 0 < self.least and 2 * self.richer <= chips

    def more(self, chip, core):
        return jnp.where(core == 0, chip < self.richer, chip >= self.chips - self.richer)

    def first(self, chip, core):
        late = jnp.maximum(chip - (self.chips - self.richer), 0)
        return self.least * chip + jnp.where(core == 0, jnp.minimum(chip, self.richer), late)

    def cut(self, ref, chip, core):
        start = self.first(chip, core)
        return (
            ref.at[:, lanes_at(start, self.least)],
            ref.at[:, lanes_at(jnp.minimum(start + self.least, self.first(self.chips, core) - 1), 1)],
        )


class Gather:
    @staticmethod
    def shape(chips, a):
        return (chips, *a.shape)

    @staticmethod
    def scratch(chips, a):
        nz, ny, nx = grid_of(chips)
        return [DMA((nz,))] * 2 + [DMA((nz, nx))] * 2 + [DMA((nz, ny))] * 2 + [DMA((nz, nx, ny))] * 4 + [DMA]

    def __init__(self, place, mine, out, sems):
        self.p, self.mine, self.out = place, mine, out
        (self.sl, self.rl, self.sx, self.rx, self.sy, self.ry, self.s1, self.r1, self.s2, self.r2, self.own) = sems
        self.half = mine.shape[0] // 2

    def line(self, k):
        p = self.p
        return remote(self.mine, self.out.at[p.me], self.sl.at[k], self.rl.at[k], p.at(k, 0, 0), p.core)

    def across(self, k, i):
        p = self.p
        b = p.at(-k, 0, 0)
        src = self.mine if k == 0 else self.out.at[b]
        return remote(src, self.out.at[b], self.sx.at[k, i], self.rx.at[k, i], p.at(0, 0, i), p.core)

    def along(self, k, j):
        p = self.p
        b = p.at(-k, 0, 0)
        src = self.mine if k == 0 else self.out.at[b]
        return remote(src, self.out.at[b], self.sy.at[k, j], self.ry.at[k, j], p.at(0, j, 0), p.core)

    def corner1(self, k, i, j):
        p = self.p
        part = self.out.at[p.at(-k, 0, -i), pl.ds(0, self.half)]
        return remote(part, part, self.s1.at[k, i, j], self.r1.at[k, i, j], p.at(0, j, 0), p.core)

    def corner2(self, k, i, j):
        p = self.p
        part = self.out.at[p.at(-k, -j, 0), pl.ds(self.half, self.half)]
        return remote(part, part, self.s2.at[k, i, j], self.r2.at[k, i, j], p.at(0, 0, i), p.core)

    def spread(self, k):
        for i in range(1, self.p.nx):
            self.across(k, i).start()
        for j in range(1, self.p.ny):
            self.along(k, j).start()

    def begin(self):
        for k in range(1, self.p.nz):
            self.line(k).start()
        self.spread(0)
        pltpu.make_async_copy(self.mine, self.out.at[self.p.me], self.own).start()

    def turn(self, k):
        p = self.p
        for i in range(1, p.nx):
            self.across(k, i).wait_recv()
            for j in range(1, p.ny):
                self.corner1(k, i, j).start()
        for j in range(1, p.ny):
            self.along(k, j).wait_recv()
            for i in range(1, p.nx):
                self.corner2(k, i, j).start()

    def steps(self):
        nz = self.p.nz
        order = [1, nz - 1] + list(range(2, nz - 1))

        def come(k):
            self.line(k).wait_recv()
            self.spread(k)

        return (
            [functools.partial(self.turn, 0)]
            + [functools.partial(come, k) for k in order]
            + [functools.partial(self.turn, k) for k in order]
        )

    def end(self):
        p = self.p
        pltpu.make_async_copy(self.mine, self.out.at[p.me], self.own).wait()
        for k in range(p.nz):
            if k:
                self.line(k).wait_send()
            for i in range(1, p.nx):
                self.across(k, i).wait_send()
            for j in range(1, p.ny):
                self.along(k, j).wait_send()
            for i in range(1, p.nx):
                for j in range(1, p.ny):
                    self.corner1(k, i, j).wait()
                    self.corner2(k, i, j).wait()


class Columns:
    @staticmethod
    def shape(chips, a):
        least, _ = tile_share(a.shape[1] // LANES, chips)
        return (chips * a.shape[0], (2 * least + 1) * LANES)

    @staticmethod
    def scratch(chips, a):
        return [DMA((chips,))] * 8 + [pltpu.VMEM((a.shape[0], LANES), a.dtype)]

    def __init__(self, place, weight, out, sems):
        self.p, self.w, self.out = place, weight, out
        self.ms, self.mr, self.es, self.er, self.fs, self.fr, self.gs, self.gr, self.nought = sems
        self.tiles = Tiles(weight.shape[1], place.chips)
        self.rows = weight.shape[0]

    def slots(self, chip, own):
        rows = rows_at(chip * self.rows, self.rows)
        least = self.tiles.least
        return self.out.at[rows, lanes_at(0 if own else least + 1, least)], self.out.at[rows, lanes_at(least, 1)]

    def sends(self, i):
        p = self.p
        chip = p.pair(i)
        (a, b), (c, d) = self.tiles.cut(self.w, chip, p.core), self.slots(p.me, True)
        return (
            remote(a, c, self.ms.at[i], self.mr.at[i], chip, p.core),
            remote(b, d, self.es.at[i], self.er.at[i], chip, p.core),
            self.tiles.more(chip, p.core),
        )

    def gets(self, i):
        p = self.p
        chip = p.pair(i)
        (a, b), (c, d) = self.tiles.cut(self.w, chip, p.core), self.slots(chip, True)
        return (
            remote(a, c, self.ms.at[i], self.mr.at[i], chip, p.core),
            remote(b, d, self.es.at[i], self.er.at[i], chip, p.core),
        )

    def passes(self, i):
        p = self.p
        chip = p.pair(i)
        a, b = self.slots(chip, True)
        if isinstance(i, int) and i == 0:
            a, b = self.tiles.cut(self.w, p.me, p.core)
        c, d = self.slots(chip, False)
        return (
            remote(a, c, self.fs.at[i], self.fr.at[i], p.me, 1 - p.core),
            remote(b, d, self.gs.at[i], self.gr.at[i], p.me, 1 - p.core),
        )

    def here(self):
        p = self.p
        (a, b), (c, d) = self.tiles.cut(self.w, p.me, p.core), self.slots(p.me, True)
        return pltpu.make_async_copy(a, c, self.ms.at[0]), pltpu.make_async_copy(b, d, self.es.at[0])

    def begin(self):
        p = self.p

        def send(i):
            main, extra, more = self.sends(i)
            main.start()
            pl.when(more)(extra.start)

        each(1, p.chips, send)
        own, pass_on = self.here(), self.passes(0)
        own[0].start()
        pass_on[0].start()

        @pl.when(self.tiles.more(p.me, p.core))
        def _():
            own[1].start()
            pass_on[1].start()

    def steps(self):
        return [self.hand_on]

    def hand_on(self):
        p = self.p
        mine = self.tiles.more(p.me, p.core)

        def hand(i):
            main, extra = self.gets(i)
            to_main, to_extra = self.passes(i)
            main.wait_recv()
            to_main.start()

            @pl.when(mine)
            def _():
                extra.wait_recv()
                to_extra.start()

        each(1, p.chips, hand)

    def end(self):
        p = self.p
        mine = self.tiles.more(p.me, p.core)
        theirs = self.tiles.more(p.me, 1 - p.core)
        own = self.here()
        own[0].wait()
        pl.when(mine)(own[1].wait)

        @pl.when(jnp.logical_not(mine | theirs))
        def _():
            self.nought[...] = jnp.zeros_like(self.nought)
            each(0, p.chips, lambda c: move(self.nought, self.slots(c, True)[1], self.es.at[0]))

        def sent(i):
            main, extra, more = self.sends(i)
            main.wait_send()
            pl.when(more)(extra.wait_send)

        each(1, p.chips, sent)

        def handed(i):
            main, extra = self.passes(i)
            main.wait()
            pl.when(mine)(extra.wait_send)
            pl.when(theirs)(extra.wait_recv)

        handed(0)
        each(1, p.chips, handed)


class Blocks:
    @staticmethod
    def shape(chips, a):
        return (chips * 2 * a.shape[1], a.shape[2])

    @staticmethod
    def scratch(chips, a):
        return [DMA((chips,))] * 4

    def __init__(self, place, blocks, out, sems):
        self.p, self.b, self.out = place, blocks, out
        self.s, self.r, self.fs, self.fr = sems
        self.rows = blocks.shape[1]

    def slot(self, chip, core):
        return self.out.at[rows_at((2 * chip + core) * self.rows, self.rows)]

    def sends(self, i):
        p = self.p
        chip = p.pair(i)
        return remote(self.b.at[chip], self.slot(p.me, p.core), self.s.at[i], self.r.at[i], chip, p.core)

    def passes(self, i):
        p = self.p
        part = self.slot(p.pair(i), p.core)
        mine = self.b.at[p.me] if isinstance(i, int) and i == 0 else part
        return remote(mine, part, self.fs.at[i], self.fr.at[i], p.me, 1 - p.core)

    def here(self):
        p = self.p
        return pltpu.make_async_copy(self.b.at[p.me], self.slot(p.me, p.core), self.s.at[0])

    def begin(self):
        each(1, self.p.chips, lambda i: self.sends(i).start())
        self.here().start()
        self.passes(0).start()

    def steps(self):
        return [self.hand_on]

    def hand_on(self):
        def hand(i):
            self.sends(i).wait_recv()
            self.passes(i).start()

        each(1, self.p.chips, hand)

    def end(self):
        p = self.p
        self.here().wait()
        each(1, p.chips, lambda i: self.sends(i).wait_send())
        self.passes(0).wait()
        each(1, p.chips, lambda i: self.passes(i).wait())


def drive(parts):
    for part in parts:
        part.begin()
    todo = [part.steps() for part in parts]
    total = max(len(steps) for steps in todo)
    for at in range(total):
        for steps in todo:
            index = at - (total - len(steps))
            if index >= 0:
                steps[index]()
    for part in parts:
        part.end()


def take(refs, counts):
    out, at = [], 0
    for count in counts:
        out.append(refs[at : at + count])
        at += count
    return out


def bring_kernel(chips, plan, *refs):
    n = len(plan)
    ins, outs, held = refs[:n], refs[n : 2 * n], refs[2 * n :]
    place = Place(chips)
    enter(place)
    held = take(held, [count for _, count in plan])
    drive([kind(place, a, o, h) for (kind, _), a, o, h in zip(plan, ins, outs, held)])


def bring(chips, number, name, *jobs):
    held = [kind.scratch(chips, a) for kind, a in jobs]
    return pl.pallas_call(
        functools.partial(bring_kernel, chips, [(kind, len(h)) for (kind, _), h in zip(jobs, held)]),
        in_specs=[ANY] * len(jobs),
        out_specs=[ANY] * len(jobs),
        out_shape=[jax.ShapeDtypeStruct(kind.shape(chips, a), a.dtype) for kind, a in jobs],
        scratch_shapes=[s for h in held for s in h],
        compiler_params=pltpu.CompilerParams(collective_id=number, has_side_effects=True, vmem_limit_bytes=16 << 20),
        name=name,
    )(*[a for _, a in jobs])


class Paired:
    @staticmethod
    def scratch(chips, shape, dtype):
        return [DMA((chips,))] * 5 + [pltpu.VMEM((chips, *shape), dtype)] * 2

    def __init__(self, place, held, views, gives=None, sums=None, comes=lambda j: None):
        self.p = place
        self.cs, self.cr, self.s, self.r, self.load, self.total, self.stage = held
        self.mine, self.theirs, self.target, self.source = views
        self.gives, self.sums, self.comes = gives, sums, comes

    def across(self, i):
        p = self.p
        return remote(self.theirs(p.pair(i)), self.stage.at[i], self.cs.at[i], self.cr.at[i], p.me, 1 - p.core)

    def fetch(self, i):
        return pltpu.make_async_copy(self.mine(self.p.pair(i)), self.total.at[i], self.load.at[i])

    def sends(self, i):
        p = self.p
        j = p.pair(i)
        return remote(self.total.at[i], self.target(j), self.s.at[i], self.r.at[i], j, p.core)

    def gets(self, i):
        p = self.p
        j = p.pair(i)
        return remote(self.total.at[i], self.source(j), self.s.at[i], self.r.at[i], j, p.core)

    def here(self):
        return pltpu.make_async_copy(self.total.at[0], self.source(self.p.me), self.s.at[0])

    def begin(self):
        chips = self.p.chips
        when(self.gives, lambda: each(0, chips, lambda i: self.across(i).start()))
        when(self.sums, lambda: each(0, chips, lambda i: self.fetch(i).start()))

    def add(self, i):
        self.fetch(i).wait()
        self.across(i).wait_recv()
        self.total[i] = (self.total[i].astype(F32) + self.stage[i].astype(F32)).astype(self.total.dtype)

    def some(self, first, last):
        def do(i):
            self.add(i)
            self.sends(i).start()

        when(self.sums, lambda: each(first, last, do))

    def own(self):
        def do():
            self.add(0)
            self.here().start()

        when(self.sums, do)

    def end(self):
        chips = self.p.chips
        when(self.gives, lambda: each(0, chips, lambda i: self.across(i).wait_send()))

        def sent():
            self.here().wait()
            each(1, chips, lambda i: self.sends(i).wait_send())

        when(self.sums, sent)

        def came(i):
            when(self.comes(self.p.pair(i)), lambda: self.gets(i).wait_recv())

        each(1, chips, came)

    def steps(self):
        chips = self.p.chips
        return [functools.partial(self.some, 1, chips), self.own]


class Scatter:
    @staticmethod
    def stages(chips, a):
        nz, _, n = grid_of(chips)
        _, t, d = a.shape
        h = t // 2
        return [(2, nz, n, n, h, d), (2, nz, n, h, d), (2, nz, n, h, d), (nz, t, d), (nz, t, d)]

    @staticmethod
    def scratch(chips, a):
        nz, _, n = grid_of(chips)
        _, t, d = a.shape
        h = t // 2
        most = max(n, nz)
        sems = [DMA((2, nz, n, n))] * 2 + [DMA((2, nz, n))] * 2 + [DMA((nz,))] * 2 + [DMA((most,)), DMA]
        return sems + [pltpu.VMEM((most, h, d), a.dtype), pltpu.VMEM((h, d), a.dtype)]

    def __init__(self, place, blocks, stages, held):
        self.p, self.b = place, blocks
        self.got1, self.sum1, self.got2, self.sum2, self.got3 = stages
        (self.s1, self.r1, self.s2, self.r2, self.s3, self.r3, self.load, self.store, self.parts, self.low) = held
        self.h = blocks.shape[1] // 2
        self.n = place.nx

    def chip(self, half, dz, du, dv):
        return self.p.at(dz, dv, du) if half == 0 else self.p.at(dz, du, dv)

    def rows(self, half):
        return pl.ds(half * self.h, self.h)

    def send1(self, half, dz, v, i):
        return remote(
            self.b.at[self.chip(half, dz, i, v), self.rows(half)],
            self.got1.at[half, dz, v, i],
            self.s1.at[half, dz, v, i],
            self.r1.at[half, dz, v, i],
            self.chip(half, 0, i, 0),
            self.p.core,
        )

    def send2(self, half, dz, v):
        return remote(
            self.sum1.at[half, dz, v],
            self.got2.at[half, dz, v],
            self.s2.at[half, dz, v],
            self.r2.at[half, dz, v],
            self.chip(half, 0, 0, v),
            self.p.core,
        )

    def send3(self, dz):
        return remote(
            self.sum2.at[dz], self.got3.at[dz], self.s3.at[dz], self.r3.at[dz], self.p.at(dz, 0, 0), self.p.core
        )

    def fetch(self, refs):
        loads = [pltpu.make_async_copy(r, self.parts.at[i], self.load.at[i]) for i, r in enumerate(refs)]
        for copy in loads:
            copy.start()
        for copy in loads:
            copy.wait()

    def add(self, refs, to):
        self.fetch(refs)
        total = self.parts[0].astype(F32)
        for i in range(1, len(refs)):
            total = total + self.parts[i].astype(F32)
        self.low[...] = total.astype(self.low.dtype)
        move(self.low, to, self.store)

    def order(self):
        nz = self.p.nz
        return [nz // 2] + [k for k in range(1, nz) if k != nz // 2] + [0]

    def begin(self):
        for dz in self.order():
            for half in (0, 1):
                for v in list(range(1, self.n)) + [0]:
                    for i in range(1, self.n):
                        self.send1(half, dz, v, i).start()

    def first(self, dz):
        for half in (0, 1):
            for v in list(range(1, self.n)) + [0]:
                for i in range(1, self.n):
                    self.send1(half, dz, v, i).wait_recv()
                mine = self.b.at[self.chip(half, dz, 0, v), self.rows(half)]
                self.add([mine] + [self.got1.at[half, dz, v, i] for i in range(1, self.n)], self.sum1.at[half, dz, v])
                if v:
                    self.send2(half, dz, v).start()

    def second(self, dz):
        for half in (0, 1):
            for v in range(1, self.n):
                self.send2(half, dz, v).wait_recv()
            parts = [self.sum1.at[half, dz, 0]] + [self.got2.at[half, dz, v] for v in range(1, self.n)]
            self.add(parts, self.sum2.at[dz, self.rows(half)])
        if dz:
            self.send3(dz).start()

    def last(self):
        for dz in range(1, self.p.nz):
            self.send3(dz).wait_recv()
        for half in (0, 1):
            rows = self.rows(half)
            self.fetch([self.sum2.at[0, rows]] + [self.got3.at[dz, rows] for dz in range(1, self.p.nz)])
            self.finish(half)

    def steps(self):
        order = self.order()
        steps = [functools.partial(self.first, order[0])]
        for old, new in zip(order[:-1], order[1:]):
            steps += [functools.partial(self.first, new), functools.partial(self.second, old)]
        return steps + [functools.partial(self.second, order[-1]), self.last]

    def end(self):
        for dz in range(self.p.nz):
            for half in (0, 1):
                for v in range(self.n):
                    for i in range(1, self.n):
                        self.send1(half, dz, v, i).wait_send()
                    if v:
                        self.send2(half, dz, v).wait_send()
            if dz:
                self.send3(dz).wait_send()


class NormBack(Scatter):
    @staticmethod
    def scratch(chips, a):
        d = a.shape[2]
        more = [pltpu.VMEM((2, 8, d), F32), pltpu.VMEM((2, d), F32), pltpu.VMEM((2, d), F32), pltpu.VMEM((chips, 2, d), F32)]
        return Scatter.scratch(chips, a) + more + [DMA((chips,))] * 2 + [DMA((3,))]

    def __init__(self, place, blocks, stages, held, operands, results, features):
        super().__init__(place, blocks, stages, held[:10])
        self.sums, self.mine, self.other, self.slots, self.ss, self.sr, self.pairs = held[10:]
        self.xhat, self.grad, self.gain, self.inverse = operands
        self.input_grad, self.stats = results
        self.features = features

    def begin(self):
        super().begin()
        self.sums[...] = jnp.zeros_like(self.sums)

    def finish(self, half):
        d = self.xhat.shape[1]

        def some(c):
            at = pl.multiple_of(c * 16, 16)
            total = self.parts[0, pl.ds(at, 16)].astype(F32)
            for i in range(1, self.p.nz):
                total = total + self.parts[i, pl.ds(at, 16)].astype(F32)
            rows = pl.ds(pl.multiple_of(half * self.h + c * 16, 16), 16)
            xhat = self.xhat[rows]
            both = total * xhat
            self.sums[0] += both[:8] + both[8:]
            self.sums[1] += total[:8] + total[8:]
            scaled = total * self.gain[...]
            mean = jnp.sum(scaled, 1, keepdims=True) / self.features
            slope = jnp.sum(scaled * xhat, 1, keepdims=True) / self.features
            change = (scaled - mean - xhat * slope) * self.inverse[rows]
            self.input_grad[rows] = self.grad[rows].astype(F32) + change

        each(0, self.h // 16, some)

    def swap_stats(self):
        p = self.p
        return remote(self.mine, self.other, self.pairs.at[0], self.pairs.at[1], p.me, 1 - p.core)

    def share_stats(self, i):
        p = self.p
        return remote(self.mine, self.slots.at[p.me], self.ss.at[i], self.sr.at[i], p.pair(i), p.core)

    def get_stats(self, i):
        p = self.p
        return remote(self.mine, self.slots.at[p.pair(i)], self.ss.at[i], self.sr.at[i], p.pair(i), p.core)

    def stats_out(self):
        self.mine[0:1] = jnp.sum(self.sums[0], 0, keepdims=True)
        self.mine[1:2] = jnp.sum(self.sums[1], 0, keepdims=True)
        self.swap_stats().start()
        self.swap_stats().wait()
        self.mine[...] += self.other[...]
        self.slots[self.p.me] = self.mine[...]
        each(1, self.p.chips, lambda i: self.share_stats(i).start())

    def steps(self):
        return super().steps() + [self.stats_out]

    def end(self):
        super().end()

        def done(i):
            self.share_stats(i).wait_send()
            self.get_stats(i).wait_recv()

        each(1, self.p.chips, done)
        self.stats[...] = self.slots[0]

        def more(c):
            self.stats[...] += self.slots[c]

        each(1, self.p.chips, more)


def return_parts(place, part, out, held):
    tiles = Tiles(out.shape[1], place.chips)
    least, rows, core, me = tiles.least, out.shape[0], place.core, place.me
    n = len(held) // 2

    def at(j, tile, count):
        return part.at[rows_at(j * rows, rows), lanes_at(tile, count)]

    main = Paired(
        place,
        held[:n],
        (
            lambda j: at(j, 0, least),
            lambda j: at(j, least + 1, least),
            lambda j: tiles.cut(out, me, core)[0],
            lambda j: tiles.cut(out, j, core)[0],
        ),
    )
    extra = Paired(
        place,
        held[n:],
        (
            lambda j: at(j, least, 1),
            lambda j: at(j, least, 1),
            lambda j: tiles.cut(out, me, core)[1],
            lambda j: tiles.cut(out, j, core)[1],
        ),
        tiles.more(me, 1 - core),
        tiles.more(me, core),
        lambda j: tiles.more(j, core),
    )
    return [main, extra]


def trade_parts(place, part, out, held):
    rows = out.shape[1]

    def at(j, core):
        return part.at[rows_at((2 * j + core) * rows, rows)]

    views = (
        lambda j: at(j, place.core),
        lambda j: at(j, 1 - place.core),
        lambda j: out.at[place.me],
        lambda j: out.at[j],
    )
    return [Paired(place, held, views)]


def send_kernel(chips, features, counts, *refs):
    blocks, wide, small, xhat, grad, gain, inverse = refs[:7]
    input_grad, stats, wide_out, small_out = refs[7:11]
    stages = refs[11:16]
    norm_held, wide_held, small_held = take(refs[16:], counts)
    place = Place(chips)
    enter(place)
    norm = NormBack(place, blocks, stages, norm_held, (xhat, grad, gain, inverse), (input_grad, stats), features)
    parts = return_parts(place, wide, wide_out, wide_held)
    parts += trade_parts(place, small, small_out, small_held)
    for part in [norm] + parts:
        part.begin()
    for part in parts + [norm]:
        for step in part.steps():
            step()
    for part in [norm] + parts:
        part.end()


def send(chips, number, features, blocks, wide, columns, small, xhat, grad, gain, inverse):
    _, tokens, d = blocks.shape
    rows = d // chips
    least, _ = tile_share(columns // LANES, chips)
    width = small.shape[1]
    held = [
        NormBack.scratch(chips, blocks),
        Paired.scratch(chips, (rows, least * LANES), BF16) + Paired.scratch(chips, (rows, LANES), BF16),
        Paired.scratch(chips, (rows // 2, width), BF16),
    ]
    low = lambda *shape: jax.ShapeDtypeStruct(shape, BF16)
    results = pl.pallas_call(
        functools.partial(send_kernel, chips, features, [len(h) for h in held]),
        in_specs=[ANY] * 3 + [WHOLE] * 4,
        out_specs=[WHOLE] * 2 + [ANY] * 7,
        out_shape=[
            jax.ShapeDtypeStruct((tokens, d), F32),
            jax.ShapeDtypeStruct((2, d), F32),
            low(rows, columns),
            low(chips, rows // 2, width),
        ]
        + [low(*s) for s in Scatter.stages(chips, blocks)],
        scratch_shapes=[s for h in held for s in h],
        compiler_params=pltpu.CompilerParams(collective_id=number, has_side_effects=True, vmem_limit_bytes=48 << 20),
        name="send",
    )(blocks, wide, small, xhat, grad, gain, inverse)
    return results[:4]


def untile_kernel(parts_ref, out_ref, low, high, load, main_sem, extra_sem):
    chips = parts_ref.shape[0]
    rows = out_ref.shape[0]
    core = lax.axis_index("fsdp")
    tiles = Tiles(out_ref.shape[1], chips)
    least = tiles.least

    def bring_in(chip, slot):
        return pltpu.make_async_copy(parts_ref.at[chip], low.at[slot], load.at[slot])

    def stores(chip, slot):
        main, extra = tiles.cut(out_ref, chip, core)
        return (
            pltpu.make_async_copy(high.at[slot, :, lanes_at(0, least)], main, main_sem.at[slot]),
            pltpu.make_async_copy(high.at[slot, :, lanes_at(least, 1)], extra, extra_sem.at[slot]),
        )

    def finish(chip, slot):
        main, extra = stores(chip, slot)
        main.wait()
        pl.when(tiles.more(chip, core))(extra.wait)

    bring_in(0, 0).start()

    def step(chip):
        slot = lax.rem(chip, 2)
        pl.when(chip + 1 < chips)(lambda: bring_in(chip + 1, 1 - slot).start())
        bring_in(chip, slot).wait()
        pl.when(chip >= 2)(lambda: finish(chip - 2, slot))
        high[slot] = low[slot, :rows].astype(F32)
        main, extra = stores(chip, slot)
        main.start()
        pl.when(tiles.more(chip, core))(extra.start)

    each(0, chips, step)
    finish(chips - 2, chips % 2)
    finish(chips - 1, 1 - chips % 2)


def untile(parts, rows, columns):
    _, high, width = parts.shape
    return pl.pallas_call(
        untile_kernel,
        in_specs=[ANY],
        out_specs=ANY,
        out_shape=jax.ShapeDtypeStruct((rows, columns), F32),
        scratch_shapes=[pltpu.VMEM((2, high, width), BF16), pltpu.VMEM((2, rows, width), F32)] + [DMA((2,))] * 3,
        compiler_params=pltpu.CompilerParams(vmem_limit_bytes=24 << 20),
        cost_estimate=pl.CostEstimate(flops=0, transcendentals=0, bytes_accessed=6 * rows * columns),
        name="untile",
    )(parts)


def rotate(values, cosines, sines):
    middle = values.shape[-1] // 2
    turned = jnp.concatenate([-values[..., middle:], values[..., :middle]], -1)
    return values * cosines + turned * sines


def rotate_back(values, cosines, sines):
    middle = values.shape[-1] // 2
    turned = jnp.concatenate([values[..., middle:], -values[..., :middle]], -1)
    return values * cosines + turned * sines


def attend_backward_kernel(q_ref, k_ref, v_ref, g_ref, o_ref, lse_ref, cos_ref, sin_ref, out_ref, acc, dk, dv):
    index = pl.program_id(0)
    heads, rows, _ = q_ref.shape
    scale = HEAD ** (-0.5)

    @pl.when(index == 0)
    def _():
        dk[...] = jnp.zeros_like(dk)
        dv[...] = jnp.zeros_like(dv)
        out_ref[...] = jnp.zeros_like(out_ref)

    here = pl.ds(pl.multiple_of(index * rows, rows), rows)
    cosines, sines = cos_ref[here], sin_ref[here]
    grads = []
    for h in range(heads):
        q = q_ref[h]
        g = g_ref[h]
        lse = lse_ref[h]
        delta = jnp.sum((g.astype(F32) * o_ref[h]).T, 0, keepdims=True)
        acc[...] = jnp.zeros_like(acc)

        def block(start, masked):
            at = pl.ds(start, rows)
            k = k_ref[at, :]
            p = jnp.exp(dot(k, q, ROWS_COLS) - lse)
            if masked:
                key = lax.broadcasted_iota(jnp.int32, p.shape, 0)
                query = lax.broadcasted_iota(jnp.int32, p.shape, 1)
                p = jnp.where(key <= query, p, 0.0)
            dp = dot(v_ref[at, :], g, ROWS_COLS)
            ds = (p * (dp - delta)).astype(BF16)
            dv[at, :] += dot(p.astype(BF16), g)
            dk[at, :] += dot(ds, q)
            acc[...] += dot(ds, k, ROWS_ROWS)

        each(0, index, lambda i: block(pl.multiple_of(i * rows, rows), False))
        block(pl.multiple_of(index * rows, rows), True)
        grads.append(rotate_back(acc[...] * scale, cosines, sines).astype(BF16))
    out_ref[here, : heads * HEAD] = jnp.concatenate(grads, 1)

    @pl.when(index == pl.num_programs(0) - 1)
    def _():
        keys = rotate_back(dk[...], cos_ref[...], sin_ref[...]).astype(BF16)
        both = jnp.concatenate([keys, dv[...].astype(BF16)], 1)
        out_ref[:, heads * HEAD : (heads + 2) * HEAD] = both


def attend_backward(q, k, v, g, o, lse, cosines, sines):
    heads, length, _ = q.shape
    rows = min(512, length)
    width = -(-(heads + 2) * HEAD // LANES) * LANES
    per_query = pl.BlockSpec((heads, rows, HEAD), lambda i: (0, i, 0))
    whole = pl.BlockSpec((length, HEAD), lambda i: (0, 0))
    return pl.pallas_call(
        attend_backward_kernel,
        grid=(length // rows,),
        in_specs=[
            per_query,
            whole,
            whole,
            per_query,
            per_query,
            pl.BlockSpec((heads, 1, rows), lambda i: (0, 0, i)),
            whole,
            whole,
        ],
        out_specs=pl.BlockSpec((length, width), lambda i: (0, 0)),
        out_shape=jax.ShapeDtypeStruct((length, width), BF16),
        scratch_shapes=[pltpu.VMEM((rows, HEAD), F32), pltpu.VMEM((length, HEAD), F32), pltpu.VMEM((length, HEAD), F32)],
        compiler_params=pltpu.CompilerParams(vmem_limit_bytes=56 << 20),
        cost_estimate=pl.CostEstimate(
            flops=5 * heads * length * length * HEAD,
            transcendentals=heads * length * length // 2,
            bytes_accessed=12 * heads * length * HEAD,
        ),
        name="attend_backward",
    )(q, k, v, g, o, lse, cosines, sines)


def flat(ref):
    return ref[...].reshape(ref.shape[0] * ref.shape[1], ref.shape[2])


def chunks(width, most):
    return [(at, min(most, width - at)) for at in range(0, width, most)]


def resident(shape, column=0):
    return pl.BlockSpec(shape, lambda i: (0, column), pipeline_mode=pl.Buffered(1))


def per_row(rows, width):
    return pl.BlockSpec((rows, width), lambda i: (i, 0))


def forward_kernel(chips, plan, lead, events, *refs):
    n = len(plan)
    x_ref, small_ref, wide_ref, cos_ref, sin_ref = refs[:5]
    ins, refs = refs[5 : 5 + n], refs[5 + n :]
    q_out, k_out, v_out, hidden_ref, slope_ref, low_ref, o_ref, lse_ref = refs[:8]
    outs, refs = refs[8 : 8 + n], refs[8 + n :]
    q_all, k_all, v_all, acc, top = refs[:5]
    held = take(refs[5:], [count for _, count in plan])
    step = pl.program_id(0)
    half = pl.num_programs(0) // 2
    heads, rows, _ = q_out.shape
    place = Place(chips)
    parts = [kind(place, a, o, h) for (kind, _), a, o, h in zip(plan, ins, outs, held)]

    @pl.when(step == 0)
    def _():
        enter(place)
        for part in parts:
            part.begin()

    @pl.when(step < half)
    def _():
        here = pl.ds(pl.multiple_of(step * rows, rows), rows)
        x = flat(x_ref)
        cosines, sines = cos_ref[...], sin_ref[...]
        joined = dot(x, small_ref[...])
        for h in range(heads):
            q = rotate(joined[:, h * HEAD : (h + 1) * HEAD], cosines, sines).astype(BF16) * HEAD ** (-0.5)
            q_out[h] = q
            q_all[h, here] = q
        at = heads * HEAD
        k = rotate(joined[:, at : at + HEAD], cosines, sines).astype(BF16)
        v = joined[:, at + HEAD : at + 2 * HEAD].astype(BF16)
        k_out[...] = k
        v_out[...] = v
        k_all[here] = k
        v_all[here] = jnp.concatenate([v, jnp.ones_like(v)], 1)
        for at, width in chunks(wide_ref.shape[1], 384):
            up = dot(x, wide_ref[:, at : at + width])
            bell = 0.5 + 0.5 * lax.erf(up * 0.5**0.5)
            hidden_ref[:, at : at + width] = (up * bell).astype(BF16)
            slope = bell + up * jnp.exp(up * up * -0.5) * (2 * jnp.pi) ** (-0.5)
            slope_ref[:, at : at + width] = slope.astype(BF16)

    @pl.when(step >= half)
    def _():
        index = step - half
        here = pl.ds(pl.multiple_of(index * rows, rows), rows)
        lows = []
        for h in range(heads):
            q = q_all[h, here]
            acc[...] = jnp.zeros_like(acc)
            top[...] = jnp.full_like(top, MASKED)

            def block(start, masked):
                s = dot(q, k_all[pl.ds(start, rows), :], ROWS_COLS)
                if masked:
                    key = lax.broadcasted_iota(jnp.int32, s.shape, 1)
                    query = lax.broadcasted_iota(jnp.int32, s.shape, 0)
                    s = jnp.where(key <= query, s, MASKED)
                old = top[...]
                new = jnp.maximum(old, jnp.max(s, 1, keepdims=True))
                p = jnp.exp(s - new).astype(BF16)
                acc[...] = acc[...] * jnp.exp(old - new) + dot(p, v_all[pl.ds(start, rows), :])
                top[...] = new

            each(0, index, lambda i: block(pl.multiple_of(i * rows, rows), False))
            block(pl.multiple_of(index * rows, rows), True)
            total = acc[...]
            norm = total[:, HEAD : HEAD + 1]
            out = total[:, :HEAD] / norm
            o_ref[h] = out
            lows.append(out.astype(BF16))
            lse = jnp.broadcast_to(top[...] + jnp.log(norm), (rows, LANES))
            lse_ref[h] = lse.T[:1]
        if lead:
            lows = [jnp.zeros((rows, lead), BF16)] + lows
        low_ref[...] = jnp.concatenate(lows, 1)

    todo = []
    longest = max(len(part.steps()) for part in parts)
    for at in range(longest):
        for part in parts:
            steps = part.steps()
            index = at - (longest - len(steps))
            if index >= 0:
                todo.append(steps[index])
    cuts = [0, *[c for _, c in events], len(todo)]
    for (back, _), first, last in zip([*events, (0, None)], cuts[:-1], cuts[1:]):

        @pl.when(step == pl.num_programs(0) - 1 - back)
        def _():
            for do in todo[first:last]:
                do()

    @pl.when(step == pl.num_programs(0) - 1)
    def _():
        for part in parts:
            part.end()


def forward(x, small, wide, cosines, sines, heads, lead, number, jobs):
    chips, tokens, d = x.shape
    length = chips * tokens
    step = max(1, 512 // tokens)
    rows = step * tokens
    half = chips // step
    width = -(-(heads + 2) * HEAD // LANES) * LANES
    n = wide.shape[1]
    low = lead + heads * HEAD
    held = [kind.scratch(chips, a) for kind, a in jobs]
    plan = [(kind, len(h)) for (kind, _), h in zip(jobs, held)]
    early = lambda i: jnp.minimum(i, half - 1)
    late = lambda i: jnp.maximum(i - half, 0)
    first = lambda w: pl.BlockSpec((rows, w), lambda i: (early(i), 0))
    events = ((4, 1), (2, 3), (1, 4))
    results = pl.pallas_call(
        functools.partial(forward_kernel, chips, plan, lead, events),
        grid=(2 * half,),
        in_specs=[
            pl.BlockSpec((step, tokens, d), lambda i: (early(i), 0, 0)),
            resident((d, width)),
            resident((d, n)),
            first(HEAD),
            first(HEAD),
        ]
        + [ANY] * len(jobs),
        out_specs=[
            pl.BlockSpec((heads, rows, HEAD), lambda i: (0, early(i), 0)),
            first(HEAD),
            first(HEAD),
            first(n),
            first(n),
            pl.BlockSpec((rows, low), lambda i: (late(i), 0)),
            pl.BlockSpec((heads, rows, HEAD), lambda i: (0, late(i), 0)),
            pl.BlockSpec((heads, 1, rows), lambda i: (0, 0, late(i))),
        ]
        + [ANY] * len(jobs),
        out_shape=[
            jax.ShapeDtypeStruct((heads, length, HEAD), BF16),
            jax.ShapeDtypeStruct((length, HEAD), BF16),
            jax.ShapeDtypeStruct((length, HEAD), BF16),
            jax.ShapeDtypeStruct((length, n), BF16),
            jax.ShapeDtypeStruct((length, n), BF16),
            jax.ShapeDtypeStruct((length, low), BF16),
            jax.ShapeDtypeStruct((heads, length, HEAD), F32),
            jax.ShapeDtypeStruct((heads, 1, length), F32),
        ]
        + [jax.ShapeDtypeStruct(kind.shape(chips, a), a.dtype) for kind, a in jobs],
        scratch_shapes=[
            pltpu.VMEM((heads, length, HEAD), BF16),
            pltpu.VMEM((length, HEAD), BF16),
            pltpu.VMEM((length, 2 * HEAD), BF16),
            pltpu.VMEM((rows, 2 * HEAD), F32),
            pltpu.VMEM((rows, 1), F32),
        ]
        + [s for h in held for s in h],
        compiler_params=pltpu.CompilerParams(collective_id=number, has_side_effects=True, vmem_limit_bytes=58 << 20),
        cost_estimate=pl.CostEstimate(
            flops=2 * length * d * (n + width) + 2 * heads * length * length * HEAD,
            transcendentals=2 * length * n + heads * length * length // 2,
            bytes_accessed=2 * length * d,
        ),
        name="forward",
    )(x, small, wide, cosines, sines, *[a for _, a in jobs])
    return results[:8], results[8:]


def back_in_kernel(lead, g_ref, dense_ref, down_ref, slope_ref, heads_ref, grad_ref):
    g = flat(g_ref)
    grad = dot(g, dense_ref[...]).astype(BF16)
    for h in range(heads_ref.shape[0]):
        heads_ref[h] = grad[:, lead + h * HEAD : lead + (h + 1) * HEAD]
    for at, width in chunks(down_ref.shape[1], 384):
        part = dot(g, down_ref[:, at : at + width])
        grad_ref[:, at : at + width] = (part * slope_ref[:, at : at + width].astype(F32)).astype(BF16)


def back_in(g, small, lead, heads, down, slope):
    chips, tokens, d = g.shape
    length = chips * tokens
    step = max(1, 512 // tokens)
    rows = step * tokens
    width = lead + heads * HEAD
    n = down.shape[1]
    return pl.pallas_call(
        functools.partial(back_in_kernel, lead),
        grid=(chips // step,),
        in_specs=[
            pl.BlockSpec((step, tokens, d), lambda i: (i, 0, 0)),
            resident((d, width), small.shape[1] // width - 1),
            resident((d, n)),
            per_row(rows, n),
        ],
        out_specs=[pl.BlockSpec((heads, rows, HEAD), lambda i: (0, i, 0)), per_row(rows, n)],
        out_shape=[jax.ShapeDtypeStruct((heads, length, HEAD), BF16), jax.ShapeDtypeStruct((length, n), BF16)],
        compiler_params=pltpu.CompilerParams(vmem_limit_bytes=56 << 20),
        cost_estimate=pl.CostEstimate(
            flops=2 * length * d * (n + width), transcendentals=0, bytes_accessed=2 * length * d
        ),
        name="back_in",
    )(g, small, down, slope)


def out_kernel(a_ref, b_ref, small_ref, wide_ref, out_ref):
    step, tokens, d = out_ref.shape
    a, b = a_ref[...], b_ref[...]
    for at, width in chunks(d, 512):
        part = dot(a, small_ref[at : at + width], ROWS_COLS) + dot(b, wide_ref[at : at + width], ROWS_COLS)
        out_ref[:, :, at : at + width] = part.astype(BF16).reshape(step, tokens, width)


def out_product(a, b, small, column, wide, chips, name):
    length, width = a.shape
    tokens, d = length // chips, small.shape[0]
    step = max(1, 512 // tokens)
    rows = step * tokens
    n = wide.shape[1]
    return pl.pallas_call(
        out_kernel,
        grid=(chips // step,),
        in_specs=[per_row(rows, width), per_row(rows, n), resident((d, width), column), resident((d, n))],
        out_specs=pl.BlockSpec((step, tokens, d), lambda i: (i, 0, 0)),
        out_shape=jax.ShapeDtypeStruct((chips, tokens, d), BF16),
        compiler_params=pltpu.CompilerParams(vmem_limit_bytes=56 << 20),
        cost_estimate=pl.CostEstimate(
            flops=2 * length * d * (n + width), transcendentals=0, bytes_accessed=2 * length * d
        ),
        name=name,
    )(a, b, small, wide)


def weight_kernel(x_ref, a_ref, b_ref, small_ref, wide_ref):
    chips, tokens, width = x_ref.shape
    x = x_ref[...].reshape(chips * tokens, width)
    small_ref[...] = dot(x, a_ref[...], ROWS_ROWS).astype(BF16)
    for at, n in chunks(wide_ref.shape[1], 384):
        wide_ref[:, at : at + n] = dot(x, b_ref[:, at : at + n], ROWS_ROWS).astype(BF16)


def weight_product(x, a, b, name):
    chips, tokens, d = x.shape
    length = chips * tokens
    width = 768 if d % 768 == 0 else 512
    return pl.pallas_call(
        weight_kernel,
        grid=(d // width,),
        in_specs=[pl.BlockSpec((chips, tokens, width), lambda i: (0, 0, i)), resident(a.shape), resident(b.shape)],
        out_specs=[per_row(width, a.shape[1]), per_row(width, b.shape[1])],
        out_shape=[jax.ShapeDtypeStruct((d, a.shape[1]), BF16), jax.ShapeDtypeStruct((d, b.shape[1]), BF16)],
        compiler_params=pltpu.CompilerParams(vmem_limit_bytes=56 << 20),
        cost_estimate=pl.CostEstimate(
            flops=2 * length * d * (a.shape[1] + b.shape[1]), transcendentals=0, bytes_accessed=2 * length * d
        ),
        name=name,
    )(x, a, b)


def share_heads(columns, chips):
    rows, width = columns.shape
    heads = width // HEAD
    most = -(-heads // chips)
    richer = heads - chips * (most - 1)
    cut = richer * most * HEAD
    first = jnp.moveaxis(columns[:, :cut].reshape(rows, richer, most * HEAD), 1, 0)
    if richer == chips:
        return first
    rest = jnp.moveaxis(columns[:, cut:].reshape(rows, chips - richer, (most - 1) * HEAD), 1, 0)
    return jnp.concatenate([first, jnp.pad(rest, ((0, 0), (0, 0), (0, HEAD)))], 0)


def join_heads(parts, heads):
    chips, rows, width = parts.shape
    most = width // HEAD
    richer = heads - chips * (most - 1)
    first = jnp.moveaxis(parts[:richer], 0, 1).reshape(rows, -1)
    if richer == chips:
        return first
    rest = jnp.moveaxis(parts[richer:, :, : width - HEAD], 0, 1).reshape(rows, -1)
    return jnp.concatenate([first, rest], 1)


def swap(values):
    return lax.ppermute(values, "fsdp", [(0, 1), (1, 0)])


def in_order(mine, other, core, axis):
    return jnp.where(
        core == 0,
        jnp.concatenate([mine, other], axis),
        jnp.concatenate([other, mine], axis),
    )


def half_of(values, core, axis):
    first, second = jnp.split(values, 2, axis)
    return jnp.where(core == 0, first, second), jnp.where(core == 0, second, first)


def angles(length):
    inverse_freq = ROPE_BASE ** (-jnp.arange(0, HEAD, 2).astype(F32) / HEAD)
    phases = jnp.arange(length, dtype=jnp.int32).astype(F32)[:, None] * inverse_freq[None, :]
    phases = jnp.concatenate([phases, phases], -1)
    return jnp.cos(phases), jnp.sin(phases)


def body(layer_input, cotangent, norm_gain, norm_bias, qkv_weight, up_weight, dense_weight, down_weight):
    chips = lax.axis_size("ctx")
    core = lax.axis_index("fsdp")
    inputs = layer_input[0].astype(F32)
    tokens, features = inputs.shape
    length = tokens * chips
    heads = features // HEAD
    most = -(-heads // chips)
    qwide = most * HEAD
    rows = qkv_weight.shape[0]
    high = padded_rows(rows)
    wide_columns = up_weight.shape[1]
    lead = (qwide + 2 * HEAD) % LANES

    def pad(values):
        apart = values.reshape(*values.shape[:-1], chips, rows)
        apart = jnp.pad(apart, [(0, 0)] * (apart.ndim - 1) + [(0, high - rows)])
        return apart.reshape(*values.shape[:-1], chips * high)

    def unpad(values):
        apart = values.reshape(*values.shape[:-1], chips, high)[..., :rows]
        return apart.reshape(*values.shape[:-1], features)

    def pad_rows(weight):
        return jnp.pad(weight, ((0, high - rows), (0, 0)))

    center = inputs - jnp.mean(inputs, -1, keepdims=True)
    inverse = lax.rsqrt(jnp.mean(center * center, -1, keepdims=True) + EPS)
    xhat = center * inverse
    normed_low = pad((xhat * norm_gain + norm_bias).astype(BF16))
    grad_low = pad(cotangent[0])

    mine, other = half_of(pad_rows(jnp.concatenate([qkv_weight, dense_weight], 1)), core, 0)
    other = swap(other)
    qkv_columns = qkv_weight.shape[1]
    qkv_rows = in_order(mine[:, :qkv_columns], other[:, :qkv_columns], core, 1)
    dense_rows = in_order(mine[:, qkv_columns:], other[:, qkv_columns:], core, 1)
    blocks = jnp.concatenate(
        [
            share_heads(qkv_rows[:, :features], chips),
            jnp.broadcast_to(qkv_rows[:, features:], (chips, high // 2, 2 * HEAD)),
            share_heads(dense_rows, chips),
        ],
        2,
    )
    normed_all, up_cols, small = bring(
        chips, 0, "bring", (Gather, normed_low), (Columns, pad_rows(up_weight)), (Blocks, blocks)
    )

    cosines, sines = angles(length)
    dense_block = small.shape[1] // (lead + qwide) - 1
    (queries, keys, values, hidden_low, slope, attended_low, attention, log_sum), (grad_all, down_cols) = forward(
        normed_all,
        small,
        up_cols,
        cosines,
        sines,
        most,
        lead,
        2,
        [(Gather, grad_low), (Columns, pad_rows(down_weight))],
    )
    branch = out_product(attended_low, hidden_low, small, dense_block, down_cols, chips, "forward_out")
    branch, grad_all = lax.optimization_barrier((branch, grad_all))
    branch = unpad(lax.psum_scatter(branch, "ctx", scatter_dimension=0, tiled=False))
    layer_output = (inputs + branch.astype(F32)).astype(BF16)

    least, _ = tile_share(wide_columns // LANES, chips)
    own_wide, one_wide = (least + 1) * LANES, least * LANES
    dense_part, down_part = weight_product(grad_all, attended_low, hidden_low, "late_weights")
    down_part, grad_all = lax.optimization_barrier((down_part, grad_all))
    other = jnp.concatenate([down_part[:, own_wide:], down_part[:, one_wide:own_wide]], 1)
    down_total = (down_part[:, :own_wide] + swap(other)).reshape(chips, high, own_wide)
    down_total = lax.all_to_all(down_total, "ctx", 0, 0, tiled=True)
    down_grad = untile(down_total, rows, wide_columns)
    grad_heads, grad_up = back_in(grad_all, small, lead, most, down_cols, slope)
    grad_joined = attend_backward(queries, keys, values, grad_heads, attention, log_sum, cosines, sines)
    qkv_part, up_part = weight_product(normed_all, grad_joined, grad_up, "early_weights")
    grad_normed = out_product(grad_joined, grad_up, small, 0, up_cols, chips, "back_out")

    small_part = jnp.concatenate([qkv_part[:, : qwide + 2 * HEAD], dense_part[:, lead:]], 1)
    input_grad, stats, up_grad, total = send(
        chips,
        1,
        features,
        grad_normed,
        up_part,
        wide_columns,
        small_part,
        pad(xhat),
        grad_low,
        pad(norm_gain[None]),
        inverse,
    )
    up_grad = up_grad[:rows].astype(F32)
    qkv_rows = jnp.concatenate(
        [
            join_heads(total[:, :, :qwide], heads),
            jnp.sum(total[:, :, qwide : qwide + 2 * HEAD].astype(F32), 0).astype(BF16),
        ],
        1,
    )
    dense_rows = join_heads(total[:, :, qwide + 2 * HEAD :], heads)

    def own_columns(values):
        mine, other = half_of(values, core, 1)
        return in_order(mine, swap(other), core, 0)[:rows].astype(F32)

    stats = unpad(stats)
    return (
        layer_output[None],
        unpad(input_grad)[None],
        stats[0],
        stats[1],
        own_columns(qkv_rows),
        up_grad,
        own_columns(dense_rows),
        down_grad,
    )


def solution(mesh):
    split = P("ctx", "fsdp")
    stream = P("fsdp", "ctx", None)
    return jax.shard_map(
        body,
        mesh=mesh,
        in_specs=(stream, stream, P(), P(), split, split, split, split),
        out_specs=(stream, stream, P(), P(), split, split, split, split),
        check_vma=False,
    )
```

```python
import functools

import jax
import jax.numpy as jnp
from jax import lax
from jax.experimental import pallas as pl
from jax.experimental.pallas import tpu as pltpu
from jax.sharding import PartitionSpec as P

HEADS = 71
HEAD = 64
EPS = 1e-05
ROPE_BASE = 10000.0
MASKED = -1e30
LANES = 128
F32 = jnp.float32
BF16 = jnp.bfloat16
ROWS_COLS = (((1,), (1,)), ((), ()))
ROWS_ROWS = (((0,), (0,)), ((), ()))
MESH = pl.DeviceIdType.MESH
ANY = pl.BlockSpec(memory_space=pl.ANY)
WHOLE = pl.BlockSpec(memory_space=pltpu.VMEM)
DMA = pltpu.SemaphoreType.DMA


def dot(a, b, dims=None):
    if dims is None:
        return jnp.dot(a, b, preferred_element_type=F32)
    return lax.dot_general(a, b, dims, preferred_element_type=F32)


def grid_of(chips):
    return (4, 4, 4) if chips == 64 else (chips // 4, 2, 2)


def padded_rows(rows):
    return -(-rows // 16) * 16


def tile_share(tiles, chips):
    return tiles // chips, tiles % chips


class Place:
    def __init__(self, chips):
        self.chips = chips
        self.nz, self.ny, self.nx = grid_of(chips)
        self.me = lax.axis_index("ctx")
        self.core = lax.axis_index("fsdp")
        self.z = self.me // (self.ny * self.nx)
        self.y = lax.rem(self.me // self.nx, self.ny)
        self.x = lax.rem(self.me, self.nx)

    def at(self, dz, dy, dx):
        z = lax.rem(self.z + dz + self.nz, self.nz)
        y = lax.rem(self.y + dy + self.ny, self.ny)
        x = lax.rem(self.x + dx + self.nx, self.nx)
        return (z * self.ny + y) * self.nx + x

    def pair(self, i):
        return self.me ^ i


def enter(place):
    barrier = pltpu.get_barrier_semaphore()

    def greet(i):
        pl.semaphore_signal(barrier, 1, device_id=(place.pair(i), place.core), device_id_type=MESH)

    each(1, place.chips, greet)
    pl.semaphore_signal(barrier, 1, device_id=(place.me, 1 - place.core), device_id_type=MESH)
    pl.semaphore_wait(barrier, place.chips)


def remote(src, dst, send, recv, chip, core):
    return pltpu.make_async_remote_copy(
        src_ref=src, dst_ref=dst, send_sem=send, recv_sem=recv, device_id=(chip, core), device_id_type=MESH
    )


def each(first, last, do):
    def step(i, carry):
        do(i)
        return carry

    lax.fori_loop(first, last, step, 0)


def when(condition, do):
    if condition is None:
        do()
    else:
        pl.when(condition)(do)


def rows_at(start, count):
    return pl.ds(pl.multiple_of(start, 8), count)


def lanes_at(tile, count):
    return pl.ds(pl.multiple_of(tile * LANES, LANES), count * LANES)


def move(src, dst, sem):
    copy = pltpu.make_async_copy(src, dst, sem)
    copy.start()
    copy.wait()


class Tiles:
    def __init__(self, columns, chips):
        self.chips = chips
        self.least, self.richer = tile_share(columns // LANES, chips)
        assert 0 < self.least and 2 * self.richer <= chips

    def more(self, chip, core):
        return jnp.where(core == 0, chip < self.richer, chip >= self.chips - self.richer)

    def first(self, chip, core):
        late = jnp.maximum(chip - (self.chips - self.richer), 0)
        return self.least * chip + jnp.where(core == 0, jnp.minimum(chip, self.richer), late)

    def cut(self, ref, chip, core):
        start = self.first(chip, core)
        return (
            ref.at[:, lanes_at(start, self.least)],
            ref.at[:, lanes_at(jnp.minimum(start + self.least, self.first(self.chips, core) - 1), 1)],
        )


class Gather:
    @staticmethod
    def shape(chips, a):
        return (chips, *a.shape)

    @staticmethod
    def scratch(chips, a):
        nz, ny, nx = grid_of(chips)
        return [DMA((nz,))] * 2 + [DMA((nz, nx))] * 2 + [DMA((nz, ny))] * 2 + [DMA((nz, nx, ny))] * 4 + [DMA]

    def __init__(self, place, mine, out, sems):
        self.p, self.mine, self.out = place, mine, out
        (self.sl, self.rl, self.sx, self.rx, self.sy, self.ry, self.s1, self.r1, self.s2, self.r2, self.own) = sems
        self.half = mine.shape[0] // 2

    def line(self, k):
        p = self.p
        return remote(self.mine, self.out.at[p.me], self.sl.at[k], self.rl.at[k], p.at(k, 0, 0), p.core)

    def across(self, k, i):
        p = self.p
        b = p.at(-k, 0, 0)
        src = self.mine if k == 0 else self.out.at[b]
        return remote(src, self.out.at[b], self.sx.at[k, i], self.rx.at[k, i], p.at(0, 0, i), p.core)

    def along(self, k, j):
        p = self.p
        b = p.at(-k, 0, 0)
        src = self.mine if k == 0 else self.out.at[b]
        return remote(src, self.out.at[b], self.sy.at[k, j], self.ry.at[k, j], p.at(0, j, 0), p.core)

    def corner1(self, k, i, j):
        p = self.p
        part = self.out.at[p.at(-k, 0, -i), pl.ds(0, self.half)]
        return remote(part, part, self.s1.at[k, i, j], self.r1.at[k, i, j], p.at(0, j, 0), p.core)

    def corner2(self, k, i, j):
        p = self.p
        part = self.out.at[p.at(-k, -j, 0), pl.ds(self.half, self.half)]
        return remote(part, part, self.s2.at[k, i, j], self.r2.at[k, i, j], p.at(0, 0, i), p.core)

    def spread(self, k):
        for i in range(1, self.p.nx):
            self.across(k, i).start()
        for j in range(1, self.p.ny):
            self.along(k, j).start()

    def begin(self):
        for k in range(1, self.p.nz):
            self.line(k).start()
        self.spread(0)
        pltpu.make_async_copy(self.mine, self.out.at[self.p.me], self.own).start()

    def turn(self, k):
        p = self.p
        for i in range(1, p.nx):
            self.across(k, i).wait_recv()
            for j in range(1, p.ny):
                self.corner1(k, i, j).start()
        for j in range(1, p.ny):
            self.along(k, j).wait_recv()
            for i in range(1, p.nx):
                self.corner2(k, i, j).start()

    def steps(self):
        nz = self.p.nz
        order = [1, nz - 1] + list(range(2, nz - 1))

        def come(k):
            self.line(k).wait_recv()
            self.spread(k)

        return (
            [functools.partial(self.turn, 0)]
            + [functools.partial(come, k) for k in order]
            + [functools.partial(self.turn, k) for k in order]
        )

    def end(self):
        p = self.p
        pltpu.make_async_copy(self.mine, self.out.at[p.me], self.own).wait()
        for k in range(p.nz):
            if k:
                self.line(k).wait_send()
            for i in range(1, p.nx):
                self.across(k, i).wait_send()
            for j in range(1, p.ny):
                self.along(k, j).wait_send()
            for i in range(1, p.nx):
                for j in range(1, p.ny):
                    self.corner1(k, i, j).wait()
                    self.corner2(k, i, j).wait()


class Columns:
    @staticmethod
    def shape(chips, a):
        least, _ = tile_share(a.shape[1] // LANES, chips)
        return (chips * a.shape[0], (2 * least + 1) * LANES)

    @staticmethod
    def scratch(chips, a):
        return [DMA((chips,))] * 8 + [pltpu.VMEM((a.shape[0], LANES), a.dtype)]

    def __init__(self, place, weight, out, sems):
        self.p, self.w, self.out = place, weight, out
        self.ms, self.mr, self.es, self.er, self.fs, self.fr, self.gs, self.gr, self.nought = sems
        self.tiles = Tiles(weight.shape[1], place.chips)
        self.rows = weight.shape[0]

    def slots(self, chip, own):
        rows = rows_at(chip * self.rows, self.rows)
        least = self.tiles.least
        return self.out.at[rows, lanes_at(0 if own else least + 1, least)], self.out.at[rows, lanes_at(least, 1)]

    def sends(self, i):
        p = self.p
        chip = p.pair(i)
        (a, b), (c, d) = self.tiles.cut(self.w, chip, p.core), self.slots(p.me, True)
        return (
            remote(a, c, self.ms.at[i], self.mr.at[i], chip, p.core),
            remote(b, d, self.es.at[i], self.er.at[i], chip, p.core),
            self.tiles.more(chip, p.core),
        )

    def gets(self, i):
        p = self.p
        chip = p.pair(i)
        (a, b), (c, d) = self.tiles.cut(self.w, chip, p.core), self.slots(chip, True)
        return (
            remote(a, c, self.ms.at[i], self.mr.at[i], chip, p.core),
            remote(b, d, self.es.at[i], self.er.at[i], chip, p.core),
        )

    def passes(self, i):
        p = self.p
        chip = p.pair(i)
        a, b = self.slots(chip, True)
        if isinstance(i, int) and i == 0:
            a, b = self.tiles.cut(self.w, p.me, p.core)
        c, d = self.slots(chip, False)
        return (
            remote(a, c, self.fs.at[i], self.fr.at[i], p.me, 1 - p.core),
            remote(b, d, self.gs.at[i], self.gr.at[i], p.me, 1 - p.core),
        )

    def here(self):
        p = self.p
        (a, b), (c, d) = self.tiles.cut(self.w, p.me, p.core), self.slots(p.me, True)
        return pltpu.make_async_copy(a, c, self.ms.at[0]), pltpu.make_async_copy(b, d, self.es.at[0])

    def begin(self):
        p = self.p

        def send(i):
            main, extra, more = self.sends(i)
            main.start()
            pl.when(more)(extra.start)

        each(1, p.chips, send)
        own, pass_on = self.here(), self.passes(0)
        own[0].start()
        pass_on[0].start()

        @pl.when(self.tiles.more(p.me, p.core))
        def _():
            own[1].start()
            pass_on[1].start()

    def steps(self):
        return [self.hand_on]

    def hand_on(self):
        p = self.p
        mine = self.tiles.more(p.me, p.core)

        def hand(i):
            main, extra = self.gets(i)
            to_main, to_extra = self.passes(i)
            main.wait_recv()
            to_main.start()

            @pl.when(mine)
            def _():
                extra.wait_recv()
                to_extra.start()

        each(1, p.chips, hand)

    def end(self):
        p = self.p
        mine = self.tiles.more(p.me, p.core)
        theirs = self.tiles.more(p.me, 1 - p.core)
        own = self.here()
        own[0].wait()
        pl.when(mine)(own[1].wait)

        @pl.when(jnp.logical_not(mine | theirs))
        def _():
            self.nought[...] = jnp.zeros_like(self.nought)
            each(0, p.chips, lambda c: move(self.nought, self.slots(c, True)[1], self.es.at[0]))

        def sent(i):
            main, extra, more = self.sends(i)
            main.wait_send()
            pl.when(more)(extra.wait_send)

        each(1, p.chips, sent)

        def handed(i):
            main, extra = self.passes(i)
            main.wait()
            pl.when(mine)(extra.wait_send)
            pl.when(theirs)(extra.wait_recv)

        handed(0)
        each(1, p.chips, handed)


class Blocks:
    @staticmethod
    def shape(chips, a):
        return (chips * 2 * a.shape[1], a.shape[2])

    @staticmethod
    def scratch(chips, a):
        return [DMA((chips,))] * 4

    def __init__(self, place, blocks, out, sems):
        self.p, self.b, self.out = place, blocks, out
        self.s, self.r, self.fs, self.fr = sems
        self.rows = blocks.shape[1]

    def slot(self, chip, core):
        return self.out.at[rows_at((2 * chip + core) * self.rows, self.rows)]

    def sends(self, i):
        p = self.p
        chip = p.pair(i)
        return remote(self.b.at[chip], self.slot(p.me, p.core), self.s.at[i], self.r.at[i], chip, p.core)

    def passes(self, i):
        p = self.p
        part = self.slot(p.pair(i), p.core)
        mine = self.b.at[p.me] if isinstance(i, int) and i == 0 else part
        return remote(mine, part, self.fs.at[i], self.fr.at[i], p.me, 1 - p.core)

    def here(self):
        p = self.p
        return pltpu.make_async_copy(self.b.at[p.me], self.slot(p.me, p.core), self.s.at[0])

    def begin(self):
        each(1, self.p.chips, lambda i: self.sends(i).start())
        self.here().start()
        self.passes(0).start()

    def steps(self):
        return [self.hand_on]

    def hand_on(self):
        def hand(i):
            self.sends(i).wait_recv()
            self.passes(i).start()

        each(1, self.p.chips, hand)

    def end(self):
        p = self.p
        self.here().wait()
        each(1, p.chips, lambda i: self.sends(i).wait_send())
        self.passes(0).wait()
        each(1, p.chips, lambda i: self.passes(i).wait())


def drive(parts):
    for part in parts:
        part.begin()
    todo = [part.steps() for part in parts]
    total = max(len(steps) for steps in todo)
    for at in range(total):
        for steps in todo:
            index = at - (total - len(steps))
            if index >= 0:
                steps[index]()
    for part in parts:
        part.end()


def take(refs, counts):
    out, at = [], 0
    for count in counts:
        out.append(refs[at : at + count])
        at += count
    return out


def bring_kernel(chips, plan, *refs):
    n = len(plan)
    ins, outs, held = refs[:n], refs[n : 2 * n], refs[2 * n :]
    place = Place(chips)
    enter(place)
    held = take(held, [count for _, count in plan])
    drive([kind(place, a, o, h) for (kind, _), a, o, h in zip(plan, ins, outs, held)])


def bring(chips, number, name, *jobs):
    held = [kind.scratch(chips, a) for kind, a in jobs]
    return pl.pallas_call(
        functools.partial(bring_kernel, chips, [(kind, len(h)) for (kind, _), h in zip(jobs, held)]),
        in_specs=[ANY] * len(jobs),
        out_specs=[ANY] * len(jobs),
        out_shape=[jax.ShapeDtypeStruct(kind.shape(chips, a), a.dtype) for kind, a in jobs],
        scratch_shapes=[s for h in held for s in h],
        compiler_params=pltpu.CompilerParams(collective_id=number, has_side_effects=True, vmem_limit_bytes=16 << 20),
        name=name,
    )(*[a for _, a in jobs])


class Paired:
    @staticmethod
    def scratch(chips, shape, dtype):
        return [DMA((chips,))] * 5 + [pltpu.VMEM((chips, *shape), dtype)] * 2

    def __init__(self, place, held, views, gives=None, sums=None, comes=lambda j: None):
        self.p = place
        self.cs, self.cr, self.s, self.r, self.load, self.total, self.stage = held
        self.mine, self.theirs, self.target, self.source = views
        self.gives, self.sums, self.comes = gives, sums, comes

    def across(self, i):
        p = self.p
        return remote(self.theirs(p.pair(i)), self.stage.at[i], self.cs.at[i], self.cr.at[i], p.me, 1 - p.core)

    def fetch(self, i):
        return pltpu.make_async_copy(self.mine(self.p.pair(i)), self.total.at[i], self.load.at[i])

    def sends(self, i):
        p = self.p
        j = p.pair(i)
        return remote(self.total.at[i], self.target(j), self.s.at[i], self.r.at[i], j, p.core)

    def gets(self, i):
        p = self.p
        j = p.pair(i)
        return remote(self.total.at[i], self.source(j), self.s.at[i], self.r.at[i], j, p.core)

    def here(self):
        return pltpu.make_async_copy(self.total.at[0], self.source(self.p.me), self.s.at[0])

    def begin(self):
        chips = self.p.chips
        when(self.gives, lambda: each(0, chips, lambda i: self.across(i).start()))
        when(self.sums, lambda: each(0, chips, lambda i: self.fetch(i).start()))

    def add(self, i):
        self.fetch(i).wait()
        self.across(i).wait_recv()
        self.total[i] = (self.total[i].astype(F32) + self.stage[i].astype(F32)).astype(self.total.dtype)

    def some(self, first, last):
        def do(i):
            self.add(i)
            self.sends(i).start()

        when(self.sums, lambda: each(first, last, do))

    def own(self):
        def do():
            self.add(0)
            self.here().start()

        when(self.sums, do)

    def end(self):
        chips = self.p.chips
        when(self.gives, lambda: each(0, chips, lambda i: self.across(i).wait_send()))

        def sent():
            self.here().wait()
            each(1, chips, lambda i: self.sends(i).wait_send())

        when(self.sums, sent)

        def came(i):
            when(self.comes(self.p.pair(i)), lambda: self.gets(i).wait_recv())

        each(1, chips, came)

    def steps(self):
        chips = self.p.chips
        return [functools.partial(self.some, 1, chips), self.own]


class Scatter:
    @staticmethod
    def stages(chips, a):
        nz, _, n = grid_of(chips)
        _, t, d = a.shape
        h = t // 2
        return [(2, nz, n, n, h, d), (2, nz, n, h, d), (2, nz, n, h, d), (nz, t, d), (nz, t, d)]

    @staticmethod
    def scratch(chips, a):
        nz, _, n = grid_of(chips)
        _, t, d = a.shape
        h = t // 2
        most = max(n, nz)
        sems = [DMA((2, nz, n, n))] * 2 + [DMA((2, nz, n))] * 2 + [DMA((nz,))] * 2 + [DMA((most,)), DMA]
        return sems + [pltpu.VMEM((most, h, d), a.dtype), pltpu.VMEM((h, d), a.dtype)]

    def __init__(self, place, blocks, stages, held):
        self.p, self.b = place, blocks
        self.got1, self.sum1, self.got2, self.sum2, self.got3 = stages
        (self.s1, self.r1, self.s2, self.r2, self.s3, self.r3, self.load, self.store, self.parts, self.low) = held
        self.h = blocks.shape[1] // 2
        self.n = place.nx

    def chip(self, half, dz, du, dv):
        return self.p.at(dz, dv, du) if half == 0 else self.p.at(dz, du, dv)

    def rows(self, half):
        return pl.ds(half * self.h, self.h)

    def send1(self, half, dz, v, i):
        return remote(
            self.b.at[self.chip(half, dz, i, v), self.rows(half)],
            self.got1.at[half, dz, v, i],
            self.s1.at[half, dz, v, i],
            self.r1.at[half, dz, v, i],
            self.chip(half, 0, i, 0),
            self.p.core,
        )

    def send2(self, half, dz, v):
        return remote(
            self.sum1.at[half, dz, v],
            self.got2.at[half, dz, v],
            self.s2.at[half, dz, v],
            self.r2.at[half, dz, v],
            self.chip(half, 0, 0, v),
            self.p.core,
        )

    def send3(self, dz):
        return remote(
            self.sum2.at[dz], self.got3.at[dz], self.s3.at[dz], self.r3.at[dz], self.p.at(dz, 0, 0), self.p.core
        )

    def fetch(self, refs):
        loads = [pltpu.make_async_copy(r, self.parts.at[i], self.load.at[i]) for i, r in enumerate(refs)]
        for copy in loads:
            copy.start()
        for copy in loads:
            copy.wait()

    def add(self, refs, to):
        self.fetch(refs)
        total = self.parts[0].astype(F32)
        for i in range(1, len(refs)):
            total = total + self.parts[i].astype(F32)
        self.low[...] = total.astype(self.low.dtype)
        move(self.low, to, self.store)

    def order(self):
        nz = self.p.nz
        return [nz // 2] + [k for k in range(1, nz) if k != nz // 2] + [0]

    def begin(self):
        for dz in self.order():
            for half in (0, 1):
                for v in list(range(1, self.n)) + [0]:
                    for i in range(1, self.n):
                        self.send1(half, dz, v, i).start()

    def first(self, dz):
        for half in (0, 1):
            for v in list(range(1, self.n)) + [0]:
                for i in range(1, self.n):
                    self.send1(half, dz, v, i).wait_recv()
                mine = self.b.at[self.chip(half, dz, 0, v), self.rows(half)]
                self.add([mine] + [self.got1.at[half, dz, v, i] for i in range(1, self.n)], self.sum1.at[half, dz, v])
                if v:
                    self.send2(half, dz, v).start()

    def second(self, dz):
        for half in (0, 1):
            for v in range(1, self.n):
                self.send2(half, dz, v).wait_recv()
            parts = [self.sum1.at[half, dz, 0]] + [self.got2.at[half, dz, v] for v in range(1, self.n)]
            self.add(parts, self.sum2.at[dz, self.rows(half)])
        if dz:
            self.send3(dz).start()

    def last(self):
        for dz in range(1, self.p.nz):
            self.send3(dz).wait_recv()
        for half in (0, 1):
            rows = self.rows(half)
            self.fetch([self.sum2.at[0, rows]] + [self.got3.at[dz, rows] for dz in range(1, self.p.nz)])
            self.finish(half)

    def steps(self):
        order = self.order()
        steps = [functools.partial(self.first, order[0])]
        for old, new in zip(order[:-1], order[1:]):
            steps += [functools.partial(self.first, new), functools.partial(self.second, old)]
        return steps + [functools.partial(self.second, order[-1]), self.last]

    def end(self):
        for dz in range(self.p.nz):
            for half in (0, 1):
                for v in range(self.n):
                    for i in range(1, self.n):
                        self.send1(half, dz, v, i).wait_send()
                    if v:
                        self.send2(half, dz, v).wait_send()
            if dz:
                self.send3(dz).wait_send()


class NormBack(Scatter):
    @staticmethod
    def scratch(chips, a):
        d = a.shape[2]
        more = [pltpu.VMEM((2, 8, d), F32), pltpu.VMEM((2, d), F32), pltpu.VMEM((2, d), F32), pltpu.VMEM((chips, 2, d), F32)]
        return Scatter.scratch(chips, a) + more + [DMA((chips,))] * 2 + [DMA((3,))]

    def __init__(self, place, blocks, stages, held, operands, results, features):
        super().__init__(place, blocks, stages, held[:10])
        self.sums, self.mine, self.other, self.slots, self.ss, self.sr, self.pairs = held[10:]
        self.xhat, self.grad, self.gain, self.inverse = operands
        self.input_grad, self.stats = results
        self.features = features

    def begin(self):
        super().begin()
        self.sums[...] = jnp.zeros_like(self.sums)

    def finish(self, half):
        d = self.xhat.shape[1]

        def some(c):
            at = pl.multiple_of(c * 16, 16)
            total = self.parts[0, pl.ds(at, 16)].astype(F32)
            for i in range(1, self.p.nz):
                total = total + self.parts[i, pl.ds(at, 16)].astype(F32)
            rows = pl.ds(pl.multiple_of(half * self.h + c * 16, 16), 16)
            xhat = self.xhat[rows]
            both = total * xhat
            self.sums[0] += both[:8] + both[8:]
            self.sums[1] += total[:8] + total[8:]
            scaled = total * self.gain[...]
            mean = jnp.sum(scaled, 1, keepdims=True) / self.features
            slope = jnp.sum(scaled * xhat, 1, keepdims=True) / self.features
            change = (scaled - mean - xhat * slope) * self.inverse[rows]
            self.input_grad[rows] = self.grad[rows].astype(F32) + change

        each(0, self.h // 16, some)

    def swap_stats(self):
        p = self.p
        return remote(self.mine, self.other, self.pairs.at[0], self.pairs.at[1], p.me, 1 - p.core)

    def share_stats(self, i):
        p = self.p
        return remote(self.mine, self.slots.at[p.me], self.ss.at[i], self.sr.at[i], p.pair(i), p.core)

    def get_stats(self, i):
        p = self.p
        return remote(self.mine, self.slots.at[p.pair(i)], self.ss.at[i], self.sr.at[i], p.pair(i), p.core)

    def stats_out(self):
        self.mine[0:1] = jnp.sum(self.sums[0], 0, keepdims=True)
        self.mine[1:2] = jnp.sum(self.sums[1], 0, keepdims=True)
        self.swap_stats().start()
        self.swap_stats().wait()
        self.mine[...] += self.other[...]
        self.slots[self.p.me] = self.mine[...]
        each(1, self.p.chips, lambda i: self.share_stats(i).start())

    def steps(self):
        return super().steps() + [self.stats_out]

    def end(self):
        super().end()

        def done(i):
            self.share_stats(i).wait_send()
            self.get_stats(i).wait_recv()

        each(1, self.p.chips, done)
        self.stats[...] = self.slots[0]

        def more(c):
            self.stats[...] += self.slots[c]

        each(1, self.p.chips, more)


def return_parts(place, part, out, held):
    tiles = Tiles(out.shape[1], place.chips)
    least, rows, core, me = tiles.least, out.shape[0], place.core, place.me
    n = len(held) // 2

    def at(j, tile, count):
        return part.at[rows_at(j * rows, rows), lanes_at(tile, count)]

    main = Paired(
        place,
        held[:n],
        (
            lambda j: at(j, 0, least),
            lambda j: at(j, least + 1, least),
            lambda j: tiles.cut(out, me, core)[0],
            lambda j: tiles.cut(out, j, core)[0],
        ),
    )
    extra = Paired(
        place,
        held[n:],
        (
            lambda j: at(j, least, 1),
            lambda j: at(j, least, 1),
            lambda j: tiles.cut(out, me, core)[1],
            lambda j: tiles.cut(out, j, core)[1],
        ),
        tiles.more(me, 1 - core),
        tiles.more(me, core),
        lambda j: tiles.more(j, core),
    )
    return [main, extra]


def trade_parts(place, part, out, held):
    rows = out.shape[1]

    def at(j, core):
        return part.at[rows_at((2 * j + core) * rows, rows)]

    views = (
        lambda j: at(j, place.core),
        lambda j: at(j, 1 - place.core),
        lambda j: out.at[place.me],
        lambda j: out.at[j],
    )
    return [Paired(place, held, views)]


def send_kernel(chips, features, counts, *refs):
    blocks, wide, small, xhat, grad, gain, inverse = refs[:7]
    input_grad, stats, wide_out, small_out = refs[7:11]
    stages = refs[11:16]
    norm_held, wide_held, small_held = take(refs[16:], counts)
    place = Place(chips)
    enter(place)
    norm = NormBack(place, blocks, stages, norm_held, (xhat, grad, gain, inverse), (input_grad, stats), features)
    parts = return_parts(place, wide, wide_out, wide_held)
    parts += trade_parts(place, small, small_out, small_held)
    for part in [norm] + parts:
        part.begin()
    for part in parts + [norm]:
        for step in part.steps():
            step()
    for part in [norm] + parts:
        part.end()


def send(chips, number, features, blocks, wide, columns, small, xhat, grad, gain, inverse):
    _, tokens, d = blocks.shape
    rows = d // chips
    least, _ = tile_share(columns // LANES, chips)
    width = small.shape[1]
    held = [
        NormBack.scratch(chips, blocks),
        Paired.scratch(chips, (rows, least * LANES), BF16) + Paired.scratch(chips, (rows, LANES), BF16),
        Paired.scratch(chips, (rows // 2, width), BF16),
    ]
    low = lambda *shape: jax.ShapeDtypeStruct(shape, BF16)
    results = pl.pallas_call(
        functools.partial(send_kernel, chips, features, [len(h) for h in held]),
        in_specs=[ANY] * 3 + [WHOLE] * 4,
        out_specs=[WHOLE] * 2 + [ANY] * 7,
        out_shape=[
            jax.ShapeDtypeStruct((tokens, d), F32),
            jax.ShapeDtypeStruct((2, d), F32),
            low(rows, columns),
            low(chips, rows // 2, width),
        ]
        + [low(*s) for s in Scatter.stages(chips, blocks)],
        scratch_shapes=[s for h in held for s in h],
        compiler_params=pltpu.CompilerParams(collective_id=number, has_side_effects=True, vmem_limit_bytes=48 << 20),
        name="send",
    )(blocks, wide, small, xhat, grad, gain, inverse)
    return results[:4]


def rotate(values, cosines, sines):
    middle = values.shape[-1] // 2
    turned = jnp.concatenate([-values[..., middle:], values[..., :middle]], -1)
    return values * cosines + turned * sines


def rotate_back(values, cosines, sines):
    middle = values.shape[-1] // 2
    turned = jnp.concatenate([values[..., middle:], -values[..., :middle]], -1)
    return values * cosines + turned * sines


def flat(ref):
    return ref[...].reshape(ref.shape[0] * ref.shape[1], ref.shape[2])


def chunks(width, most):
    return [(at, min(most, width - at)) for at in range(0, width, most)]


def resident(shape, column=0):
    return pl.BlockSpec(shape, lambda i: (0, column), pipeline_mode=pl.Buffered(1))


def per_row(rows, width):
    return pl.BlockSpec((rows, width), lambda i: (i, 0))


def forward_kernel(chips, plan, lead, events, *refs):
    n = len(plan)
    x_ref, small_ref, wide_ref, cos_ref, sin_ref = refs[:5]
    ins, refs = refs[5 : 5 + n], refs[5 + n :]
    q_out, k_out, v_out, hidden_ref, slope_ref, low_ref, o_ref, lse_ref = refs[:8]
    outs, refs = refs[8 : 8 + n], refs[8 + n :]
    q_all, k_all, v_all, acc, top = refs[:5]
    held = take(refs[5:], [count for _, count in plan])
    step = pl.program_id(0)
    half = pl.num_programs(0) // 2
    heads, rows, _ = q_out.shape
    place = Place(chips)
    parts = [kind(place, a, o, h) for (kind, _), a, o, h in zip(plan, ins, outs, held)]

    @pl.when(step == 0)
    def _():
        enter(place)
        for part in parts:
            part.begin()

    @pl.when(step < half)
    def _():
        here = pl.ds(pl.multiple_of(step * rows, rows), rows)
        x = flat(x_ref)
        cosines, sines = cos_ref[...], sin_ref[...]
        joined = dot(x, small_ref[...])
        for h in range(heads):
            q = rotate(joined[:, h * HEAD : (h + 1) * HEAD], cosines, sines).astype(BF16) * HEAD ** (-0.5)
            q_out[h] = q
            q_all[h, here] = q
        at = heads * HEAD
        k = rotate(joined[:, at : at + HEAD], cosines, sines).astype(BF16)
        v = joined[:, at + HEAD : at + 2 * HEAD].astype(BF16)
        k_out[...] = k
        v_out[...] = v
        k_all[here] = k
        v_all[here] = jnp.concatenate([v, jnp.ones_like(v)], 1)
        for at, width in chunks(wide_ref.shape[1], 384):
            up = dot(x, wide_ref[:, at : at + width])
            bell = 0.5 + 0.5 * lax.erf(up * 0.5**0.5)
            hidden_ref[:, at : at + width] = (up * bell).astype(BF16)
            slope = bell + up * jnp.exp(up * up * -0.5) * (2 * jnp.pi) ** (-0.5)
            slope_ref[:, at : at + width] = slope.astype(BF16)

    @pl.when(step >= half)
    def _():
        index = step - half
        here = pl.ds(pl.multiple_of(index * rows, rows), rows)
        lows = []
        for h in range(heads):
            q = q_all[h, here]
            acc[...] = jnp.zeros_like(acc)
            top[...] = jnp.full_like(top, MASKED)

            def block(start, masked):
                s = dot(q, k_all[pl.ds(start, rows), :], ROWS_COLS)
                if masked:
                    key = lax.broadcasted_iota(jnp.int32, s.shape, 1)
                    query = lax.broadcasted_iota(jnp.int32, s.shape, 0)
                    s = jnp.where(key <= query, s, MASKED)
                old = top[...]
                new = jnp.maximum(old, jnp.max(s, 1, keepdims=True))
                p = jnp.exp(s - new).astype(BF16)
                acc[...] = acc[...] * jnp.exp(old - new) + dot(p, v_all[pl.ds(start, rows), :])
                top[...] = new

            each(0, index, lambda i: block(pl.multiple_of(i * rows, rows), False))
            block(pl.multiple_of(index * rows, rows), True)
            total = acc[...]
            norm = total[:, HEAD : HEAD + 1]
            out = total[:, :HEAD] / norm
            o_ref[h] = out
            lows.append(out.astype(BF16))
            lse = jnp.broadcast_to(top[...] + jnp.log(norm), (rows, LANES))
            lse_ref[h] = lse.T[:1]
        if lead:
            lows = [jnp.zeros((rows, lead), BF16)] + lows
        low_ref[...] = jnp.concatenate(lows, 1)

    todo = []
    longest = max(len(part.steps()) for part in parts)
    for at in range(longest):
        for part in parts:
            steps = part.steps()
            index = at - (longest - len(steps))
            if index >= 0:
                todo.append(steps[index])
    cuts = [0, *[c for _, c in events], len(todo)]
    for (back, _), first, last in zip([*events, (0, None)], cuts[:-1], cuts[1:]):

        @pl.when(step == pl.num_programs(0) - 1 - back)
        def _():
            for do in todo[first:last]:
                do()

    @pl.when(step == pl.num_programs(0) - 1)
    def _():
        for part in parts:
            part.end()


def forward(x, small, wide, cosines, sines, heads, lead, number, jobs):
    chips, tokens, d = x.shape
    length = chips * tokens
    step = max(1, 512 // tokens)
    rows = step * tokens
    half = chips // step
    width = -(-(heads + 2) * HEAD // LANES) * LANES
    n = wide.shape[1]
    low = lead + heads * HEAD
    held = [kind.scratch(chips, a) for kind, a in jobs]
    plan = [(kind, len(h)) for (kind, _), h in zip(jobs, held)]
    early = lambda i: jnp.minimum(i, half - 1)
    late = lambda i: jnp.maximum(i - half, 0)
    first = lambda w: pl.BlockSpec((rows, w), lambda i: (early(i), 0))
    events = ((4, 1), (2, 3), (1, 4))
    results = pl.pallas_call(
        functools.partial(forward_kernel, chips, plan, lead, events),
        grid=(2 * half,),
        in_specs=[
            pl.BlockSpec((step, tokens, d), lambda i: (early(i), 0, 0)),
            resident((d, width)),
            resident((d, n)),
            first(HEAD),
            first(HEAD),
        ]
        + [ANY] * len(jobs),
        out_specs=[
            pl.BlockSpec((heads, rows, HEAD), lambda i: (0, early(i), 0)),
            first(HEAD),
            first(HEAD),
            first(n),
            first(n),
            pl.BlockSpec((rows, low), lambda i: (late(i), 0)),
            pl.BlockSpec((heads, rows, HEAD), lambda i: (0, late(i), 0)),
            pl.BlockSpec((heads, 1, rows), lambda i: (0, 0, late(i))),
        ]
        + [ANY] * len(jobs),
        out_shape=[
            jax.ShapeDtypeStruct((heads, length, HEAD), BF16),
            jax.ShapeDtypeStruct((length, HEAD), BF16),
            jax.ShapeDtypeStruct((length, HEAD), BF16),
            jax.ShapeDtypeStruct((length, n), BF16),
            jax.ShapeDtypeStruct((length, n), BF16),
            jax.ShapeDtypeStruct((length, low), BF16),
            jax.ShapeDtypeStruct((heads, length, HEAD), F32),
            jax.ShapeDtypeStruct((heads, 1, length), F32),
        ]
        + [jax.ShapeDtypeStruct(kind.shape(chips, a), a.dtype) for kind, a in jobs],
        scratch_shapes=[
            pltpu.VMEM((heads, length, HEAD), BF16),
            pltpu.VMEM((length, HEAD), BF16),
            pltpu.VMEM((length, 2 * HEAD), BF16),
            pltpu.VMEM((rows, 2 * HEAD), F32),
            pltpu.VMEM((rows, 1), F32),
        ]
        + [s for h in held for s in h],
        compiler_params=pltpu.CompilerParams(collective_id=number, has_side_effects=True, vmem_limit_bytes=58 << 20),
        cost_estimate=pl.CostEstimate(
            flops=2 * length * d * (n + width) + 2 * heads * length * length * HEAD,
            transcendentals=2 * length * n + heads * length * length // 2,
            bytes_accessed=2 * length * d,
        ),
        name="forward",
    )(x, small, wide, cosines, sines, *[a for _, a in jobs])
    return results[:8], results[8:]


def backward_kernel(chips, lead, counts, *refs):
    g_ref, dense_ref, down_ref, slope_ref, q_ref, k_ref, v_ref, o_ref, lse_ref, cos_ref, sin_ref = refs[:11]
    wide, small = refs[11:13]
    grad_ref, out_ref, wide_out, small_out = refs[13:17]
    g_all, acc, dk, dv = refs[17:21]
    wide_held, small_held = take(refs[21:], counts)
    heads, rows, _ = q_ref.shape
    length = g_all.shape[1]
    count = pl.num_programs(0) - length // rows
    step = pl.program_id(0)
    scale = HEAD ** (-0.5)
    place = Place(chips)
    parts = return_parts(place, wide, wide_out, wide_held) + trade_parts(place, small, small_out, small_held)

    @pl.when(step == 0)
    def _():
        enter(place)
        for part in parts:
            part.begin()

    @pl.when(step < count)
    def _():
        g = flat(g_ref)
        low = g.shape[0]
        here = pl.ds(pl.multiple_of(step * low, low), low)
        grad = dot(g, dense_ref[...]).astype(BF16)
        for h in range(heads):
            g_all[h, here] = grad[:, lead + h * HEAD : lead + (h + 1) * HEAD]
        for at, width in chunks(down_ref.shape[1], 384):
            part = dot(g, down_ref[:, at : at + width])
            grad_ref[:, at : at + width] = (part * slope_ref[:, at : at + width].astype(F32)).astype(BF16)

    @pl.when(step == count)
    def _():
        dk[...] = jnp.zeros_like(dk)
        dv[...] = jnp.zeros_like(dv)
        out_ref[...] = jnp.zeros_like(out_ref)

    @pl.when(step >= count)
    def _():
        index = step - count
        here = pl.ds(pl.multiple_of(index * rows, rows), rows)
        cosines, sines = cos_ref[here], sin_ref[here]
        grads = []
        for h in range(heads):
            q = q_ref[h]
            g = g_all[h, here]
            lse = lse_ref[h]
            delta = jnp.sum((g.astype(F32) * o_ref[h]).T, 0, keepdims=True)
            acc[...] = jnp.zeros_like(acc)

            def block(start, masked):
                at = pl.ds(start, rows)
                k = k_ref[at, :]
                p = jnp.exp(dot(k, q, ROWS_COLS) - lse)
                if masked:
                    key = lax.broadcasted_iota(jnp.int32, p.shape, 0)
                    query = lax.broadcasted_iota(jnp.int32, p.shape, 1)
                    p = jnp.where(key <= query, p, 0.0)
                dp = dot(v_ref[at, :], g, ROWS_COLS)
                ds = (p * (dp - delta)).astype(BF16)
                dv[at, :] += dot(p.astype(BF16), g)
                dk[at, :] += dot(ds, q)
                acc[...] += dot(ds, k, ROWS_ROWS)

            each(0, index, lambda i: block(pl.multiple_of(i * rows, rows), False))
            block(pl.multiple_of(index * rows, rows), True)
            grads.append(rotate_back(acc[...] * scale, cosines, sines).astype(BF16))
        out_ref[here, : heads * HEAD] = jnp.concatenate(grads, 1)

    @pl.when(step == 1)
    def _():
        for part in parts:
            for do in part.steps():
                do()

    @pl.when(step == pl.num_programs(0) - 1)
    def _():
        keys = rotate_back(dk[...], cos_ref[...], sin_ref[...]).astype(BF16)
        both = jnp.concatenate([keys, dv[...].astype(BF16)], 1)
        out_ref[:, heads * HEAD : (heads + 2) * HEAD] = both
        for part in parts:
            part.end()


def backward(g, small, lead, down, slope, q, k, v, o, lse, cosines, sines, number, down_part, dense_part, columns):
    chips, tokens, d = g.shape
    heads, length, _ = q.shape
    group = max(1, 256 // tokens)
    low = group * tokens
    count = chips // group
    rows = min(512, length)
    width = lead + heads * HEAD
    n = down.shape[1]
    out_width = -(-(heads + 2) * HEAD // LANES) * LANES
    high = d // chips
    least, _ = tile_share(columns // LANES, chips)
    held = [
        Paired.scratch(chips, (high, least * LANES), BF16) + Paired.scratch(chips, (high, LANES), BF16),
        Paired.scratch(chips, (high // 2, width), BF16),
    ]
    early = lambda i: jnp.minimum(i, count - 1)
    late = lambda i: jnp.maximum(i - count, 0)
    first = pl.BlockSpec((low, n), lambda i: (early(i), 0))
    per_query = pl.BlockSpec((heads, rows, HEAD), lambda i: (0, late(i), 0))
    whole = resident((length, HEAD))
    return pl.pallas_call(
        functools.partial(backward_kernel, chips, lead, [len(h) for h in held]),
        grid=(count + length // rows,),
        in_specs=[
            pl.BlockSpec((group, tokens, d), lambda i: (early(i), 0, 0)),
            resident((d, width), small.shape[1] // width - 1),
            resident((d, n)),
            first,
            per_query,
            whole,
            whole,
            per_query,
            pl.BlockSpec((heads, 1, rows), lambda i: (0, 0, late(i))),
            whole,
            whole,
            ANY,
            ANY,
        ],
        out_specs=[first, resident((length, out_width)), ANY, ANY],
        out_shape=[
            jax.ShapeDtypeStruct((length, n), BF16),
            jax.ShapeDtypeStruct((length, out_width), BF16),
            jax.ShapeDtypeStruct((high, columns), BF16),
            jax.ShapeDtypeStruct((chips, high // 2, width), BF16),
        ],
        scratch_shapes=[
            pltpu.VMEM((heads, length, HEAD), BF16),
            pltpu.VMEM((rows, HEAD), F32),
            pltpu.VMEM((length, HEAD), F32),
            pltpu.VMEM((length, HEAD), F32),
        ]
        + [s for h in held for s in h],
        compiler_params=pltpu.CompilerParams(collective_id=number, has_side_effects=True, vmem_limit_bytes=60 << 20),
        cost_estimate=pl.CostEstimate(
            flops=2 * length * d * (n + width) + 5 * heads * length * length * HEAD,
            transcendentals=heads * length * length // 2,
            bytes_accessed=2 * length * d,
        ),
        name="backward",
    )(g, small, down, slope, q, k, v, o, lse, cosines, sines, down_part, dense_part)


def out_kernel(a_ref, b_ref, small_ref, wide_ref, out_ref):
    tokens, d = out_ref.shape[-2:]
    step = a_ref.shape[0] // tokens
    a, b = a_ref[...], b_ref[...]
    for at, width in chunks(d, 512):
        part = dot(a, small_ref[at : at + width], ROWS_COLS) + dot(b, wide_ref[at : at + width], ROWS_COLS)
        part = part.astype(BF16).reshape(step, tokens, width)
        if out_ref.ndim == 4:
            out_ref[:, 0, :, at : at + width] = part
        else:
            out_ref[:, :, at : at + width] = part


def out_product(a, b, small, column, wide, chips, name, by_plane=False):
    length, width = a.shape
    tokens, d = length // chips, small.shape[0]
    step = max(1, 512 // tokens)
    rows = step * tokens
    n = wide.shape[1]
    shape, spec = (chips, tokens, d), pl.BlockSpec((step, tokens, d), lambda i: (i, 0, 0))
    if by_plane:
        nz, ny, nx = grid_of(chips)
        per = ny * nx // step
        shape = (ny * nx, nz, tokens, d)
        spec = pl.BlockSpec((step, 1, tokens, d), lambda i: (lax.rem(i, per), i // per, 0, 0))
    return pl.pallas_call(
        out_kernel,
        grid=(chips // step,),
        in_specs=[per_row(rows, width), per_row(rows, n), resident((d, width), column), resident((d, n))],
        out_specs=spec,
        out_shape=jax.ShapeDtypeStruct(shape, BF16),
        compiler_params=pltpu.CompilerParams(vmem_limit_bytes=56 << 20),
        cost_estimate=pl.CostEstimate(
            flops=2 * length * d * (n + width), transcendentals=0, bytes_accessed=2 * length * d
        ),
        name=name,
    )(a, b, small, wide)


def weight_kernel(x_ref, a_ref, b_ref, small_ref, wide_ref):
    chips, tokens, width = x_ref.shape
    x = x_ref[...].reshape(chips * tokens, width)
    small_ref[...] = dot(x, a_ref[...], ROWS_ROWS).astype(BF16)
    for at, n in chunks(wide_ref.shape[1], 384):
        wide_ref[:, at : at + n] = dot(x, b_ref[:, at : at + n], ROWS_ROWS).astype(BF16)


def weight_product(x, a, b, name):
    chips, tokens, d = x.shape
    length = chips * tokens
    width = 768 if d % 768 == 0 else 512
    return pl.pallas_call(
        weight_kernel,
        grid=(d // width,),
        in_specs=[pl.BlockSpec((chips, tokens, width), lambda i: (0, 0, i)), resident(a.shape), resident(b.shape)],
        out_specs=[per_row(width, a.shape[1]), per_row(width, b.shape[1])],
        out_shape=[jax.ShapeDtypeStruct((d, a.shape[1]), BF16), jax.ShapeDtypeStruct((d, b.shape[1]), BF16)],
        compiler_params=pltpu.CompilerParams(vmem_limit_bytes=56 << 20),
        cost_estimate=pl.CostEstimate(
            flops=2 * length * d * (a.shape[1] + b.shape[1]), transcendentals=0, bytes_accessed=2 * length * d
        ),
        name=name,
    )(x, a, b)


def share_heads(columns, chips):
    rows, width = columns.shape
    heads = width // HEAD
    most = -(-heads // chips)
    richer = heads - chips * (most - 1)
    cut = richer * most * HEAD
    first = jnp.moveaxis(columns[:, :cut].reshape(rows, richer, most * HEAD), 1, 0)
    if richer == chips:
        return first
    rest = jnp.moveaxis(columns[:, cut:].reshape(rows, chips - richer, (most - 1) * HEAD), 1, 0)
    return jnp.concatenate([first, jnp.pad(rest, ((0, 0), (0, 0), (0, HEAD)))], 0)


def join_heads(parts, heads):
    chips, rows, width = parts.shape
    most = width // HEAD
    richer = heads - chips * (most - 1)
    first = jnp.moveaxis(parts[:richer], 0, 1).reshape(rows, -1)
    if richer == chips:
        return first
    rest = jnp.moveaxis(parts[richer:, :, : width - HEAD], 0, 1).reshape(rows, -1)
    return jnp.concatenate([first, rest], 1)


def swap(values):
    return lax.ppermute(values, "fsdp", [(0, 1), (1, 0)])


def in_order(mine, other, core, axis):
    return jnp.where(
        core == 0,
        jnp.concatenate([mine, other], axis),
        jnp.concatenate([other, mine], axis),
    )


def half_of(values, core, axis):
    first, second = jnp.split(values, 2, axis)
    return jnp.where(core == 0, first, second), jnp.where(core == 0, second, first)


def angles(length):
    inverse_freq = ROPE_BASE ** (-jnp.arange(0, HEAD, 2).astype(F32) / HEAD)
    phases = jnp.arange(length, dtype=jnp.int32).astype(F32)[:, None] * inverse_freq[None, :]
    phases = jnp.concatenate([phases, phases], -1)
    return jnp.cos(phases), jnp.sin(phases)


def body(layer_input, cotangent, norm_gain, norm_bias, qkv_weight, up_weight, dense_weight, down_weight):
    chips = lax.axis_size("ctx")
    core = lax.axis_index("fsdp")
    inputs = layer_input[0].astype(F32)
    tokens, features = inputs.shape
    length = tokens * chips
    heads = features // HEAD
    most = -(-heads // chips)
    qwide = most * HEAD
    rows = qkv_weight.shape[0]
    high = padded_rows(rows)
    wide_columns = up_weight.shape[1]
    lead = (qwide + 2 * HEAD) % LANES

    def pad(values):
        apart = values.reshape(*values.shape[:-1], chips, rows)
        apart = jnp.pad(apart, [(0, 0)] * (apart.ndim - 1) + [(0, high - rows)])
        return apart.reshape(*values.shape[:-1], chips * high)

    def unpad(values):
        apart = values.reshape(*values.shape[:-1], chips, high)[..., :rows]
        return apart.reshape(*values.shape[:-1], features)

    def pad_rows(weight):
        return jnp.pad(weight, ((0, high - rows), (0, 0)))

    center = inputs - jnp.mean(inputs, -1, keepdims=True)
    inverse = lax.rsqrt(jnp.mean(center * center, -1, keepdims=True) + EPS)
    xhat = center * inverse
    normed_low = pad((xhat * norm_gain + norm_bias).astype(BF16))
    grad_low = pad(cotangent[0])

    mine, other = half_of(pad_rows(jnp.concatenate([qkv_weight, dense_weight], 1)), core, 0)
    other = swap(other)
    qkv_columns = qkv_weight.shape[1]
    qkv_rows = in_order(mine[:, :qkv_columns], other[:, :qkv_columns], core, 1)
    dense_rows = in_order(mine[:, qkv_columns:], other[:, qkv_columns:], core, 1)
    blocks = jnp.concatenate(
        [
            share_heads(qkv_rows[:, :features], chips),
            jnp.broadcast_to(qkv_rows[:, features:], (chips, high // 2, 2 * HEAD)),
            share_heads(dense_rows, chips),
        ],
        2,
    )
    normed_all, up_cols, small = bring(
        chips, 0, "bring", (Gather, normed_low), (Columns, pad_rows(up_weight)), (Blocks, blocks)
    )

    cosines, sines = angles(length)
    dense_block = small.shape[1] // (lead + qwide) - 1
    (queries, keys, values, hidden_low, slope, attended_low, attention, log_sum), (grad_all, down_cols) = forward(
        normed_all,
        small,
        up_cols,
        cosines,
        sines,
        most,
        lead,
        2,
        [(Gather, grad_low), (Columns, pad_rows(down_weight))],
    )
    branch = out_product(attended_low, hidden_low, small, dense_block, down_cols, chips, "forward_out", True)
    branch, grad_all = lax.optimization_barrier((branch, grad_all))
    nz, ny, nx = grid_of(chips)
    planes = [[z * ny * nx + i for i in range(ny * nx)] for z in range(nz)]
    lines = [[z * ny * nx + i for z in range(nz)] for i in range(ny * nx)]
    branch = branch.reshape(ny * nx, nz * tokens, -1)
    branch = lax.psum_scatter(branch, "ctx", scatter_dimension=0, axis_index_groups=planes, tiled=False)

    dense_part, down_part = weight_product(grad_all, attended_low, hidden_low, "late_weights")
    grad_up, grad_joined, down_grad, dense_total = backward(
        grad_all,
        small,
        lead,
        down_cols,
        slope,
        queries,
        keys,
        values,
        attention,
        log_sum,
        cosines,
        sines,
        3,
        down_part,
        dense_part,
        wide_columns,
    )
    branch, grad_joined = lax.optimization_barrier((branch, grad_joined))
    branch = branch.reshape(nz, tokens, -1)
    branch = lax.psum_scatter(branch, "ctx", scatter_dimension=0, axis_index_groups=lines, tiled=False)
    layer_output = (inputs + unpad(branch).astype(F32)).astype(BF16)
    grad_normed = out_product(grad_joined, grad_up, small, 0, up_cols, chips, "back_out")
    qkv_part, up_part = weight_product(normed_all, grad_joined, grad_up, "early_weights")

    input_grad, stats, up_grad, total = send(
        chips,
        1,
        features,
        grad_normed,
        up_part,
        wide_columns,
        qkv_part,
        pad(xhat),
        grad_low,
        pad(norm_gain[None]),
        inverse,
    )
    up_grad = up_grad[:rows].astype(F32)
    down_grad = down_grad[:rows].astype(F32)
    qkv_rows = jnp.concatenate(
        [
            join_heads(total[:, :, :qwide], heads),
            jnp.sum(total[:, :, qwide : qwide + 2 * HEAD].astype(F32), 0).astype(BF16),
        ],
        1,
    )
    dense_rows = join_heads(dense_total[:, :, lead:], heads)

    def own_columns(values):
        mine, other = half_of(values, core, 1)
        return in_order(mine, swap(other), core, 0)[:rows].astype(F32)

    stats = unpad(stats)
    return (
        layer_output[None],
        unpad(input_grad)[None],
        stats[0],
        stats[1],
        own_columns(qkv_rows),
        up_grad,
        own_columns(dense_rows),
        down_grad,
    )


def solution(mesh):
    split = P("ctx", "fsdp")
    stream = P("fsdp", "ctx", None)
    return jax.shard_map(
        body,
        mesh=mesh,
        in_specs=(stream, stream, P(), P(), split, split, split, split),
        out_specs=(stream, stream, P(), P(), split, split, split, split),
        check_vma=False,
    )
```

```python
import functools

import jax
import jax.numpy as jnp
from jax import lax
from jax.experimental import pallas as pl
from jax.experimental.pallas import tpu as pltpu
from jax.sharding import PartitionSpec as P

HEADS = 71
HEAD = 64
EPS = 1e-05
ROPE_BASE = 10000.0
MASKED = -1e30
LANES = 128
F32 = jnp.float32
BF16 = jnp.bfloat16
ROWS_COLS = (((1,), (1,)), ((), ()))
ROWS_ROWS = (((0,), (0,)), ((), ()))
MESH = pl.DeviceIdType.MESH
ANY = pl.BlockSpec(memory_space=pl.ANY)
WHOLE = pl.BlockSpec(memory_space=pltpu.VMEM)
DMA = pltpu.SemaphoreType.DMA


def dot(a, b, dims=None):
    if dims is None:
        return jnp.dot(a, b, preferred_element_type=F32)
    return lax.dot_general(a, b, dims, preferred_element_type=F32)


def grid_of(chips):
    return (4, 4, 4) if chips == 64 else (chips // 4, 2, 2)


def padded_rows(rows):
    return -(-rows // 16) * 16


def tile_share(tiles, chips):
    return tiles // chips, tiles % chips


class Place:
    def __init__(self, chips):
        self.chips = chips
        self.nz, self.ny, self.nx = grid_of(chips)
        self.me = lax.axis_index("ctx")
        self.core = lax.axis_index("fsdp")
        self.z = self.me // (self.ny * self.nx)
        self.y = lax.rem(self.me // self.nx, self.ny)
        self.x = lax.rem(self.me, self.nx)

    def at(self, dz, dy, dx):
        z = lax.rem(self.z + dz + self.nz, self.nz)
        y = lax.rem(self.y + dy + self.ny, self.ny)
        x = lax.rem(self.x + dx + self.nx, self.nx)
        return (z * self.ny + y) * self.nx + x

    def pair(self, i):
        return self.me ^ i


def enter(place):
    barrier = pltpu.get_barrier_semaphore()

    def greet(i):
        pl.semaphore_signal(barrier, 1, device_id=(place.pair(i), place.core), device_id_type=MESH)

    each(1, place.chips, greet)
    pl.semaphore_signal(barrier, 1, device_id=(place.me, 1 - place.core), device_id_type=MESH)
    pl.semaphore_wait(barrier, place.chips)


def remote(src, dst, send, recv, chip, core):
    return pltpu.make_async_remote_copy(
        src_ref=src, dst_ref=dst, send_sem=send, recv_sem=recv, device_id=(chip, core), device_id_type=MESH
    )


def each(first, last, do):
    def step(i, carry):
        do(i)
        return carry

    lax.fori_loop(first, last, step, 0)


def when(condition, do):
    if condition is None:
        do()
    else:
        pl.when(condition)(do)


def rows_at(start, count):
    return pl.ds(pl.multiple_of(start, 8), count)


def lanes_at(tile, count):
    return pl.ds(pl.multiple_of(tile * LANES, LANES), count * LANES)


def move(src, dst, sem):
    copy = pltpu.make_async_copy(src, dst, sem)
    copy.start()
    copy.wait()


class Tiles:
    def __init__(self, columns, chips):
        self.chips = chips
        self.least, self.richer = tile_share(columns // LANES, chips)
        assert 0 < self.least and 2 * self.richer <= chips

    def more(self, chip, core):
        return jnp.where(core == 0, chip < self.richer, chip >= self.chips - self.richer)

    def first(self, chip, core):
        late = jnp.maximum(chip - (self.chips - self.richer), 0)
        return self.least * chip + jnp.where(core == 0, jnp.minimum(chip, self.richer), late)

    def cut(self, ref, chip, core):
        start = self.first(chip, core)
        return (
            ref.at[:, lanes_at(start, self.least)],
            ref.at[:, lanes_at(jnp.minimum(start + self.least, self.first(self.chips, core) - 1), 1)],
        )


class Gather:
    @staticmethod
    def shape(chips, a):
        return (chips, *a.shape)

    @staticmethod
    def scratch(chips, a):
        nz, ny, nx = grid_of(chips)
        return [DMA((nz,))] * 2 + [DMA((nz, nx))] * 2 + [DMA((nz, ny))] * 2 + [DMA((nz, nx, ny))] * 4 + [DMA, DMA((nz,))]

    def __init__(self, place, mine, out, sems):
        self.p, self.mine, self.out = place, mine, out
        (self.sl, self.rl, self.sx, self.rx, self.sy, self.ry, self.s1, self.r1, self.s2, self.r2, self.own, self.sr) = sems
        self.half = mine.shape[0] // 2

    def line(self, k):
        p = self.p
        return remote(self.mine, self.out.at[p.me], self.sl.at[k], self.rl.at[k], p.at(k, 0, 0), p.core)

    def direct(self, k):
        p = self.p
        to = lax.rem(p.z + k, p.nz)
        middle = p.nz // 2
        far = ((to == p.nz - 1) & (p.z < middle)) | ((to == 0) & (p.z >= middle))
        return jnp.logical_not(far)

    def relay(self, k):
        p = self.p
        source = lax.rem(p.z - k + p.nz, p.nz)
        middle = p.nz // 2
        up = (p.z == p.nz - 2) & (source < middle)
        down = (p.z == 1) & (source >= middle)
        b = p.at(-k, 0, 0)
        index = jnp.where(up, k + 1, k - 1)
        copy = remote(self.out.at[b], self.out.at[b], self.sr.at[k], self.rl.at[index], p.at(jnp.where(up, 1, -1), 0, 0), p.core)
        return copy, up | down

    def across(self, k, i):
        p = self.p
        b = p.at(-k, 0, 0)
        src = self.mine if isinstance(k, int) and k == 0 else self.out.at[b]
        return remote(src, self.out.at[b], self.sx.at[k, i], self.rx.at[k, i], p.at(0, 0, i), p.core)

    def along(self, k, j):
        p = self.p
        b = p.at(-k, 0, 0)
        src = self.mine if isinstance(k, int) and k == 0 else self.out.at[b]
        return remote(src, self.out.at[b], self.sy.at[k, j], self.ry.at[k, j], p.at(0, j, 0), p.core)

    def corner1(self, k, i, j):
        p = self.p
        part = self.out.at[p.at(-k, 0, -i), pl.ds(0, self.half)]
        return remote(part, part, self.s1.at[k, i, j], self.r1.at[k, i, j], p.at(0, j, 0), p.core)

    def corner2(self, k, i, j):
        p = self.p
        part = self.out.at[p.at(-k, -j, 0), pl.ds(self.half, self.half)]
        return remote(part, part, self.s2.at[k, i, j], self.r2.at[k, i, j], p.at(0, 0, i), p.core)

    def spread(self, k):
        for i in range(1, self.p.nx):
            self.across(k, i).start()
        for j in range(1, self.p.ny):
            self.along(k, j).start()

    def begin(self):
        for k in range(1, self.p.nz):
            pl.when(self.direct(k))(self.line(k).start)
        self.spread(0)
        pltpu.make_async_copy(self.mine, self.out.at[self.p.me], self.own).start()

    def turn(self, k):
        p = self.p
        for i in range(1, p.nx):
            self.across(k, i).wait_recv()
            for j in range(1, p.ny):
                self.corner1(k, i, j).start()
        for j in range(1, p.ny):
            self.along(k, j).wait_recv()
            for i in range(1, p.nx):
                self.corner2(k, i, j).start()

    def steps(self):
        p = self.p
        assert p.nz == 4
        first = jnp.where(p.z == 0, 3, 1)
        last = jnp.where(p.z == 0, 1, jnp.where(p.z == 3, 3, 2))
        order = [first, 6 - first - last, last]

        def come(k):
            self.line(k).wait_recv()
            copy, needed = self.relay(k)
            pl.when(needed)(copy.start)
            self.spread(k)

        return (
            [functools.partial(self.turn, 0)]
            + [functools.partial(come, k) for k in order]
            + [functools.partial(self.turn, k) for k in order]
        )

    def end(self):
        p = self.p
        pltpu.make_async_copy(self.mine, self.out.at[p.me], self.own).wait()
        for k in range(p.nz):
            if k:
                pl.when(self.direct(k))(self.line(k).wait_send)
                copy, needed = self.relay(k)
                pl.when(needed)(copy.wait_send)
            for i in range(1, p.nx):
                self.across(k, i).wait_send()
            for j in range(1, p.ny):
                self.along(k, j).wait_send()
            for i in range(1, p.nx):
                for j in range(1, p.ny):
                    self.corner1(k, i, j).wait()
                    self.corner2(k, i, j).wait()


class Columns:
    @staticmethod
    def shape(chips, a):
        least, _ = tile_share(a.shape[1] // LANES, chips)
        return (chips * a.shape[0], (2 * least + 1) * LANES)

    @staticmethod
    def scratch(chips, a):
        return [DMA((chips,))] * 8 + [pltpu.VMEM((a.shape[0], LANES), a.dtype)]

    def __init__(self, place, weight, out, sems):
        self.p, self.w, self.out = place, weight, out
        self.ms, self.mr, self.es, self.er, self.fs, self.fr, self.gs, self.gr, self.nought = sems
        self.tiles = Tiles(weight.shape[1], place.chips)
        self.rows = weight.shape[0]

    def slots(self, chip, own):
        rows = rows_at(chip * self.rows, self.rows)
        least = self.tiles.least
        return self.out.at[rows, lanes_at(0 if own else least + 1, least)], self.out.at[rows, lanes_at(least, 1)]

    def sends(self, i):
        p = self.p
        chip = p.pair(i)
        (a, b), (c, d) = self.tiles.cut(self.w, chip, p.core), self.slots(p.me, True)
        return (
            remote(a, c, self.ms.at[i], self.mr.at[i], chip, p.core),
            remote(b, d, self.es.at[i], self.er.at[i], chip, p.core),
            self.tiles.more(chip, p.core),
        )

    def gets(self, i):
        p = self.p
        chip = p.pair(i)
        (a, b), (c, d) = self.tiles.cut(self.w, chip, p.core), self.slots(chip, True)
        return (
            remote(a, c, self.ms.at[i], self.mr.at[i], chip, p.core),
            remote(b, d, self.es.at[i], self.er.at[i], chip, p.core),
        )

    def passes(self, i):
        p = self.p
        chip = p.pair(i)
        a, b = self.slots(chip, True)
        if isinstance(i, int) and i == 0:
            a, b = self.tiles.cut(self.w, p.me, p.core)
        c, d = self.slots(chip, False)
        return (
            remote(a, c, self.fs.at[i], self.fr.at[i], p.me, 1 - p.core),
            remote(b, d, self.gs.at[i], self.gr.at[i], p.me, 1 - p.core),
        )

    def here(self):
        p = self.p
        (a, b), (c, d) = self.tiles.cut(self.w, p.me, p.core), self.slots(p.me, True)
        return pltpu.make_async_copy(a, c, self.ms.at[0]), pltpu.make_async_copy(b, d, self.es.at[0])

    def begin(self):
        p = self.p

        def send(i):
            main, extra, more = self.sends(i)
            main.start()
            pl.when(more)(extra.start)

        each(1, p.chips, send)
        own, pass_on = self.here(), self.passes(0)
        own[0].start()
        pass_on[0].start()

        @pl.when(self.tiles.more(p.me, p.core))
        def _():
            own[1].start()
            pass_on[1].start()

    def steps(self):
        return [self.hand_on]

    def hand_on(self):
        p = self.p
        mine = self.tiles.more(p.me, p.core)

        def hand(i):
            main, extra = self.gets(i)
            to_main, to_extra = self.passes(i)
            main.wait_recv()
            to_main.start()

            @pl.when(mine)
            def _():
                extra.wait_recv()
                to_extra.start()

        each(1, p.chips, hand)

    def end(self):
        p = self.p
        mine = self.tiles.more(p.me, p.core)
        theirs = self.tiles.more(p.me, 1 - p.core)
        own = self.here()
        own[0].wait()
        pl.when(mine)(own[1].wait)

        @pl.when(jnp.logical_not(mine | theirs))
        def _():
            self.nought[...] = jnp.zeros_like(self.nought)
            each(0, p.chips, lambda c: move(self.nought, self.slots(c, True)[1], self.es.at[0]))

        def sent(i):
            main, extra, more = self.sends(i)
            main.wait_send()
            pl.when(more)(extra.wait_send)

        each(1, p.chips, sent)

        def handed(i):
            main, extra = self.passes(i)
            main.wait()
            pl.when(mine)(extra.wait_send)
            pl.when(theirs)(extra.wait_recv)

        handed(0)
        each(1, p.chips, handed)


class Blocks:
    @staticmethod
    def shape(chips, a):
        return (chips * 2 * a.shape[1], a.shape[2])

    @staticmethod
    def scratch(chips, a):
        return [DMA((chips,))] * 4

    def __init__(self, place, blocks, out, sems):
        self.p, self.b, self.out = place, blocks, out
        self.s, self.r, self.fs, self.fr = sems
        self.rows = blocks.shape[1]

    def slot(self, chip, core):
        return self.out.at[rows_at((2 * chip + core) * self.rows, self.rows)]

    def sends(self, i):
        p = self.p
        chip = p.pair(i)
        return remote(self.b.at[chip], self.slot(p.me, p.core), self.s.at[i], self.r.at[i], chip, p.core)

    def passes(self, i):
        p = self.p
        part = self.slot(p.pair(i), p.core)
        mine = self.b.at[p.me] if isinstance(i, int) and i == 0 else part
        return remote(mine, part, self.fs.at[i], self.fr.at[i], p.me, 1 - p.core)

    def here(self):
        p = self.p
        return pltpu.make_async_copy(self.b.at[p.me], self.slot(p.me, p.core), self.s.at[0])

    def begin(self):
        each(1, self.p.chips, lambda i: self.sends(i).start())
        self.here().start()
        self.passes(0).start()

    def steps(self):
        return [self.hand_on]

    def hand_on(self):
        def hand(i):
            self.sends(i).wait_recv()
            self.passes(i).start()

        each(1, self.p.chips, hand)

    def end(self):
        p = self.p
        self.here().wait()
        each(1, p.chips, lambda i: self.sends(i).wait_send())
        self.passes(0).wait()
        each(1, p.chips, lambda i: self.passes(i).wait())


def drive(parts):
    for part in parts:
        part.begin()
    todo = [part.steps() for part in parts]
    total = max(len(steps) for steps in todo)
    for at in range(total):
        for steps in todo:
            index = at - (total - len(steps))
            if index >= 0:
                steps[index]()
    for part in parts:
        part.end()


def take(refs, counts):
    out, at = [], 0
    for count in counts:
        out.append(refs[at : at + count])
        at += count
    return out


def bring_kernel(chips, plan, *refs):
    n = len(plan)
    ins, outs, held = refs[:n], refs[n : 2 * n], refs[2 * n :]
    place = Place(chips)
    enter(place)
    held = take(held, [count for _, count in plan])
    drive([kind(place, a, o, h) for (kind, _), a, o, h in zip(plan, ins, outs, held)])


def bring(chips, number, name, *jobs):
    held = [kind.scratch(chips, a) for kind, a in jobs]
    return pl.pallas_call(
        functools.partial(bring_kernel, chips, [(kind, len(h)) for (kind, _), h in zip(jobs, held)]),
        in_specs=[ANY] * len(jobs),
        out_specs=[ANY] * len(jobs),
        out_shape=[jax.ShapeDtypeStruct(kind.shape(chips, a), a.dtype) for kind, a in jobs],
        scratch_shapes=[s for h in held for s in h],
        compiler_params=pltpu.CompilerParams(collective_id=number, has_side_effects=True, vmem_limit_bytes=16 << 20),
        name=name,
    )(*[a for _, a in jobs])


class Paired:
    @staticmethod
    def scratch(chips, shape, dtype):
        return [DMA((chips,))] * 5 + [pltpu.VMEM((chips, *shape), dtype)] * 2

    def __init__(self, place, held, views, gives=None, sums=None, comes=lambda j: None):
        self.p = place
        self.cs, self.cr, self.s, self.r, self.load, self.total, self.stage = held
        self.mine, self.theirs, self.target, self.source = views
        self.gives, self.sums, self.comes = gives, sums, comes

    def across(self, i):
        p = self.p
        return remote(self.theirs(p.pair(i)), self.stage.at[i], self.cs.at[i], self.cr.at[i], p.me, 1 - p.core)

    def fetch(self, i):
        return pltpu.make_async_copy(self.mine(self.p.pair(i)), self.total.at[i], self.load.at[i])

    def sends(self, i):
        p = self.p
        j = p.pair(i)
        return remote(self.total.at[i], self.target(j), self.s.at[i], self.r.at[i], j, p.core)

    def gets(self, i):
        p = self.p
        j = p.pair(i)
        return remote(self.total.at[i], self.source(j), self.s.at[i], self.r.at[i], j, p.core)

    def here(self):
        return pltpu.make_async_copy(self.total.at[0], self.source(self.p.me), self.s.at[0])

    def begin(self):
        chips = self.p.chips
        when(self.gives, lambda: each(0, chips, lambda i: self.across(i).start()))
        when(self.sums, lambda: each(0, chips, lambda i: self.fetch(i).start()))

    def add(self, i):
        self.fetch(i).wait()
        self.across(i).wait_recv()
        self.total[i] = (self.total[i].astype(F32) + self.stage[i].astype(F32)).astype(self.total.dtype)

    def some(self, first, last):
        def do(i):
            self.add(i)
            self.sends(i).start()

        when(self.sums, lambda: each(first, last, do))

    def own(self):
        def do():
            self.add(0)
            self.here().start()

        when(self.sums, do)

    def end(self):
        chips = self.p.chips
        when(self.gives, lambda: each(0, chips, lambda i: self.across(i).wait_send()))

        def sent():
            self.here().wait()
            each(1, chips, lambda i: self.sends(i).wait_send())

        when(self.sums, sent)

        def came(i):
            when(self.comes(self.p.pair(i)), lambda: self.gets(i).wait_recv())

        each(1, chips, came)

    def steps(self):
        chips = self.p.chips
        return [functools.partial(self.some, 1, chips), self.own]


class Scatter:
    @staticmethod
    def stages(chips, a):
        nz, _, n = grid_of(chips)
        _, t, d = a.shape
        h = t // 2
        return [(2, nz, n, n, h, d), (2, nz, n, h, d), (2, nz, n, h, d), (nz, t, d), (nz, t, d)]

    @staticmethod
    def scratch(chips, a):
        nz, _, n = grid_of(chips)
        _, t, d = a.shape
        h = t // 2
        most = max(n, nz)
        sems = [DMA((2, nz, n, n))] * 2 + [DMA((2, nz, n))] * 2 + [DMA((nz,))] * 2 + [DMA((most,)), DMA]
        return sems + [pltpu.VMEM((most, h, d), a.dtype), pltpu.VMEM((h, d), a.dtype)]

    def __init__(self, place, blocks, stages, held):
        self.p, self.b = place, blocks
        self.got1, self.sum1, self.got2, self.sum2, self.got3 = stages
        (self.s1, self.r1, self.s2, self.r2, self.s3, self.r3, self.load, self.store, self.parts, self.low) = held
        self.h = blocks.shape[1] // 2
        self.n = place.nx

    def chip(self, half, dz, du, dv):
        return self.p.at(dz, dv, du) if half == 0 else self.p.at(dz, du, dv)

    def rows(self, half):
        return pl.ds(half * self.h, self.h)

    def send1(self, half, dz, v, i):
        return remote(
            self.b.at[self.chip(half, dz, i, v), self.rows(half)],
            self.got1.at[half, dz, v, i],
            self.s1.at[half, dz, v, i],
            self.r1.at[half, dz, v, i],
            self.chip(half, 0, i, 0),
            self.p.core,
        )

    def send2(self, half, dz, v):
        return remote(
            self.sum1.at[half, dz, v],
            self.got2.at[half, dz, v],
            self.s2.at[half, dz, v],
            self.r2.at[half, dz, v],
            self.chip(half, 0, 0, v),
            self.p.core,
        )

    def send3(self, dz):
        return remote(
            self.sum2.at[dz], self.got3.at[dz], self.s3.at[dz], self.r3.at[dz], self.p.at(dz, 0, 0), self.p.core
        )

    def fetch(self, refs):
        loads = [pltpu.make_async_copy(r, self.parts.at[i], self.load.at[i]) for i, r in enumerate(refs)]
        for copy in loads:
            copy.start()
        for copy in loads:
            copy.wait()

    def add(self, refs, to):
        self.fetch(refs)
        total = self.parts[0].astype(F32)
        for i in range(1, len(refs)):
            total = total + self.parts[i].astype(F32)
        self.low[...] = total.astype(self.low.dtype)
        move(self.low, to, self.store)

    def order(self):
        nz = self.p.nz
        return [nz // 2] + [k for k in range(1, nz) if k != nz // 2] + [0]

    def begin(self):
        for dz in self.order():
            for half in (0, 1):
                for v in list(range(1, self.n)) + [0]:
                    for i in range(1, self.n):
                        self.send1(half, dz, v, i).start()

    def first(self, dz):
        for half in (0, 1):
            for v in list(range(1, self.n)) + [0]:
                for i in range(1, self.n):
                    self.send1(half, dz, v, i).wait_recv()
                mine = self.b.at[self.chip(half, dz, 0, v), self.rows(half)]
                self.add([mine] + [self.got1.at[half, dz, v, i] for i in range(1, self.n)], self.sum1.at[half, dz, v])
                if v:
                    self.send2(half, dz, v).start()

    def second(self, dz):
        for half in (0, 1):
            for v in range(1, self.n):
                self.send2(half, dz, v).wait_recv()
            parts = [self.sum1.at[half, dz, 0]] + [self.got2.at[half, dz, v] for v in range(1, self.n)]
            self.add(parts, self.sum2.at[dz, self.rows(half)])
        if dz:
            self.send3(dz).start()

    def last(self):
        for dz in range(1, self.p.nz):
            self.send3(dz).wait_recv()
        for half in (0, 1):
            rows = self.rows(half)
            self.fetch([self.sum2.at[0, rows]] + [self.got3.at[dz, rows] for dz in range(1, self.p.nz)])
            self.finish(half)

    def steps(self):
        order = self.order()
        steps = [functools.partial(self.first, order[0])]
        for old, new in zip(order[:-1], order[1:]):
            steps += [functools.partial(self.first, new), functools.partial(self.second, old)]
        return steps + [functools.partial(self.second, order[-1]), self.last]

    def end(self):
        for dz in range(self.p.nz):
            for half in (0, 1):
                for v in range(self.n):
                    for i in range(1, self.n):
                        self.send1(half, dz, v, i).wait_send()
                    if v:
                        self.send2(half, dz, v).wait_send()
            if dz:
                self.send3(dz).wait_send()


class NormBack(Scatter):
    @staticmethod
    def scratch(chips, a):
        d = a.shape[2]
        more = [pltpu.VMEM((2, 8, d), F32), pltpu.VMEM((2, d), F32), pltpu.VMEM((2, d), F32), pltpu.VMEM((chips, 2, d), F32)]
        return Scatter.scratch(chips, a) + more + [DMA((chips,))] * 2 + [DMA((3,))]

    def __init__(self, place, blocks, stages, held, operands, results, features):
        super().__init__(place, blocks, stages, held[:10])
        self.sums, self.mine, self.other, self.slots, self.ss, self.sr, self.pairs = held[10:]
        self.xhat, self.grad, self.gain, self.inverse = operands
        self.input_grad, self.stats = results
        self.features = features

    def begin(self):
        super().begin()
        self.sums[...] = jnp.zeros_like(self.sums)

    def finish(self, half):
        d = self.xhat.shape[1]

        def some(c):
            at = pl.multiple_of(c * 16, 16)
            total = self.parts[0, pl.ds(at, 16)].astype(F32)
            for i in range(1, self.p.nz):
                total = total + self.parts[i, pl.ds(at, 16)].astype(F32)
            rows = pl.ds(pl.multiple_of(half * self.h + c * 16, 16), 16)
            xhat = self.xhat[rows]
            both = total * xhat
            self.sums[0] += both[:8] + both[8:]
            self.sums[1] += total[:8] + total[8:]
            scaled = total * self.gain[...]
            mean = jnp.sum(scaled, 1, keepdims=True) / self.features
            slope = jnp.sum(scaled * xhat, 1, keepdims=True) / self.features
            change = (scaled - mean - xhat * slope) * self.inverse[rows]
            self.input_grad[rows] = self.grad[rows].astype(F32) + change

        each(0, self.h // 16, some)

    def swap_stats(self):
        p = self.p
        return remote(self.mine, self.other, self.pairs.at[0], self.pairs.at[1], p.me, 1 - p.core)

    def share_stats(self, i):
        p = self.p
        return remote(self.mine, self.slots.at[p.me], self.ss.at[i], self.sr.at[i], p.pair(i), p.core)

    def get_stats(self, i):
        p = self.p
        return remote(self.mine, self.slots.at[p.pair(i)], self.ss.at[i], self.sr.at[i], p.pair(i), p.core)

    def stats_out(self):
        self.mine[0:1] = jnp.sum(self.sums[0], 0, keepdims=True)
        self.mine[1:2] = jnp.sum(self.sums[1], 0, keepdims=True)
        self.swap_stats().start()
        self.swap_stats().wait()
        self.mine[...] += self.other[...]
        self.slots[self.p.me] = self.mine[...]
        each(1, self.p.chips, lambda i: self.share_stats(i).start())

    def steps(self):
        return super().steps() + [self.stats_out]

    def end(self):
        super().end()

        def done(i):
            self.share_stats(i).wait_send()
            self.get_stats(i).wait_recv()

        each(1, self.p.chips, done)
        self.stats[...] = self.slots[0]

        def more(c):
            self.stats[...] += self.slots[c]

        each(1, self.p.chips, more)


def return_parts(place, part, out, held):
    tiles = Tiles(out.shape[1], place.chips)
    least, rows, core, me = tiles.least, out.shape[0], place.core, place.me
    n = len(held) // 2

    def at(j, tile, count):
        return part.at[rows_at(j * rows, rows), lanes_at(tile, count)]

    main = Paired(
        place,
        held[:n],
        (
            lambda j: at(j, 0, least),
            lambda j: at(j, least + 1, least),
            lambda j: tiles.cut(out, me, core)[0],
            lambda j: tiles.cut(out, j, core)[0],
        ),
    )
    extra = Paired(
        place,
        held[n:],
        (
            lambda j: at(j, least, 1),
            lambda j: at(j, least, 1),
            lambda j: tiles.cut(out, me, core)[1],
            lambda j: tiles.cut(out, j, core)[1],
        ),
        tiles.more(me, 1 - core),
        tiles.more(me, core),
        lambda j: tiles.more(j, core),
    )
    return [main, extra]


def trade_parts(place, part, out, held):
    rows = out.shape[1]

    def at(j, core):
        return part.at[rows_at((2 * j + core) * rows, rows)]

    views = (
        lambda j: at(j, place.core),
        lambda j: at(j, 1 - place.core),
        lambda j: out.at[place.me],
        lambda j: out.at[j],
    )
    return [Paired(place, held, views)]


def send_kernel(chips, features, counts, *refs):
    x_ref, a_ref, b_ref, blocks, xhat, grad, gain, inverse = refs[:8]
    input_grad, stats, wide_out, small_out, wide, small = refs[8:14]
    stages = refs[14:19]
    wide_tile, small_tile, stored = refs[19:22]
    norm_held, wide_held, small_held = take(refs[22:], counts)
    step = pl.program_id(0)
    count = pl.num_programs(0) - 1
    width = x_ref.shape[2]
    place = Place(chips)
    norm = NormBack(place, blocks, stages, norm_held, (xhat, grad, gain, inverse), (input_grad, stats), features)
    parts = return_parts(place, wide, wide_out, wide_held)
    parts += trade_parts(place, small, small_out, small_held)

    def stores(at):
        slot = lax.rem(at, 2)
        rows = rows_at(at * width, width)
        return (
            pltpu.make_async_copy(wide_tile.at[slot], wide.at[rows], stored.at[0, slot]),
            pltpu.make_async_copy(small_tile.at[slot], small.at[rows], stored.at[1, slot]),
        )

    def done(at):
        for copy in stores(at):
            copy.wait()

    @pl.when(step == 0)
    def _():
        enter(place)
        norm.begin()

    @pl.when(step < count)
    def _():
        slot = lax.rem(step, 2)
        pl.when(step >= 2)(lambda: done(step - 2))
        x = flat(x_ref)
        small_tile[slot] = dot(x, a_ref[...], ROWS_ROWS).astype(BF16)
        for at, n in chunks(b_ref.shape[1], 384):
            wide_tile[slot, :, at : at + n] = dot(x, b_ref[:, at : at + n], ROWS_ROWS).astype(BF16)
        for copy in stores(step):
            copy.start()

    @pl.when(step == count)
    def _():
        done(step - 2)
        done(step - 1)
        for part in parts:
            part.begin()
        ahead, *rest = norm.steps()
        ahead()
        for part in parts:
            for do in part.steps():
                do()
        for do in rest:
            do()
        for part in [norm] + parts:
            part.end()


def send(chips, number, features, blocks, x, a, b, columns, xhat, grad, gain, inverse):
    _, tokens, d = blocks.shape
    length = chips * tokens
    rows = d // chips
    least, _ = tile_share(columns // LANES, chips)
    low, wide = a.shape[1], b.shape[1]
    width = 768 if d % 768 == 0 else 512
    count = d // width
    held = [
        NormBack.scratch(chips, blocks),
        Paired.scratch(chips, (rows, least * LANES), BF16) + Paired.scratch(chips, (rows, LANES), BF16),
        Paired.scratch(chips, (rows // 2, low), BF16),
    ]
    half = lambda *shape: jax.ShapeDtypeStruct(shape, BF16)
    results = pl.pallas_call(
        functools.partial(send_kernel, chips, features, [len(h) for h in held]),
        grid=(count + 1,),
        in_specs=[
            pl.BlockSpec((chips, tokens, width), lambda i: (0, 0, jnp.minimum(i, count - 1))),
            resident(a.shape),
            resident(b.shape),
            ANY,
            resident(xhat.shape),
            resident(grad.shape),
            resident(gain.shape),
            resident(inverse.shape),
        ],
        out_specs=[resident((tokens, d)), resident((2, d))] + [ANY] * 9,
        out_shape=[
            jax.ShapeDtypeStruct((tokens, d), F32),
            jax.ShapeDtypeStruct((2, d), F32),
            half(rows, columns),
            half(chips, rows // 2, low),
            half(d, wide),
            half(d, low),
        ]
        + [half(*s) for s in Scatter.stages(chips, blocks)],
        scratch_shapes=[pltpu.VMEM((2, width, wide), BF16), pltpu.VMEM((2, width, low), BF16), DMA((2, 2))]
        + [s for h in held for s in h],
        compiler_params=pltpu.CompilerParams(collective_id=number, has_side_effects=True, vmem_limit_bytes=60 << 20),
        cost_estimate=pl.CostEstimate(
            flops=2 * length * d * (low + wide), transcendentals=0, bytes_accessed=2 * length * d
        ),
        name="send",
    )(x, a, b, blocks, xhat, grad, gain, inverse)
    return results[:4]


def rotate(values, cosines, sines):
    middle = values.shape[-1] // 2
    turned = jnp.concatenate([-values[..., middle:], values[..., :middle]], -1)
    return values * cosines + turned * sines


def rotate_back(values, cosines, sines):
    middle = values.shape[-1] // 2
    turned = jnp.concatenate([values[..., middle:], -values[..., :middle]], -1)
    return values * cosines + turned * sines


def flat(ref):
    return ref[...].reshape(ref.shape[0] * ref.shape[1], ref.shape[2])


def chunks(width, most):
    return [(at, min(most, width - at)) for at in range(0, width, most)]


def resident(shape, column=0):
    return pl.BlockSpec(shape, lambda i: (0, column), pipeline_mode=pl.Buffered(1))


def per_row(rows, width):
    return pl.BlockSpec((rows, width), lambda i: (i, 0))


def forward_kernel(chips, plan, lead, events, *refs):
    n = len(plan)
    x_ref, small_ref, wide_ref, cos_ref, sin_ref = refs[:5]
    ins, refs = refs[5 : 5 + n], refs[5 + n :]
    q_out, k_out, v_out, hidden_ref, slope_ref, low_ref, o_ref, lse_ref = refs[:8]
    outs, refs = refs[8 : 8 + n], refs[8 + n :]
    q_all, k_all, v_all, acc, top = refs[:5]
    held = take(refs[5:], [count for _, count in plan])
    step = pl.program_id(0)
    half = pl.num_programs(0) // 2
    heads, rows, _ = q_out.shape
    place = Place(chips)
    parts = [kind(place, a, o, h) for (kind, _), a, o, h in zip(plan, ins, outs, held)]

    @pl.when(step == 0)
    def _():
        enter(place)
        for part in parts:
            part.begin()

    @pl.when(step < half)
    def _():
        here = pl.ds(pl.multiple_of(step * rows, rows), rows)
        x = flat(x_ref)
        cosines, sines = cos_ref[...], sin_ref[...]
        joined = dot(x, small_ref[...])
        for h in range(heads):
            q = rotate(joined[:, h * HEAD : (h + 1) * HEAD], cosines, sines).astype(BF16) * HEAD ** (-0.5)
            q_out[h] = q
            q_all[h, here] = q
        at = heads * HEAD
        k = rotate(joined[:, at : at + HEAD], cosines, sines).astype(BF16)
        v = joined[:, at + HEAD : at + 2 * HEAD].astype(BF16)
        k_out[...] = k
        v_out[...] = v
        k_all[here] = k
        v_all[here] = jnp.concatenate([v, jnp.ones_like(v)], 1)
        for at, width in chunks(wide_ref.shape[1], 384):
            up = dot(x, wide_ref[:, at : at + width])
            bell = 0.5 + 0.5 * lax.erf(up * 0.5**0.5)
            hidden_ref[:, at : at + width] = (up * bell).astype(BF16)
            slope = bell + up * jnp.exp(up * up * -0.5) * (2 * jnp.pi) ** (-0.5)
            slope_ref[:, at : at + width] = slope.astype(BF16)

    @pl.when(step >= half)
    def _():
        index = step - half
        here = pl.ds(pl.multiple_of(index * rows, rows), rows)
        lows = []
        for h in range(heads):
            q = q_all[h, here]
            acc[...] = jnp.zeros_like(acc)
            top[...] = jnp.full_like(top, MASKED)

            def block(start, masked):
                s = dot(q, k_all[pl.ds(start, rows), :], ROWS_COLS)
                if masked:
                    key = lax.broadcasted_iota(jnp.int32, s.shape, 1)
                    query = lax.broadcasted_iota(jnp.int32, s.shape, 0)
                    s = jnp.where(key <= query, s, MASKED)
                old = top[...]
                new = jnp.maximum(old, jnp.max(s, 1, keepdims=True))
                p = jnp.exp(s - new).astype(BF16)
                acc[...] = acc[...] * jnp.exp(old - new) + dot(p, v_all[pl.ds(start, rows), :])
                top[...] = new

            each(0, index, lambda i: block(pl.multiple_of(i * rows, rows), False))
            block(pl.multiple_of(index * rows, rows), True)
            total = acc[...]
            norm = total[:, HEAD : HEAD + 1]
            out = total[:, :HEAD] / norm
            o_ref[h] = out
            lows.append(out.astype(BF16))
            lse = jnp.broadcast_to(top[...] + jnp.log(norm), (rows, LANES))
            lse_ref[h] = lse.T[:1]
        if lead:
            lows = [jnp.zeros((rows, lead), BF16)] + lows
        low_ref[...] = jnp.concatenate(lows, 1)

    todo = []
    longest = max(len(part.steps()) for part in parts)
    for at in range(longest):
        for part in parts:
            steps = part.steps()
            index = at - (longest - len(steps))
            if index >= 0:
                todo.append(steps[index])
    cuts = [0, *[c for _, c in events], len(todo)]
    for (back, _), first, last in zip([*events, (0, None)], cuts[:-1], cuts[1:]):

        @pl.when(step == pl.num_programs(0) - 1 - back)
        def _():
            for do in todo[first:last]:
                do()

    @pl.when(step == pl.num_programs(0) - 1)
    def _():
        for part in parts:
            part.end()


def forward(x, small, wide, cosines, sines, heads, lead, number, jobs):
    chips, tokens, d = x.shape
    length = chips * tokens
    step = max(1, 512 // tokens)
    rows = step * tokens
    half = chips // step
    width = -(-(heads + 2) * HEAD // LANES) * LANES
    n = wide.shape[1]
    low = lead + heads * HEAD
    held = [kind.scratch(chips, a) for kind, a in jobs]
    plan = [(kind, len(h)) for (kind, _), h in zip(jobs, held)]
    early = lambda i: jnp.minimum(i, half - 1)
    late = lambda i: jnp.maximum(i - half, 0)
    first = lambda w: pl.BlockSpec((rows, w), lambda i: (early(i), 0))
    events = ((4, 1), (2, 3), (1, 4))
    results = pl.pallas_call(
        functools.partial(forward_kernel, chips, plan, lead, events),
        grid=(2 * half,),
        in_specs=[
            pl.BlockSpec((step, tokens, d), lambda i: (early(i), 0, 0)),
            resident((d, width)),
            resident((d, n)),
            first(HEAD),
            first(HEAD),
        ]
        + [ANY] * len(jobs),
        out_specs=[
            pl.BlockSpec((heads, rows, HEAD), lambda i: (0, early(i), 0)),
            first(HEAD),
            first(HEAD),
            first(n),
            first(n),
            pl.BlockSpec((rows, low), lambda i: (late(i), 0)),
            pl.BlockSpec((heads, rows, HEAD), lambda i: (0, late(i), 0)),
            pl.BlockSpec((heads, 1, rows), lambda i: (0, 0, late(i))),
        ]
        + [ANY] * len(jobs),
        out_shape=[
            jax.ShapeDtypeStruct((heads, length, HEAD), BF16),
            jax.ShapeDtypeStruct((length, HEAD), BF16),
            jax.ShapeDtypeStruct((length, HEAD), BF16),
            jax.ShapeDtypeStruct((length, n), BF16),
            jax.ShapeDtypeStruct((length, n), BF16),
            jax.ShapeDtypeStruct((length, low), BF16),
            jax.ShapeDtypeStruct((heads, length, HEAD), F32),
            jax.ShapeDtypeStruct((heads, 1, length), F32),
        ]
        + [jax.ShapeDtypeStruct(kind.shape(chips, a), a.dtype) for kind, a in jobs],
        scratch_shapes=[
            pltpu.VMEM((heads, length, HEAD), BF16),
            pltpu.VMEM((length, HEAD), BF16),
            pltpu.VMEM((length, 2 * HEAD), BF16),
            pltpu.VMEM((rows, 2 * HEAD), F32),
            pltpu.VMEM((rows, 1), F32),
        ]
        + [s for h in held for s in h],
        compiler_params=pltpu.CompilerParams(collective_id=number, has_side_effects=True, vmem_limit_bytes=58 << 20),
        cost_estimate=pl.CostEstimate(
            flops=2 * length * d * (n + width) + 2 * heads * length * length * HEAD,
            transcendentals=2 * length * n + heads * length * length // 2,
            bytes_accessed=2 * length * d,
        ),
        name="forward",
    )(x, small, wide, cosines, sines, *[a for _, a in jobs])
    return results[:8], results[8:]


def backward_kernel(chips, lead, counts, *refs):
    g_ref, dense_ref, down_ref, slope_ref, q_ref, k_ref, v_ref, o_ref, lse_ref, cos_ref, sin_ref = refs[:11]
    wide, small = refs[11:13]
    grad_ref, out_ref, wide_out, small_out = refs[13:17]
    g_all, acc, dk, dv = refs[17:21]
    wide_held, small_held = take(refs[21:], counts)
    heads, rows, _ = q_ref.shape
    length = g_all.shape[1]
    count = pl.num_programs(0) - length // rows
    step = pl.program_id(0)
    scale = HEAD ** (-0.5)
    place = Place(chips)
    parts = return_parts(place, wide, wide_out, wide_held) + trade_parts(place, small, small_out, small_held)

    @pl.when(step == 0)
    def _():
        enter(place)
        for part in parts:
            part.begin()

    @pl.when(step < count)
    def _():
        g = flat(g_ref)
        low = g.shape[0]
        here = pl.ds(pl.multiple_of(step * low, low), low)
        grad = dot(g, dense_ref[...]).astype(BF16)
        for h in range(heads):
            g_all[h, here] = grad[:, lead + h * HEAD : lead + (h + 1) * HEAD]
        for at, width in chunks(down_ref.shape[1], 384):
            part = dot(g, down_ref[:, at : at + width])
            grad_ref[:, at : at + width] = (part * slope_ref[:, at : at + width].astype(F32)).astype(BF16)

    @pl.when(step == count)
    def _():
        dk[...] = jnp.zeros_like(dk)
        dv[...] = jnp.zeros_like(dv)
        out_ref[...] = jnp.zeros_like(out_ref)

    @pl.when(step >= count)
    def _():
        index = step - count
        here = pl.ds(pl.multiple_of(index * rows, rows), rows)
        cosines, sines = cos_ref[here], sin_ref[here]
        grads = []
        for h in range(heads):
            q = q_ref[h]
            g = g_all[h, here]
            lse = lse_ref[h]
            delta = jnp.sum((g.astype(F32) * o_ref[h]).T, 0, keepdims=True)
            acc[...] = jnp.zeros_like(acc)

            def block(start, masked):
                at = pl.ds(start, rows)
                k = k_ref[at, :]
                p = jnp.exp(dot(k, q, ROWS_COLS) - lse)
                if masked:
                    key = lax.broadcasted_iota(jnp.int32, p.shape, 0)
                    query = lax.broadcasted_iota(jnp.int32, p.shape, 1)
                    p = jnp.where(key <= query, p, 0.0)
                dp = dot(v_ref[at, :], g, ROWS_COLS)
                ds = (p * (dp - delta)).astype(BF16)
                dv[at, :] += dot(p.astype(BF16), g)
                dk[at, :] += dot(ds, q)
                acc[...] += dot(ds, k, ROWS_ROWS)

            each(0, index, lambda i: block(pl.multiple_of(i * rows, rows), False))
            block(pl.multiple_of(index * rows, rows), True)
            grads.append(rotate_back(acc[...] * scale, cosines, sines).astype(BF16))
        out_ref[here, : heads * HEAD] = jnp.concatenate(grads, 1)

    @pl.when(step == 1)
    def _():
        for part in parts:
            for do in part.steps():
                do()

    @pl.when(step == pl.num_programs(0) - 1)
    def _():
        keys = rotate_back(dk[...], cos_ref[...], sin_ref[...]).astype(BF16)
        both = jnp.concatenate([keys, dv[...].astype(BF16)], 1)
        out_ref[:, heads * HEAD : (heads + 2) * HEAD] = both
        for part in parts:
            part.end()


def backward(g, small, lead, down, slope, q, k, v, o, lse, cosines, sines, number, down_part, dense_part, columns):
    chips, tokens, d = g.shape
    heads, length, _ = q.shape
    group = max(1, 256 // tokens)
    low = group * tokens
    count = chips // group
    rows = min(512, length)
    width = lead + heads * HEAD
    n = down.shape[1]
    out_width = -(-(heads + 2) * HEAD // LANES) * LANES
    high = d // chips
    least, _ = tile_share(columns // LANES, chips)
    held = [
        Paired.scratch(chips, (high, least * LANES), BF16) + Paired.scratch(chips, (high, LANES), BF16),
        Paired.scratch(chips, (high // 2, width), BF16),
    ]
    early = lambda i: jnp.minimum(i, count - 1)
    late = lambda i: jnp.maximum(i - count, 0)
    first = pl.BlockSpec((low, n), lambda i: (early(i), 0))
    per_query = pl.BlockSpec((heads, rows, HEAD), lambda i: (0, late(i), 0))
    whole = resident((length, HEAD))
    return pl.pallas_call(
        functools.partial(backward_kernel, chips, lead, [len(h) for h in held]),
        grid=(count + length // rows,),
        in_specs=[
            pl.BlockSpec((group, tokens, d), lambda i: (early(i), 0, 0)),
            resident((d, width), small.shape[1] // width - 1),
            resident((d, n)),
            first,
            per_query,
            whole,
            whole,
            per_query,
            pl.BlockSpec((heads, 1, rows), lambda i: (0, 0, late(i))),
            whole,
            whole,
            ANY,
            ANY,
        ],
        out_specs=[first, resident((length, out_width)), ANY, ANY],
        out_shape=[
            jax.ShapeDtypeStruct((length, n), BF16),
            jax.ShapeDtypeStruct((length, out_width), BF16),
            jax.ShapeDtypeStruct((high, columns), BF16),
            jax.ShapeDtypeStruct((chips, high // 2, width), BF16),
        ],
        scratch_shapes=[
            pltpu.VMEM((heads, length, HEAD), BF16),
            pltpu.VMEM((rows, HEAD), F32),
            pltpu.VMEM((length, HEAD), F32),
            pltpu.VMEM((length, HEAD), F32),
        ]
        + [s for h in held for s in h],
        compiler_params=pltpu.CompilerParams(collective_id=number, has_side_effects=True, vmem_limit_bytes=60 << 20),
        cost_estimate=pl.CostEstimate(
            flops=2 * length * d * (n + width) + 5 * heads * length * length * HEAD,
            transcendentals=heads * length * length // 2,
            bytes_accessed=2 * length * d,
        ),
        name="backward",
    )(g, small, down, slope, q, k, v, o, lse, cosines, sines, down_part, dense_part)


def out_kernel(a_ref, b_ref, small_ref, wide_ref, out_ref):
    tokens, d = out_ref.shape[-2:]
    step = a_ref.shape[0] // tokens
    a, b = a_ref[...], b_ref[...]
    for at, width in chunks(d, 512):
        part = dot(a, small_ref[at : at + width], ROWS_COLS) + dot(b, wide_ref[at : at + width], ROWS_COLS)
        part = part.astype(BF16).reshape(step, tokens, width)
        if out_ref.ndim == 4:
            out_ref[:, 0, :, at : at + width] = part
        else:
            out_ref[:, :, at : at + width] = part


def out_product(a, b, small, column, wide, chips, name, by_plane=False):
    length, width = a.shape
    tokens, d = length // chips, small.shape[0]
    step = max(1, 512 // tokens)
    rows = step * tokens
    n = wide.shape[1]
    shape, spec = (chips, tokens, d), pl.BlockSpec((step, tokens, d), lambda i: (i, 0, 0))
    if by_plane:
        nz, ny, nx = grid_of(chips)
        per = ny * nx // step
        shape = (ny * nx, nz, tokens, d)
        spec = pl.BlockSpec((step, 1, tokens, d), lambda i: (lax.rem(i, per), i // per, 0, 0))
    return pl.pallas_call(
        out_kernel,
        grid=(chips // step,),
        in_specs=[per_row(rows, width), per_row(rows, n), resident((d, width), column), resident((d, n))],
        out_specs=spec,
        out_shape=jax.ShapeDtypeStruct(shape, BF16),
        compiler_params=pltpu.CompilerParams(vmem_limit_bytes=56 << 20),
        cost_estimate=pl.CostEstimate(
            flops=2 * length * d * (n + width), transcendentals=0, bytes_accessed=2 * length * d
        ),
        name=name,
    )(a, b, small, wide)


def weight_kernel(x_ref, a_ref, b_ref, small_ref, wide_ref):
    chips, tokens, width = x_ref.shape
    x = x_ref[...].reshape(chips * tokens, width)
    small_ref[...] = dot(x, a_ref[...], ROWS_ROWS).astype(BF16)
    for at, n in chunks(wide_ref.shape[1], 384):
        wide_ref[:, at : at + n] = dot(x, b_ref[:, at : at + n], ROWS_ROWS).astype(BF16)


def weight_product(x, a, b, name):
    chips, tokens, d = x.shape
    length = chips * tokens
    width = 768 if d % 768 == 0 else 512
    return pl.pallas_call(
        weight_kernel,
        grid=(d // width,),
        in_specs=[pl.BlockSpec((chips, tokens, width), lambda i: (0, 0, i)), resident(a.shape), resident(b.shape)],
        out_specs=[per_row(width, a.shape[1]), per_row(width, b.shape[1])],
        out_shape=[jax.ShapeDtypeStruct((d, a.shape[1]), BF16), jax.ShapeDtypeStruct((d, b.shape[1]), BF16)],
        compiler_params=pltpu.CompilerParams(vmem_limit_bytes=56 << 20),
        cost_estimate=pl.CostEstimate(
            flops=2 * length * d * (a.shape[1] + b.shape[1]), transcendentals=0, bytes_accessed=2 * length * d
        ),
        name=name,
    )(x, a, b)


def share_heads(columns, chips):
    rows, width = columns.shape
    heads = width // HEAD
    most = -(-heads // chips)
    richer = heads - chips * (most - 1)
    cut = richer * most * HEAD
    first = jnp.moveaxis(columns[:, :cut].reshape(rows, richer, most * HEAD), 1, 0)
    if richer == chips:
        return first
    rest = jnp.moveaxis(columns[:, cut:].reshape(rows, chips - richer, (most - 1) * HEAD), 1, 0)
    return jnp.concatenate([first, jnp.pad(rest, ((0, 0), (0, 0), (0, HEAD)))], 0)


def join_heads(parts, heads):
    chips, rows, width = parts.shape
    most = width // HEAD
    richer = heads - chips * (most - 1)
    first = jnp.moveaxis(parts[:richer], 0, 1).reshape(rows, -1)
    if richer == chips:
        return first
    rest = jnp.moveaxis(parts[richer:, :, : width - HEAD], 0, 1).reshape(rows, -1)
    return jnp.concatenate([first, rest], 1)


def swap(values):
    return lax.ppermute(values, "fsdp", [(0, 1), (1, 0)])


def in_order(mine, other, core, axis):
    return jnp.where(
        core == 0,
        jnp.concatenate([mine, other], axis),
        jnp.concatenate([other, mine], axis),
    )


def half_of(values, core, axis):
    first, second = jnp.split(values, 2, axis)
    return jnp.where(core == 0, first, second), jnp.where(core == 0, second, first)


def angles(length):
    inverse_freq = ROPE_BASE ** (-jnp.arange(0, HEAD, 2).astype(F32) / HEAD)
    phases = jnp.arange(length, dtype=jnp.int32).astype(F32)[:, None] * inverse_freq[None, :]
    phases = jnp.concatenate([phases, phases], -1)
    return jnp.cos(phases), jnp.sin(phases)


def body(layer_input, cotangent, norm_gain, norm_bias, qkv_weight, up_weight, dense_weight, down_weight):
    chips = lax.axis_size("ctx")
    core = lax.axis_index("fsdp")
    inputs = layer_input[0].astype(F32)
    tokens, features = inputs.shape
    length = tokens * chips
    heads = features // HEAD
    most = -(-heads // chips)
    qwide = most * HEAD
    rows = qkv_weight.shape[0]
    high = padded_rows(rows)
    wide_columns = up_weight.shape[1]
    lead = (qwide + 2 * HEAD) % LANES

    def pad(values):
        apart = values.reshape(*values.shape[:-1], chips, rows)
        apart = jnp.pad(apart, [(0, 0)] * (apart.ndim - 1) + [(0, high - rows)])
        return apart.reshape(*values.shape[:-1], chips * high)

    def unpad(values):
        apart = values.reshape(*values.shape[:-1], chips, high)[..., :rows]
        return apart.reshape(*values.shape[:-1], features)

    def pad_rows(weight):
        return jnp.pad(weight, ((0, high - rows), (0, 0)))

    center = inputs - jnp.mean(inputs, -1, keepdims=True)
    inverse = lax.rsqrt(jnp.mean(center * center, -1, keepdims=True) + EPS)
    xhat = center * inverse
    normed_low = pad((xhat * norm_gain + norm_bias).astype(BF16))
    grad_low = pad(cotangent[0])

    mine, other = half_of(pad_rows(jnp.concatenate([qkv_weight, dense_weight], 1)), core, 0)
    other = swap(other)
    qkv_columns = qkv_weight.shape[1]
    qkv_rows = in_order(mine[:, :qkv_columns], other[:, :qkv_columns], core, 1)
    dense_rows = in_order(mine[:, qkv_columns:], other[:, qkv_columns:], core, 1)
    blocks = jnp.concatenate(
        [
            share_heads(qkv_rows[:, :features], chips),
            jnp.broadcast_to(qkv_rows[:, features:], (chips, high // 2, 2 * HEAD)),
            share_heads(dense_rows, chips),
        ],
        2,
    )
    normed_all, up_cols, small = bring(
        chips, 0, "bring", (Gather, normed_low), (Columns, pad_rows(up_weight)), (Blocks, blocks)
    )

    cosines, sines = angles(length)
    dense_block = small.shape[1] // (lead + qwide) - 1
    (queries, keys, values, hidden_low, slope, attended_low, attention, log_sum), (grad_all, down_cols) = forward(
        normed_all,
        small,
        up_cols,
        cosines,
        sines,
        most,
        lead,
        2,
        [(Gather, grad_low), (Columns, pad_rows(down_weight))],
    )
    branch = out_product(attended_low, hidden_low, small, dense_block, down_cols, chips, "forward_out", True)
    branch, grad_all = lax.optimization_barrier((branch, grad_all))
    nz, ny, nx = grid_of(chips)
    planes = [[z * ny * nx + i for i in range(ny * nx)] for z in range(nz)]
    lines = [[z * ny * nx + i for z in range(nz)] for i in range(ny * nx)]
    branch = branch.reshape(ny * nx, nz * tokens, -1)
    branch = lax.psum_scatter(branch, "ctx", scatter_dimension=0, axis_index_groups=planes, tiled=False)

    dense_part, down_part = weight_product(grad_all, attended_low, hidden_low, "late_weights")
    grad_up, grad_joined, down_grad, dense_total = backward(
        grad_all,
        small,
        lead,
        down_cols,
        slope,
        queries,
        keys,
        values,
        attention,
        log_sum,
        cosines,
        sines,
        3,
        down_part,
        dense_part,
        wide_columns,
    )
    branch, grad_joined = lax.optimization_barrier((branch, grad_joined))
    branch = branch.reshape(nz, tokens, -1)
    branch = lax.psum_scatter(branch, "ctx", scatter_dimension=0, axis_index_groups=lines, tiled=False)
    layer_output = (inputs + unpad(branch).astype(F32)).astype(BF16)
    grad_normed = out_product(grad_joined, grad_up, small, 0, up_cols, chips, "back_out")

    input_grad, stats, up_grad, total = send(
        chips,
        1,
        features,
        grad_normed,
        normed_all,
        grad_joined,
        grad_up,
        wide_columns,
        pad(xhat),
        grad_low,
        pad(norm_gain[None]),
        inverse,
    )
    up_grad = up_grad[:rows].astype(F32)
    down_grad = down_grad[:rows].astype(F32)
    qkv_rows = jnp.concatenate(
        [
            join_heads(total[:, :, :qwide], heads),
            jnp.sum(total[:, :, qwide : qwide + 2 * HEAD].astype(F32), 0).astype(BF16),
        ],
        1,
    )
    dense_rows = join_heads(dense_total[:, :, lead:], heads)

    def own_columns(values):
        mine, other = half_of(values, core, 1)
        return in_order(mine, swap(other), core, 0)[:rows].astype(F32)

    stats = unpad(stats)
    return (
        layer_output[None],
        unpad(input_grad)[None],
        stats[0],
        stats[1],
        own_columns(qkv_rows),
        up_grad,
        own_columns(dense_rows),
        down_grad,
    )


def solution(mesh):
    split = P("ctx", "fsdp")
    stream = P("fsdp", "ctx", None)
    return jax.shard_map(
        body,
        mesh=mesh,
        in_specs=(stream, stream, P(), P(), split, split, split, split),
        out_specs=(stream, stream, P(), P(), split, split, split, split),
        check_vma=False,
    )
```

```python
import functools

import jax
import jax.numpy as jnp
from jax import lax
from jax.experimental import pallas as pl
from jax.experimental.pallas import tpu as pltpu
from jax.sharding import PartitionSpec as P

HEADS = 71
HEAD = 64
EPS = 1e-05
ROPE_BASE = 10000.0
MASKED = -1e30
LANES = 128
F32 = jnp.float32
BF16 = jnp.bfloat16
ROWS_COLS = (((1,), (1,)), ((), ()))
ROWS_ROWS = (((0,), (0,)), ((), ()))
MESH = pl.DeviceIdType.MESH
ANY = pl.BlockSpec(memory_space=pl.ANY)
WHOLE = pl.BlockSpec(memory_space=pltpu.VMEM)
DMA = pltpu.SemaphoreType.DMA


def dot(a, b, dims=None):
    if dims is None:
        return jnp.dot(a, b, preferred_element_type=F32)
    return lax.dot_general(a, b, dims, preferred_element_type=F32)


def grid_of(chips):
    return (4, 4, 4) if chips == 64 else (chips // 4, 2, 2)


def padded_rows(rows):
    return -(-rows // 16) * 16


def tile_share(tiles, chips):
    return tiles // chips, tiles % chips


class Place:
    def __init__(self, chips):
        self.chips = chips
        self.nz, self.ny, self.nx = grid_of(chips)
        self.me = lax.axis_index("ctx")
        self.core = lax.axis_index("fsdp")
        self.z = self.me // (self.ny * self.nx)
        self.y = lax.rem(self.me // self.nx, self.ny)
        self.x = lax.rem(self.me, self.nx)

    def at(self, dz, dy, dx):
        z = lax.rem(self.z + dz + self.nz, self.nz)
        y = lax.rem(self.y + dy + self.ny, self.ny)
        x = lax.rem(self.x + dx + self.nx, self.nx)
        return (z * self.ny + y) * self.nx + x

    def pair(self, i):
        return self.me ^ i


def enter(place):
    barrier = pltpu.get_barrier_semaphore()

    def greet(i):
        pl.semaphore_signal(barrier, 1, device_id=(place.pair(i), place.core), device_id_type=MESH)

    each(1, place.chips, greet)
    pl.semaphore_signal(barrier, 1, device_id=(place.me, 1 - place.core), device_id_type=MESH)
    pl.semaphore_wait(barrier, place.chips)


def remote(src, dst, send, recv, chip, core):
    return pltpu.make_async_remote_copy(
        src_ref=src, dst_ref=dst, send_sem=send, recv_sem=recv, device_id=(chip, core), device_id_type=MESH
    )


def each(first, last, do):
    def step(i, carry):
        do(i)
        return carry

    lax.fori_loop(first, last, step, 0)


def when(condition, do):
    if condition is None:
        do()
    else:
        pl.when(condition)(do)


def rows_at(start, count):
    return pl.ds(pl.multiple_of(start, 8), count)


def lanes_at(tile, count):
    return pl.ds(pl.multiple_of(tile * LANES, LANES), count * LANES)


def move(src, dst, sem):
    copy = pltpu.make_async_copy(src, dst, sem)
    copy.start()
    copy.wait()


class Tiles:
    def __init__(self, columns, chips):
        self.chips = chips
        self.least, self.richer = tile_share(columns // LANES, chips)
        assert 0 < self.least and 2 * self.richer <= chips

    def more(self, chip, core):
        return jnp.where(core == 0, chip < self.richer, chip >= self.chips - self.richer)

    def first(self, chip, core):
        late = jnp.maximum(chip - (self.chips - self.richer), 0)
        return self.least * chip + jnp.where(core == 0, jnp.minimum(chip, self.richer), late)

    def cut(self, ref, chip, core):
        start = self.first(chip, core)
        return (
            ref.at[:, lanes_at(start, self.least)],
            ref.at[:, lanes_at(jnp.minimum(start + self.least, self.first(self.chips, core) - 1), 1)],
        )


class Gather:
    @staticmethod
    def shape(chips, a):
        return (chips, *a.shape)

    @staticmethod
    def scratch(chips, a):
        nz, ny, nx = grid_of(chips)
        return [DMA((nz,))] * 2 + [DMA((nz, nx))] * 2 + [DMA((nz, ny))] * 2 + [DMA((nz, nx, ny))] * 4 + [DMA, DMA((nz,))]

    def __init__(self, place, mine, out, sems):
        self.p, self.mine, self.out = place, mine, out
        (self.sl, self.rl, self.sx, self.rx, self.sy, self.ry, self.s1, self.r1, self.s2, self.r2, self.own, self.sr) = sems
        self.half = mine.shape[0] // 2

    def line(self, k):
        p = self.p
        return remote(self.mine, self.out.at[p.me], self.sl.at[k], self.rl.at[k], p.at(k, 0, 0), p.core)

    def direct(self, k):
        p = self.p
        to = lax.rem(p.z + k, p.nz)
        middle = p.nz // 2
        far = ((to == p.nz - 1) & (p.z < middle)) | ((to == 0) & (p.z >= middle))
        return jnp.logical_not(far)

    def relay(self, k):
        p = self.p
        source = lax.rem(p.z - k + p.nz, p.nz)
        middle = p.nz // 2
        up = (p.z == p.nz - 2) & (source < middle)
        down = (p.z == 1) & (source >= middle)
        b = p.at(-k, 0, 0)
        index = jnp.where(up, k + 1, k - 1)
        copy = remote(self.out.at[b], self.out.at[b], self.sr.at[k], self.rl.at[index], p.at(jnp.where(up, 1, -1), 0, 0), p.core)
        return copy, up | down

    def across(self, k, i):
        p = self.p
        b = p.at(-k, 0, 0)
        src = self.mine if isinstance(k, int) and k == 0 else self.out.at[b]
        return remote(src, self.out.at[b], self.sx.at[k, i], self.rx.at[k, i], p.at(0, 0, i), p.core)

    def along(self, k, j):
        p = self.p
        b = p.at(-k, 0, 0)
        src = self.mine if isinstance(k, int) and k == 0 else self.out.at[b]
        return remote(src, self.out.at[b], self.sy.at[k, j], self.ry.at[k, j], p.at(0, j, 0), p.core)

    def corner1(self, k, i, j):
        p = self.p
        part = self.out.at[p.at(-k, 0, -i), pl.ds(0, self.half)]
        return remote(part, part, self.s1.at[k, i, j], self.r1.at[k, i, j], p.at(0, j, 0), p.core)

    def corner2(self, k, i, j):
        p = self.p
        part = self.out.at[p.at(-k, -j, 0), pl.ds(self.half, self.half)]
        return remote(part, part, self.s2.at[k, i, j], self.r2.at[k, i, j], p.at(0, 0, i), p.core)

    def spread(self, k):
        for i in range(1, self.p.nx):
            self.across(k, i).start()
        for j in range(1, self.p.ny):
            self.along(k, j).start()

    def begin(self):
        for k in range(1, self.p.nz):
            pl.when(self.direct(k))(self.line(k).start)
        self.spread(0)
        pltpu.make_async_copy(self.mine, self.out.at[self.p.me], self.own).start()

    def turn(self, k):
        p = self.p
        for i in range(1, p.nx):
            self.across(k, i).wait_recv()
            for j in range(1, p.ny):
                self.corner1(k, i, j).start()
        for j in range(1, p.ny):
            self.along(k, j).wait_recv()
            for i in range(1, p.nx):
                self.corner2(k, i, j).start()

    def steps(self):
        p = self.p
        assert p.nz == 4
        first = jnp.where(p.z == 0, 3, 1)
        last = jnp.where(p.z == 0, 1, jnp.where(p.z == 3, 3, 2))
        order = [first, 6 - first - last, last]

        def come(k):
            self.line(k).wait_recv()
            copy, needed = self.relay(k)
            pl.when(needed)(copy.start)
            self.spread(k)

        return (
            [functools.partial(self.turn, 0)]
            + [functools.partial(come, k) for k in order]
            + [functools.partial(self.turn, k) for k in order]
        )

    def end(self):
        p = self.p
        pltpu.make_async_copy(self.mine, self.out.at[p.me], self.own).wait()
        for k in range(p.nz):
            if k:
                pl.when(self.direct(k))(self.line(k).wait_send)
                copy, needed = self.relay(k)
                pl.when(needed)(copy.wait_send)
            for i in range(1, p.nx):
                self.across(k, i).wait_send()
            for j in range(1, p.ny):
                self.along(k, j).wait_send()
            for i in range(1, p.nx):
                for j in range(1, p.ny):
                    self.corner1(k, i, j).wait()
                    self.corner2(k, i, j).wait()


class Columns:
    @staticmethod
    def shape(chips, a):
        least, _ = tile_share(a.shape[1] // LANES, chips)
        return (chips * a.shape[0], (2 * least + 1) * LANES)

    @staticmethod
    def scratch(chips, a):
        return [DMA((chips,))] * 8 + [pltpu.VMEM((a.shape[0], LANES), a.dtype)]

    def __init__(self, place, weight, out, sems):
        self.p, self.w, self.out = place, weight, out
        self.ms, self.mr, self.es, self.er, self.fs, self.fr, self.gs, self.gr, self.nought = sems
        self.tiles = Tiles(weight.shape[1], place.chips)
        self.rows = weight.shape[0]

    def slots(self, chip, own):
        rows = rows_at(chip * self.rows, self.rows)
        least = self.tiles.least
        return self.out.at[rows, lanes_at(0 if own else least + 1, least)], self.out.at[rows, lanes_at(least, 1)]

    def sends(self, i):
        p = self.p
        chip = p.pair(i)
        (a, b), (c, d) = self.tiles.cut(self.w, chip, p.core), self.slots(p.me, True)
        return (
            remote(a, c, self.ms.at[i], self.mr.at[i], chip, p.core),
            remote(b, d, self.es.at[i], self.er.at[i], chip, p.core),
            self.tiles.more(chip, p.core),
        )

    def gets(self, i):
        p = self.p
        chip = p.pair(i)
        (a, b), (c, d) = self.tiles.cut(self.w, chip, p.core), self.slots(chip, True)
        return (
            remote(a, c, self.ms.at[i], self.mr.at[i], chip, p.core),
            remote(b, d, self.es.at[i], self.er.at[i], chip, p.core),
        )

    def passes(self, i):
        p = self.p
        chip = p.pair(i)
        a, b = self.slots(chip, True)
        if isinstance(i, int) and i == 0:
            a, b = self.tiles.cut(self.w, p.me, p.core)
        c, d = self.slots(chip, False)
        return (
            remote(a, c, self.fs.at[i], self.fr.at[i], p.me, 1 - p.core),
            remote(b, d, self.gs.at[i], self.gr.at[i], p.me, 1 - p.core),
        )

    def here(self):
        p = self.p
        (a, b), (c, d) = self.tiles.cut(self.w, p.me, p.core), self.slots(p.me, True)
        return pltpu.make_async_copy(a, c, self.ms.at[0]), pltpu.make_async_copy(b, d, self.es.at[0])

    def begin(self):
        p = self.p

        def send(i):
            main, extra, more = self.sends(i)
            main.start()
            pl.when(more)(extra.start)

        each(1, p.chips, send)
        own, pass_on = self.here(), self.passes(0)
        own[0].start()
        pass_on[0].start()

        @pl.when(self.tiles.more(p.me, p.core))
        def _():
            own[1].start()
            pass_on[1].start()

    def steps(self):
        return [self.hand_on]

    def hand_on(self):
        p = self.p
        mine = self.tiles.more(p.me, p.core)

        def hand(i):
            main, extra = self.gets(i)
            to_main, to_extra = self.passes(i)
            main.wait_recv()
            to_main.start()

            @pl.when(mine)
            def _():
                extra.wait_recv()
                to_extra.start()

        each(1, p.chips, hand)

    def end(self):
        p = self.p
        mine = self.tiles.more(p.me, p.core)
        theirs = self.tiles.more(p.me, 1 - p.core)
        own = self.here()
        own[0].wait()
        pl.when(mine)(own[1].wait)

        @pl.when(jnp.logical_not(mine | theirs))
        def _():
            self.nought[...] = jnp.zeros_like(self.nought)
            each(0, p.chips, lambda c: move(self.nought, self.slots(c, True)[1], self.es.at[0]))

        def sent(i):
            main, extra, more = self.sends(i)
            main.wait_send()
            pl.when(more)(extra.wait_send)

        each(1, p.chips, sent)

        def handed(i):
            main, extra = self.passes(i)
            main.wait()
            pl.when(mine)(extra.wait_send)
            pl.when(theirs)(extra.wait_recv)

        handed(0)
        each(1, p.chips, handed)


class Blocks:
    @staticmethod
    def shape(chips, a):
        return (chips * 2 * a.shape[1], a.shape[2])

    @staticmethod
    def scratch(chips, a):
        return [DMA((chips,))] * 4

    def __init__(self, place, blocks, out, sems):
        self.p, self.b, self.out = place, blocks, out
        self.s, self.r, self.fs, self.fr = sems
        self.rows = blocks.shape[1]

    def slot(self, chip, core):
        return self.out.at[rows_at((2 * chip + core) * self.rows, self.rows)]

    def sends(self, i):
        p = self.p
        chip = p.pair(i)
        return remote(self.b.at[chip], self.slot(p.me, p.core), self.s.at[i], self.r.at[i], chip, p.core)

    def passes(self, i):
        p = self.p
        part = self.slot(p.pair(i), p.core)
        mine = self.b.at[p.me] if isinstance(i, int) and i == 0 else part
        return remote(mine, part, self.fs.at[i], self.fr.at[i], p.me, 1 - p.core)

    def here(self):
        p = self.p
        return pltpu.make_async_copy(self.b.at[p.me], self.slot(p.me, p.core), self.s.at[0])

    def begin(self):
        each(1, self.p.chips, lambda i: self.sends(i).start())
        self.here().start()
        self.passes(0).start()

    def steps(self):
        return [self.hand_on]

    def hand_on(self):
        def hand(i):
            self.sends(i).wait_recv()
            self.passes(i).start()

        each(1, self.p.chips, hand)

    def end(self):
        p = self.p
        self.here().wait()
        each(1, p.chips, lambda i: self.sends(i).wait_send())
        self.passes(0).wait()
        each(1, p.chips, lambda i: self.passes(i).wait())


def drive(parts):
    for part in parts:
        part.begin()
    todo = [part.steps() for part in parts]
    total = max(len(steps) for steps in todo)
    for at in range(total):
        for steps in todo:
            index = at - (total - len(steps))
            if index >= 0:
                steps[index]()
    for part in parts:
        part.end()


def take(refs, counts):
    out, at = [], 0
    for count in counts:
        out.append(refs[at : at + count])
        at += count
    return out


def bring_kernel(chips, plan, *refs):
    n = len(plan)
    ins, outs, held = refs[:n], refs[n : 2 * n], refs[2 * n :]
    place = Place(chips)
    enter(place)
    held = take(held, [count for _, count in plan])
    drive([kind(place, a, o, h) for (kind, _), a, o, h in zip(plan, ins, outs, held)])


def bring(chips, number, name, *jobs):
    held = [kind.scratch(chips, a) for kind, a in jobs]
    return pl.pallas_call(
        functools.partial(bring_kernel, chips, [(kind, len(h)) for (kind, _), h in zip(jobs, held)]),
        in_specs=[ANY] * len(jobs),
        out_specs=[ANY] * len(jobs),
        out_shape=[jax.ShapeDtypeStruct(kind.shape(chips, a), a.dtype) for kind, a in jobs],
        scratch_shapes=[s for h in held for s in h],
        compiler_params=pltpu.CompilerParams(collective_id=number, has_side_effects=True, vmem_limit_bytes=16 << 20),
        name=name,
    )(*[a for _, a in jobs])


class Paired:
    @staticmethod
    def scratch(chips, shape, dtype):
        return [DMA((chips,))] * 5 + [pltpu.VMEM((chips, *shape), dtype)] * 2

    def __init__(self, place, held, views, gives=None, sums=None, comes=lambda j: None):
        self.p = place
        self.cs, self.cr, self.s, self.r, self.load, self.total, self.stage = held
        self.mine, self.theirs, self.target, self.source = views
        self.gives, self.sums, self.comes = gives, sums, comes

    def across(self, i):
        p = self.p
        return remote(self.theirs(p.pair(i)), self.stage.at[i], self.cs.at[i], self.cr.at[i], p.me, 1 - p.core)

    def fetch(self, i):
        return pltpu.make_async_copy(self.mine(self.p.pair(i)), self.total.at[i], self.load.at[i])

    def sends(self, i):
        p = self.p
        j = p.pair(i)
        return remote(self.total.at[i], self.target(j), self.s.at[i], self.r.at[i], j, p.core)

    def gets(self, i):
        p = self.p
        j = p.pair(i)
        return remote(self.total.at[i], self.source(j), self.s.at[i], self.r.at[i], j, p.core)

    def here(self):
        return pltpu.make_async_copy(self.total.at[0], self.source(self.p.me), self.s.at[0])

    def begin(self):
        chips = self.p.chips
        when(self.gives, lambda: each(0, chips, lambda i: self.across(i).start()))
        when(self.sums, lambda: each(0, chips, lambda i: self.fetch(i).start()))

    def add(self, i):
        self.fetch(i).wait()
        self.across(i).wait_recv()
        self.total[i] = (self.total[i].astype(F32) + self.stage[i].astype(F32)).astype(self.total.dtype)

    def some(self, first, last):
        def do(i):
            self.add(i)
            self.sends(i).start()

        when(self.sums, lambda: each(first, last, do))

    def own(self):
        def do():
            self.add(0)
            self.here().start()

        when(self.sums, do)

    def end(self):
        chips = self.p.chips
        when(self.gives, lambda: each(0, chips, lambda i: self.across(i).wait_send()))

        def sent():
            self.here().wait()
            each(1, chips, lambda i: self.sends(i).wait_send())

        when(self.sums, sent)

        def came(i):
            when(self.comes(self.p.pair(i)), lambda: self.gets(i).wait_recv())

        each(1, chips, came)

    def steps(self):
        chips = self.p.chips
        return [functools.partial(self.some, 1, chips), self.own]


class Scatter:
    @staticmethod
    def stages(chips, a):
        nz, _, n = grid_of(chips)
        _, t, d = a.shape
        h = t // 2
        return [(2, nz, n, n, h, d), (2, nz, n, h, d), (2, nz, n, h, d), (nz, t, d), (nz, t, d)]

    @staticmethod
    def scratch(chips, a):
        nz, _, n = grid_of(chips)
        _, t, d = a.shape
        h = t // 2
        most = max(n, nz)
        sems = [DMA((2, nz, n, n))] * 2 + [DMA((2, nz, n))] * 2 + [DMA((nz,))] * 2 + [DMA((most,)), DMA]
        return sems + [pltpu.VMEM((most, h, d), a.dtype), pltpu.VMEM((h, d), a.dtype)]

    def __init__(self, place, blocks, stages, held):
        self.p, self.b = place, blocks
        self.got1, self.sum1, self.got2, self.sum2, self.got3 = stages
        (self.s1, self.r1, self.s2, self.r2, self.s3, self.r3, self.load, self.store, self.parts, self.low) = held
        self.h = blocks.shape[1] // 2
        self.n = place.nx

    def chip(self, half, dz, du, dv):
        return self.p.at(dz, dv, du) if half == 0 else self.p.at(dz, du, dv)

    def rows(self, half):
        return pl.ds(half * self.h, self.h)

    def send1(self, half, dz, v, i):
        return remote(
            self.b.at[self.chip(half, dz, i, v), self.rows(half)],
            self.got1.at[half, dz, v, i],
            self.s1.at[half, dz, v, i],
            self.r1.at[half, dz, v, i],
            self.chip(half, 0, i, 0),
            self.p.core,
        )

    def send2(self, half, dz, v):
        return remote(
            self.sum1.at[half, dz, v],
            self.got2.at[half, dz, v],
            self.s2.at[half, dz, v],
            self.r2.at[half, dz, v],
            self.chip(half, 0, 0, v),
            self.p.core,
        )

    def beside(self):
        return jnp.where(lax.rem(self.p.z, 2) == 0, 1, self.p.nz - 1)

    def beyond(self, side):
        other = jnp.where(self.p.z < 2, 2, 0) + side
        return lax.rem(other - self.p.z + self.p.nz, self.p.nz)

    def inner(self):
        return (self.p.z == 1) | (self.p.z == 2)

    def near(self):
        p, dz = self.p, self.beside()
        return remote(self.sum2.at[dz], self.got3.at[0], self.s3.at[0], self.r3.at[0], p.at(dz, 0, 0), p.core)

    def lift(self, side):
        p, dz = self.p, self.beyond(side)
        to = p.at(self.beside(), 0, 0)
        return remote(self.sum2.at[dz], self.got3.at[2 + side], self.s3.at[1 + side], self.r3.at[2 + side], to, p.core)

    def far(self, side):
        p, dz = self.p, self.beyond(side)
        return remote(self.sum2.at[dz], self.got3.at[1], self.s3.at[1 + side], self.r3.at[1], p.at(dz, 0, 0), p.core)

    def fetch(self, refs):
        loads = [pltpu.make_async_copy(r, self.parts.at[i], self.load.at[i]) for i, r in enumerate(refs)]
        for copy in loads:
            copy.start()
        for copy in loads:
            copy.wait()

    def add(self, refs, to):
        self.fetch(refs)
        total = self.parts[0].astype(F32)
        for i in range(1, len(refs)):
            total = total + self.parts[i].astype(F32)
        self.low[...] = total.astype(self.low.dtype)
        move(self.low, to, self.store)

    def order(self):
        nz = self.p.nz
        return [nz // 2] + [k for k in range(1, nz) if k != nz // 2] + [0]

    def begin(self):
        for dz in self.order():
            for half in (0, 1):
                for v in list(range(1, self.n)) + [0]:
                    for i in range(1, self.n):
                        self.send1(half, dz, v, i).start()

    def first(self, dz):
        for half in (0, 1):
            for v in list(range(1, self.n)) + [0]:
                for i in range(1, self.n):
                    self.send1(half, dz, v, i).wait_recv()
                mine = self.b.at[self.chip(half, dz, 0, v), self.rows(half)]
                self.add([mine] + [self.got1.at[half, dz, v, i] for i in range(1, self.n)], self.sum1.at[half, dz, v])
                if v:
                    self.send2(half, dz, v).start()

    def second(self, dz):
        for half in (0, 1):
            for v in range(1, self.n):
                self.send2(half, dz, v).wait_recv()
            parts = [self.sum1.at[half, dz, 0]] + [self.got2.at[half, dz, v] for v in range(1, self.n)]
            self.add(parts, self.sum2.at[dz, self.rows(half)])
        if dz:
            pl.when(self.beside() == dz)(self.near().start)
            for side in (0, 1):
                pl.when((self.beyond(side) == dz) & jnp.logical_not(self.inner()))(self.lift(side).start)

    def relay(self):
        @pl.when(self.inner())
        def _():
            for side in (0, 1):
                self.lift(side).wait_recv()
                for half in (0, 1):
                    mine = self.sum2.at[self.beyond(side), self.rows(half)]
                    self.add([mine, self.got3.at[2 + side, self.rows(half)]], mine)
                self.far(side).start()

    def last(self):
        self.near().wait_recv()
        self.far(0).wait_recv()
        for half in (0, 1):
            rows = self.rows(half)
            self.fetch([self.sum2.at[0, rows], self.got3.at[0, rows], self.got3.at[1, rows]])
            self.finish(half)

    def steps(self):
        assert self.p.nz == 4
        order = self.order()
        steps = [functools.partial(self.first, order[0])]
        for old, new in zip(order[:-1], order[1:]):
            steps += [functools.partial(self.first, new), functools.partial(self.second, old)]
        return steps + [self.relay, functools.partial(self.second, order[-1]), self.last]

    def end(self):
        for dz in range(self.p.nz):
            for half in (0, 1):
                for v in range(self.n):
                    for i in range(1, self.n):
                        self.send1(half, dz, v, i).wait_send()
                    if v:
                        self.send2(half, dz, v).wait_send()
        self.near().wait_send()
        inner = self.inner()
        for side in (0, 1):
            pl.when(inner)(self.far(side).wait_send)
            pl.when(jnp.logical_not(inner))(self.lift(side).wait_send)


class NormBack(Scatter):
    @staticmethod
    def scratch(chips, a):
        d = a.shape[2]
        more = [pltpu.VMEM((2, 8, d), F32), pltpu.VMEM((2, d), F32), pltpu.VMEM((2, d), F32), pltpu.VMEM((chips, 2, d), F32)]
        return Scatter.scratch(chips, a) + more + [DMA((chips,))] * 2 + [DMA((3,))]

    def __init__(self, place, blocks, stages, held, operands, results, features):
        super().__init__(place, blocks, stages, held[:10])
        self.sums, self.mine, self.other, self.slots, self.ss, self.sr, self.pairs = held[10:]
        self.xhat, self.grad, self.gain, self.inverse = operands
        self.input_grad, self.stats = results
        self.features = features

    def begin(self):
        super().begin()
        self.sums[...] = jnp.zeros_like(self.sums)

    def finish(self, half):
        d = self.xhat.shape[1]

        def some(c):
            at = pl.multiple_of(c * 16, 16)
            total = self.parts[0, pl.ds(at, 16)].astype(F32)
            for i in (1, 2):
                total = total + self.parts[i, pl.ds(at, 16)].astype(F32)
            rows = pl.ds(pl.multiple_of(half * self.h + c * 16, 16), 16)
            xhat = self.xhat[rows]
            both = total * xhat
            self.sums[0] += both[:8] + both[8:]
            self.sums[1] += total[:8] + total[8:]
            scaled = total * self.gain[...]
            mean = jnp.sum(scaled, 1, keepdims=True) / self.features
            slope = jnp.sum(scaled * xhat, 1, keepdims=True) / self.features
            change = (scaled - mean - xhat * slope) * self.inverse[rows]
            self.input_grad[rows] = self.grad[rows].astype(F32) + change

        each(0, self.h // 16, some)

    def swap_stats(self):
        p = self.p
        return remote(self.mine, self.other, self.pairs.at[0], self.pairs.at[1], p.me, 1 - p.core)

    def share_stats(self, i):
        p = self.p
        return remote(self.mine, self.slots.at[p.me], self.ss.at[i], self.sr.at[i], p.pair(i), p.core)

    def get_stats(self, i):
        p = self.p
        return remote(self.mine, self.slots.at[p.pair(i)], self.ss.at[i], self.sr.at[i], p.pair(i), p.core)

    def stats_out(self):
        self.mine[0:1] = jnp.sum(self.sums[0], 0, keepdims=True)
        self.mine[1:2] = jnp.sum(self.sums[1], 0, keepdims=True)
        self.swap_stats().start()
        self.swap_stats().wait()
        self.mine[...] += self.other[...]
        self.slots[self.p.me] = self.mine[...]
        each(1, self.p.chips, lambda i: self.share_stats(i).start())

    def steps(self):
        return super().steps() + [self.stats_out]

    def end(self):
        super().end()

        def done(i):
            self.share_stats(i).wait_send()
            self.get_stats(i).wait_recv()

        each(1, self.p.chips, done)
        self.stats[...] = self.slots[0]

        def more(c):
            self.stats[...] += self.slots[c]

        each(1, self.p.chips, more)


def return_parts(place, part, out, held):
    tiles = Tiles(out.shape[1], place.chips)
    least, rows, core, me = tiles.least, out.shape[0], place.core, place.me
    n = len(held) // 2

    def at(j, tile, count):
        return part.at[rows_at(j * rows, rows), lanes_at(tile, count)]

    main = Paired(
        place,
        held[:n],
        (
            lambda j: at(j, 0, least),
            lambda j: at(j, least + 1, least),
            lambda j: tiles.cut(out, me, core)[0],
            lambda j: tiles.cut(out, j, core)[0],
        ),
    )
    extra = Paired(
        place,
        held[n:],
        (
            lambda j: at(j, least, 1),
            lambda j: at(j, least, 1),
            lambda j: tiles.cut(out, me, core)[1],
            lambda j: tiles.cut(out, j, core)[1],
        ),
        tiles.more(me, 1 - core),
        tiles.more(me, core),
        lambda j: tiles.more(j, core),
    )
    return [main, extra]


def trade_parts(place, part, out, held):
    rows = out.shape[1]

    def at(j, core):
        return part.at[rows_at((2 * j + core) * rows, rows)]

    views = (
        lambda j: at(j, place.core),
        lambda j: at(j, 1 - place.core),
        lambda j: out.at[place.me],
        lambda j: out.at[j],
    )
    return [Paired(place, held, views)]


def send_kernel(chips, features, counts, *refs):
    x_ref, a_ref, b_ref, blocks, xhat, grad, gain, inverse = refs[:8]
    input_grad, stats, wide_out, small_out, wide, small = refs[8:14]
    stages = refs[14:19]
    wide_tile, small_tile, stored = refs[19:22]
    norm_held, wide_held, small_held = take(refs[22:], counts)
    step = pl.program_id(0)
    count = pl.num_programs(0) - 1
    width = x_ref.shape[2]
    place = Place(chips)
    norm = NormBack(place, blocks, stages, norm_held, (xhat, grad, gain, inverse), (input_grad, stats), features)
    parts = return_parts(place, wide, wide_out, wide_held)
    parts += trade_parts(place, small, small_out, small_held)

    def stores(at):
        slot = lax.rem(at, 2)
        rows = rows_at(at * width, width)
        return (
            pltpu.make_async_copy(wide_tile.at[slot], wide.at[rows], stored.at[0, slot]),
            pltpu.make_async_copy(small_tile.at[slot], small.at[rows], stored.at[1, slot]),
        )

    def done(at):
        for copy in stores(at):
            copy.wait()

    @pl.when(step == 0)
    def _():
        enter(place)
        norm.begin()

    @pl.when(step < count)
    def _():
        slot = lax.rem(step, 2)
        pl.when(step >= 2)(lambda: done(step - 2))
        x = flat(x_ref)
        small_tile[slot] = dot(x, a_ref[...], ROWS_ROWS).astype(BF16)
        for at, n in chunks(b_ref.shape[1], 384):
            wide_tile[slot, :, at : at + n] = dot(x, b_ref[:, at : at + n], ROWS_ROWS).astype(BF16)
        for copy in stores(step):
            copy.start()

    @pl.when(step == count)
    def _():
        done(step - 2)
        done(step - 1)
        for part in parts:
            part.begin()
        ahead, *rest = norm.steps()
        ahead()
        for part in parts:
            for do in part.steps():
                do()
        for do in rest:
            do()
        for part in [norm] + parts:
            part.end()


def send(chips, number, features, blocks, x, a, b, columns, xhat, grad, gain, inverse):
    _, tokens, d = blocks.shape
    length = chips * tokens
    rows = d // chips
    least, _ = tile_share(columns // LANES, chips)
    low, wide = a.shape[1], b.shape[1]
    width = 768 if d % 768 == 0 else 512
    count = d // width
    held = [
        NormBack.scratch(chips, blocks),
        Paired.scratch(chips, (rows, least * LANES), BF16) + Paired.scratch(chips, (rows, LANES), BF16),
        Paired.scratch(chips, (rows // 2, low), BF16),
    ]
    half = lambda *shape: jax.ShapeDtypeStruct(shape, BF16)
    results = pl.pallas_call(
        functools.partial(send_kernel, chips, features, [len(h) for h in held]),
        grid=(count + 1,),
        in_specs=[
            pl.BlockSpec((chips, tokens, width), lambda i: (0, 0, jnp.minimum(i, count - 1))),
            resident(a.shape),
            resident(b.shape),
            ANY,
            resident(xhat.shape),
            resident(grad.shape),
            resident(gain.shape),
            resident(inverse.shape),
        ],
        out_specs=[resident((tokens, d)), resident((2, d))] + [ANY] * 9,
        out_shape=[
            jax.ShapeDtypeStruct((tokens, d), F32),
            jax.ShapeDtypeStruct((2, d), F32),
            half(rows, columns),
            half(chips, rows // 2, low),
            half(d, wide),
            half(d, low),
        ]
        + [half(*s) for s in Scatter.stages(chips, blocks)],
        scratch_shapes=[pltpu.VMEM((2, width, wide), BF16), pltpu.VMEM((2, width, low), BF16), DMA((2, 2))]
        + [s for h in held for s in h],
        compiler_params=pltpu.CompilerParams(collective_id=number, has_side_effects=True, vmem_limit_bytes=60 << 20),
        cost_estimate=pl.CostEstimate(
            flops=2 * length * d * (low + wide), transcendentals=0, bytes_accessed=2 * length * d
        ),
        name="send",
    )(x, a, b, blocks, xhat, grad, gain, inverse)
    return results[:4]


def rotate(values, cosines, sines):
    middle = values.shape[-1] // 2
    turned = jnp.concatenate([-values[..., middle:], values[..., :middle]], -1)
    return values * cosines + turned * sines


def rotate_back(values, cosines, sines):
    middle = values.shape[-1] // 2
    turned = jnp.concatenate([values[..., middle:], -values[..., :middle]], -1)
    return values * cosines + turned * sines


def flat(ref):
    return ref[...].reshape(ref.shape[0] * ref.shape[1], ref.shape[2])


def chunks(width, most):
    return [(at, min(most, width - at)) for at in range(0, width, most)]


def resident(shape, column=0):
    return pl.BlockSpec(shape, lambda i: (0, column), pipeline_mode=pl.Buffered(1))


def per_row(rows, width):
    return pl.BlockSpec((rows, width), lambda i: (i, 0))


def forward_kernel(chips, plan, lead, events, *refs):
    n = len(plan)
    x_ref, small_ref, wide_ref, cos_ref, sin_ref = refs[:5]
    ins, refs = refs[5 : 5 + n], refs[5 + n :]
    q_out, k_out, v_out, hidden_ref, slope_ref, low_ref, o_ref, lse_ref = refs[:8]
    outs, refs = refs[8 : 8 + n], refs[8 + n :]
    q_all, k_all, v_all, acc, top = refs[:5]
    held = take(refs[5:], [count for _, count in plan])
    step = pl.program_id(0)
    half = pl.num_programs(0) // 2
    heads, rows, _ = q_out.shape
    place = Place(chips)
    parts = [kind(place, a, o, h) for (kind, _), a, o, h in zip(plan, ins, outs, held)]

    @pl.when(step == 0)
    def _():
        enter(place)
        for part in parts:
            part.begin()

    @pl.when(step < half)
    def _():
        here = pl.ds(pl.multiple_of(step * rows, rows), rows)
        x = flat(x_ref)
        cosines, sines = cos_ref[...], sin_ref[...]
        joined = dot(x, small_ref[...])
        for h in range(heads):
            q = rotate(joined[:, h * HEAD : (h + 1) * HEAD], cosines, sines).astype(BF16) * HEAD ** (-0.5)
            q_out[h] = q
            q_all[h, here] = q
        at = heads * HEAD
        k = rotate(joined[:, at : at + HEAD], cosines, sines).astype(BF16)
        v = joined[:, at + HEAD : at + 2 * HEAD].astype(BF16)
        k_out[...] = k
        v_out[...] = v
        k_all[here] = k
        v_all[here] = jnp.concatenate([v, jnp.ones_like(v)], 1)
        for at, width in chunks(wide_ref.shape[1], 384):
            up = dot(x, wide_ref[:, at : at + width])
            bell = 0.5 + 0.5 * lax.erf(up * 0.5**0.5)
            hidden_ref[:, at : at + width] = (up * bell).astype(BF16)
            slope = bell + up * jnp.exp(up * up * -0.5) * (2 * jnp.pi) ** (-0.5)
            slope_ref[:, at : at + width] = slope.astype(BF16)

    @pl.when(step >= half)
    def _():
        index = step - half
        here = pl.ds(pl.multiple_of(index * rows, rows), rows)
        lows = []
        for h in range(heads):
            q = q_all[h, here]
            acc[...] = jnp.zeros_like(acc)
            top[...] = jnp.full_like(top, MASKED)

            def block(start, masked):
                s = dot(q, k_all[pl.ds(start, rows), :], ROWS_COLS)
                if masked:
                    key = lax.broadcasted_iota(jnp.int32, s.shape, 1)
                    query = lax.broadcasted_iota(jnp.int32, s.shape, 0)
                    s = jnp.where(key <= query, s, MASKED)
                old = top[...]
                new = jnp.maximum(old, jnp.max(s, 1, keepdims=True))
                p = jnp.exp(s - new).astype(BF16)
                acc[...] = acc[...] * jnp.exp(old - new) + dot(p, v_all[pl.ds(start, rows), :])
                top[...] = new

            each(0, index, lambda i: block(pl.multiple_of(i * rows, rows), False))
            block(pl.multiple_of(index * rows, rows), True)
            total = acc[...]
            norm = total[:, HEAD : HEAD + 1]
            out = total[:, :HEAD] / norm
            o_ref[h] = out
            lows.append(out.astype(BF16))
            lse = jnp.broadcast_to(top[...] + jnp.log(norm), (rows, LANES))
            lse_ref[h] = lse.T[:1]
        if lead:
            lows = [jnp.zeros((rows, lead), BF16)] + lows
        low_ref[...] = jnp.concatenate(lows, 1)

    todo = []
    longest = max(len(part.steps()) for part in parts)
    for at in range(longest):
        for part in parts:
            steps = part.steps()
            index = at - (longest - len(steps))
            if index >= 0:
                todo.append(steps[index])
    cuts = [0, *[c for _, c in events], len(todo)]
    for (back, _), first, last in zip([*events, (0, None)], cuts[:-1], cuts[1:]):

        @pl.when(step == pl.num_programs(0) - 1 - back)
        def _():
            for do in todo[first:last]:
                do()

    @pl.when(step == pl.num_programs(0) - 1)
    def _():
        for part in parts:
            part.end()


def forward(x, small, wide, cosines, sines, heads, lead, number, jobs):
    chips, tokens, d = x.shape
    length = chips * tokens
    step = max(1, 512 // tokens)
    rows = step * tokens
    half = chips // step
    width = -(-(heads + 2) * HEAD // LANES) * LANES
    n = wide.shape[1]
    low = lead + heads * HEAD
    held = [kind.scratch(chips, a) for kind, a in jobs]
    plan = [(kind, len(h)) for (kind, _), h in zip(jobs, held)]
    early = lambda i: jnp.minimum(i, half - 1)
    late = lambda i: jnp.maximum(i - half, 0)
    first = lambda w: pl.BlockSpec((rows, w), lambda i: (early(i), 0))
    events = ((6, 2), (5, 3), (4, 4), (3, 5), (2, 6), (1, 7)) if half == 4 else ((4, 1), (2, 3), (1, 4))
    results = pl.pallas_call(
        functools.partial(forward_kernel, chips, plan, lead, events),
        grid=(2 * half,),
        in_specs=[
            pl.BlockSpec((step, tokens, d), lambda i: (early(i), 0, 0)),
            resident((d, width)),
            resident((d, n)),
            first(HEAD),
            first(HEAD),
        ]
        + [ANY] * len(jobs),
        out_specs=[
            pl.BlockSpec((heads, rows, HEAD), lambda i: (0, early(i), 0)),
            first(HEAD),
            first(HEAD),
            first(n),
            first(n),
            pl.BlockSpec((rows, low), lambda i: (late(i), 0)),
            pl.BlockSpec((heads, rows, HEAD), lambda i: (0, late(i), 0)),
            pl.BlockSpec((heads, 1, rows), lambda i: (0, 0, late(i))),
        ]
        + [ANY] * len(jobs),
        out_shape=[
            jax.ShapeDtypeStruct((heads, length, HEAD), BF16),
            jax.ShapeDtypeStruct((length, HEAD), BF16),
            jax.ShapeDtypeStruct((length, HEAD), BF16),
            jax.ShapeDtypeStruct((length, n), BF16),
            jax.ShapeDtypeStruct((length, n), BF16),
            jax.ShapeDtypeStruct((length, low), BF16),
            jax.ShapeDtypeStruct((heads, length, HEAD), F32),
            jax.ShapeDtypeStruct((heads, 1, length), F32),
        ]
        + [jax.ShapeDtypeStruct(kind.shape(chips, a), a.dtype) for kind, a in jobs],
        scratch_shapes=[
            pltpu.VMEM((heads, length, HEAD), BF16),
            pltpu.VMEM((length, HEAD), BF16),
            pltpu.VMEM((length, 2 * HEAD), BF16),
            pltpu.VMEM((rows, 2 * HEAD), F32),
            pltpu.VMEM((rows, 1), F32),
        ]
        + [s for h in held for s in h],
        compiler_params=pltpu.CompilerParams(collective_id=number, has_side_effects=True, vmem_limit_bytes=58 << 20),
        cost_estimate=pl.CostEstimate(
            flops=2 * length * d * (n + width) + 2 * heads * length * length * HEAD,
            transcendentals=2 * length * n + heads * length * length // 2,
            bytes_accessed=2 * length * d,
        ),
        name="forward",
    )(x, small, wide, cosines, sines, *[a for _, a in jobs])
    return results[:8], results[8:]


def backward_kernel(chips, lead, counts, *refs):
    g_ref, dense_ref, down_ref, slope_ref, q_ref, k_ref, v_ref, o_ref, lse_ref, cos_ref, sin_ref = refs[:11]
    wide, small = refs[11:13]
    grad_ref, out_ref, wide_out, small_out = refs[13:17]
    g_all, acc, dk, dv = refs[17:21]
    wide_held, small_held = take(refs[21:], counts)
    heads, rows, _ = q_ref.shape
    length = g_all.shape[1]
    count = pl.num_programs(0) - length // rows
    step = pl.program_id(0)
    scale = HEAD ** (-0.5)
    place = Place(chips)
    parts = return_parts(place, wide, wide_out, wide_held) + trade_parts(place, small, small_out, small_held)

    @pl.when(step == 0)
    def _():
        enter(place)
        for part in parts:
            part.begin()

    @pl.when(step < count)
    def _():
        g = flat(g_ref)
        low = g.shape[0]
        here = pl.ds(pl.multiple_of(step * low, low), low)
        grad = dot(g, dense_ref[...]).astype(BF16)
        for h in range(heads):
            g_all[h, here] = grad[:, lead + h * HEAD : lead + (h + 1) * HEAD]
        for at, width in chunks(down_ref.shape[1], 384):
            part = dot(g, down_ref[:, at : at + width])
            grad_ref[:, at : at + width] = (part * slope_ref[:, at : at + width].astype(F32)).astype(BF16)

    @pl.when(step == count)
    def _():
        dk[...] = jnp.zeros_like(dk)
        dv[...] = jnp.zeros_like(dv)
        out_ref[...] = jnp.zeros_like(out_ref)

    @pl.when(step >= count)
    def _():
        index = step - count
        here = pl.ds(pl.multiple_of(index * rows, rows), rows)
        cosines, sines = cos_ref[here], sin_ref[here]
        grads = []
        for h in range(heads):
            q = q_ref[h]
            g = g_all[h, here]
            lse = lse_ref[h]
            delta = jnp.sum((g.astype(F32) * o_ref[h]).T, 0, keepdims=True)
            acc[...] = jnp.zeros_like(acc)

            def block(start, masked):
                at = pl.ds(start, rows)
                k = k_ref[at, :]
                p = jnp.exp(dot(k, q, ROWS_COLS) - lse)
                if masked:
                    key = lax.broadcasted_iota(jnp.int32, p.shape, 0)
                    query = lax.broadcasted_iota(jnp.int32, p.shape, 1)
                    p = jnp.where(key <= query, p, 0.0)
                dp = dot(v_ref[at, :], g, ROWS_COLS)
                ds = (p * (dp - delta)).astype(BF16)
                dv[at, :] += dot(p.astype(BF16), g)
                dk[at, :] += dot(ds, q)
                acc[...] += dot(ds, k, ROWS_ROWS)

            each(0, index, lambda i: block(pl.multiple_of(i * rows, rows), False))
            block(pl.multiple_of(index * rows, rows), True)
            grads.append(rotate_back(acc[...] * scale, cosines, sines).astype(BF16))
        out_ref[here, : heads * HEAD] = jnp.concatenate(grads, 1)

    @pl.when(step == 1)
    def _():
        for part in parts:
            for do in part.steps():
                do()

    @pl.when(step == pl.num_programs(0) - 1)
    def _():
        keys = rotate_back(dk[...], cos_ref[...], sin_ref[...]).astype(BF16)
        both = jnp.concatenate([keys, dv[...].astype(BF16)], 1)
        out_ref[:, heads * HEAD : (heads + 2) * HEAD] = both
        for part in parts:
            part.end()


def backward(g, small, lead, down, slope, q, k, v, o, lse, cosines, sines, number, down_part, dense_part, columns):
    chips, tokens, d = g.shape
    heads, length, _ = q.shape
    group = max(1, 256 // tokens)
    low = group * tokens
    count = chips // group
    rows = min(512, length)
    width = lead + heads * HEAD
    n = down.shape[1]
    out_width = -(-(heads + 2) * HEAD // LANES) * LANES
    high = d // chips
    least, _ = tile_share(columns // LANES, chips)
    held = [
        Paired.scratch(chips, (high, least * LANES), BF16) + Paired.scratch(chips, (high, LANES), BF16),
        Paired.scratch(chips, (high // 2, width), BF16),
    ]
    early = lambda i: jnp.minimum(i, count - 1)
    late = lambda i: jnp.maximum(i - count, 0)
    first = pl.BlockSpec((low, n), lambda i: (early(i), 0))
    per_query = pl.BlockSpec((heads, rows, HEAD), lambda i: (0, late(i), 0))
    whole = resident((length, HEAD))
    return pl.pallas_call(
        functools.partial(backward_kernel, chips, lead, [len(h) for h in held]),
        grid=(count + length // rows,),
        in_specs=[
            pl.BlockSpec((group, tokens, d), lambda i: (early(i), 0, 0)),
            resident((d, width), small.shape[1] // width - 1),
            resident((d, n)),
            first,
            per_query,
            whole,
            whole,
            per_query,
            pl.BlockSpec((heads, 1, rows), lambda i: (0, 0, late(i))),
            whole,
            whole,
            ANY,
            ANY,
        ],
        out_specs=[first, resident((length, out_width)), ANY, ANY],
        out_shape=[
            jax.ShapeDtypeStruct((length, n), BF16),
            jax.ShapeDtypeStruct((length, out_width), BF16),
            jax.ShapeDtypeStruct((high, columns), BF16),
            jax.ShapeDtypeStruct((chips, high // 2, width), BF16),
        ],
        scratch_shapes=[
            pltpu.VMEM((heads, length, HEAD), BF16),
            pltpu.VMEM((rows, HEAD), F32),
            pltpu.VMEM((length, HEAD), F32),
            pltpu.VMEM((length, HEAD), F32),
        ]
        + [s for h in held for s in h],
        compiler_params=pltpu.CompilerParams(collective_id=number, has_side_effects=True, vmem_limit_bytes=60 << 20),
        cost_estimate=pl.CostEstimate(
            flops=2 * length * d * (n + width) + 5 * heads * length * length * HEAD,
            transcendentals=heads * length * length // 2,
            bytes_accessed=2 * length * d,
        ),
        name="backward",
    )(g, small, down, slope, q, k, v, o, lse, cosines, sines, down_part, dense_part)


def out_kernel(a_ref, b_ref, small_ref, wide_ref, out_ref):
    tokens, d = out_ref.shape[-2:]
    step = a_ref.shape[0] // tokens
    a, b = a_ref[...], b_ref[...]
    for at, width in chunks(d, 512):
        part = dot(a, small_ref[at : at + width], ROWS_COLS) + dot(b, wide_ref[at : at + width], ROWS_COLS)
        part = part.astype(BF16).reshape(step, tokens, width)
        if out_ref.ndim == 4:
            out_ref[:, 0, :, at : at + width] = part
        else:
            out_ref[:, :, at : at + width] = part


def out_product(a, b, small, column, wide, chips, name, by_plane=False):
    length, width = a.shape
    tokens, d = length // chips, small.shape[0]
    step = max(1, 512 // tokens)
    rows = step * tokens
    n = wide.shape[1]
    shape, spec = (chips, tokens, d), pl.BlockSpec((step, tokens, d), lambda i: (i, 0, 0))
    if by_plane:
        nz, ny, nx = grid_of(chips)
        per = ny * nx // step
        shape = (ny * nx, nz, tokens, d)
        spec = pl.BlockSpec((step, 1, tokens, d), lambda i: (lax.rem(i, per), i // per, 0, 0))
    return pl.pallas_call(
        out_kernel,
        grid=(chips // step,),
        in_specs=[per_row(rows, width), per_row(rows, n), resident((d, width), column), resident((d, n))],
        out_specs=spec,
        out_shape=jax.ShapeDtypeStruct(shape, BF16),
        compiler_params=pltpu.CompilerParams(vmem_limit_bytes=56 << 20),
        cost_estimate=pl.CostEstimate(
            flops=2 * length * d * (n + width), transcendentals=0, bytes_accessed=2 * length * d
        ),
        name=name,
    )(a, b, small, wide)


def weight_kernel(x_ref, a_ref, b_ref, small_ref, wide_ref):
    chips, tokens, width = x_ref.shape
    x = x_ref[...].reshape(chips * tokens, width)
    small_ref[...] = dot(x, a_ref[...], ROWS_ROWS).astype(BF16)
    for at, n in chunks(wide_ref.shape[1], 384):
        wide_ref[:, at : at + n] = dot(x, b_ref[:, at : at + n], ROWS_ROWS).astype(BF16)


def weight_product(x, a, b, name):
    chips, tokens, d = x.shape
    length = chips * tokens
    width = 768 if d % 768 == 0 else 512
    return pl.pallas_call(
        weight_kernel,
        grid=(d // width,),
        in_specs=[pl.BlockSpec((chips, tokens, width), lambda i: (0, 0, i)), resident(a.shape), resident(b.shape)],
        out_specs=[per_row(width, a.shape[1]), per_row(width, b.shape[1])],
        out_shape=[jax.ShapeDtypeStruct((d, a.shape[1]), BF16), jax.ShapeDtypeStruct((d, b.shape[1]), BF16)],
        compiler_params=pltpu.CompilerParams(vmem_limit_bytes=56 << 20),
        cost_estimate=pl.CostEstimate(
            flops=2 * length * d * (a.shape[1] + b.shape[1]), transcendentals=0, bytes_accessed=2 * length * d
        ),
        name=name,
    )(x, a, b)


def share_heads(columns, chips):
    rows, width = columns.shape
    heads = width // HEAD
    most = -(-heads // chips)
    richer = heads - chips * (most - 1)
    cut = richer * most * HEAD
    first = jnp.moveaxis(columns[:, :cut].reshape(rows, richer, most * HEAD), 1, 0)
    if richer == chips:
        return first
    rest = jnp.moveaxis(columns[:, cut:].reshape(rows, chips - richer, (most - 1) * HEAD), 1, 0)
    return jnp.concatenate([first, jnp.pad(rest, ((0, 0), (0, 0), (0, HEAD)))], 0)


def join_heads(parts, heads):
    chips, rows, width = parts.shape
    most = width // HEAD
    richer = heads - chips * (most - 1)
    first = jnp.moveaxis(parts[:richer], 0, 1).reshape(rows, -1)
    if richer == chips:
        return first
    rest = jnp.moveaxis(parts[richer:, :, : width - HEAD], 0, 1).reshape(rows, -1)
    return jnp.concatenate([first, rest], 1)


def swap(values):
    return lax.ppermute(values, "fsdp", [(0, 1), (1, 0)])


def in_order(mine, other, core, axis):
    return jnp.where(
        core == 0,
        jnp.concatenate([mine, other], axis),
        jnp.concatenate([other, mine], axis),
    )


def half_of(values, core, axis):
    first, second = jnp.split(values, 2, axis)
    return jnp.where(core == 0, first, second), jnp.where(core == 0, second, first)


def angles(length):
    inverse_freq = ROPE_BASE ** (-jnp.arange(0, HEAD, 2).astype(F32) / HEAD)
    phases = jnp.arange(length, dtype=jnp.int32).astype(F32)[:, None] * inverse_freq[None, :]
    phases = jnp.concatenate([phases, phases], -1)
    return jnp.cos(phases), jnp.sin(phases)


def body(layer_input, cotangent, norm_gain, norm_bias, qkv_weight, up_weight, dense_weight, down_weight):
    chips = lax.axis_size("ctx")
    core = lax.axis_index("fsdp")
    inputs = layer_input[0].astype(F32)
    tokens, features = inputs.shape
    length = tokens * chips
    heads = features // HEAD
    most = -(-heads // chips)
    qwide = most * HEAD
    rows = qkv_weight.shape[0]
    high = padded_rows(rows)
    wide_columns = up_weight.shape[1]
    lead = (qwide + 2 * HEAD) % LANES

    def pad(values):
        apart = values.reshape(*values.shape[:-1], chips, rows)
        apart = jnp.pad(apart, [(0, 0)] * (apart.ndim - 1) + [(0, high - rows)])
        return apart.reshape(*values.shape[:-1], chips * high)

    def unpad(values):
        apart = values.reshape(*values.shape[:-1], chips, high)[..., :rows]
        return apart.reshape(*values.shape[:-1], features)

    def pad_rows(weight):
        return jnp.pad(weight, ((0, high - rows), (0, 0)))

    center = inputs - jnp.mean(inputs, -1, keepdims=True)
    inverse = lax.rsqrt(jnp.mean(center * center, -1, keepdims=True) + EPS)
    xhat = center * inverse
    normed_low = pad((xhat * norm_gain + norm_bias).astype(BF16))
    grad_low = pad(cotangent[0])

    mine, other = half_of(pad_rows(jnp.concatenate([qkv_weight, dense_weight], 1)), core, 0)
    other = swap(other)
    qkv_columns = qkv_weight.shape[1]
    qkv_rows = in_order(mine[:, :qkv_columns], other[:, :qkv_columns], core, 1)
    dense_rows = in_order(mine[:, qkv_columns:], other[:, qkv_columns:], core, 1)
    blocks = jnp.concatenate(
        [
            share_heads(qkv_rows[:, :features], chips),
            jnp.broadcast_to(qkv_rows[:, features:], (chips, high // 2, 2 * HEAD)),
            share_heads(dense_rows, chips),
        ],
        2,
    )
    normed_all, up_cols, small = bring(
        chips, 0, "bring", (Gather, normed_low), (Columns, pad_rows(up_weight)), (Blocks, blocks)
    )

    cosines, sines = angles(length)
    dense_block = small.shape[1] // (lead + qwide) - 1
    (queries, keys, values, hidden_low, slope, attended_low, attention, log_sum), (grad_all, down_cols) = forward(
        normed_all,
        small,
        up_cols,
        cosines,
        sines,
        most,
        lead,
        2,
        [(Gather, grad_low), (Columns, pad_rows(down_weight))],
    )
    branch = out_product(attended_low, hidden_low, small, dense_block, down_cols, chips, "forward_out", True)
    branch, grad_all = lax.optimization_barrier((branch, grad_all))
    nz, ny, nx = grid_of(chips)
    planes = [[z * ny * nx + i for i in range(ny * nx)] for z in range(nz)]
    lines = [[z * ny * nx + i for z in range(nz)] for i in range(ny * nx)]
    branch = branch.reshape(ny * nx, nz * tokens, -1)
    branch = lax.psum_scatter(branch, "ctx", scatter_dimension=0, axis_index_groups=planes, tiled=False)

    dense_part, down_part = weight_product(grad_all, attended_low, hidden_low, "late_weights")
    grad_up, grad_joined, down_grad, dense_total = backward(
        grad_all,
        small,
        lead,
        down_cols,
        slope,
        queries,
        keys,
        values,
        attention,
        log_sum,
        cosines,
        sines,
        3,
        down_part,
        dense_part,
        wide_columns,
    )
    branch, grad_joined = lax.optimization_barrier((branch, grad_joined))
    branch = branch.reshape(nz, tokens, -1)
    branch = lax.psum_scatter(branch, "ctx", scatter_dimension=0, axis_index_groups=lines, tiled=False)
    layer_output = (inputs + unpad(branch).astype(F32)).astype(BF16)
    grad_normed = out_product(grad_joined, grad_up, small, 0, up_cols, chips, "back_out")

    input_grad, stats, up_grad, total = send(
        chips,
        1,
        features,
        grad_normed,
        normed_all,
        grad_joined,
        grad_up,
        wide_columns,
        pad(xhat),
        grad_low,
        pad(norm_gain[None]),
        inverse,
    )
    up_grad = up_grad[:rows].astype(F32)
    down_grad = down_grad[:rows].astype(F32)
    qkv_rows = jnp.concatenate(
        [
            join_heads(total[:, :, :qwide], heads),
            jnp.sum(total[:, :, qwide : qwide + 2 * HEAD].astype(F32), 0).astype(BF16),
        ],
        1,
    )
    dense_rows = join_heads(dense_total[:, :, lead:], heads)

    def own_columns(values):
        mine, other = half_of(values, core, 1)
        return in_order(mine, swap(other), core, 0)[:rows].astype(F32)

    stats = unpad(stats)
    return (
        layer_output[None],
        unpad(input_grad)[None],
        stats[0],
        stats[1],
        own_columns(qkv_rows),
        up_grad,
        own_columns(dense_rows),
        down_grad,
    )


def solution(mesh):
    split = P("ctx", "fsdp")
    stream = P("fsdp", "ctx", None)
    return jax.shard_map(
        body,
        mesh=mesh,
        in_specs=(stream, stream, P(), P(), split, split, split, split),
        out_specs=(stream, stream, P(), P(), split, split, split, split),
        check_vma=False,
    )
```

```python
import functools

import jax
import jax.numpy as jnp
from jax import lax
from jax.experimental import pallas as pl
from jax.experimental.pallas import tpu as pltpu
from jax.sharding import PartitionSpec as P

HEADS = 71
HEAD = 64
EPS = 1e-05
ROPE_BASE = 10000.0
MASKED = -1e30
LANES = 128
F32 = jnp.float32
BF16 = jnp.bfloat16
ROWS_COLS = (((1,), (1,)), ((), ()))
ROWS_ROWS = (((0,), (0,)), ((), ()))
MESH = pl.DeviceIdType.MESH
ANY = pl.BlockSpec(memory_space=pl.ANY)
WHOLE = pl.BlockSpec(memory_space=pltpu.VMEM)
DMA = pltpu.SemaphoreType.DMA


def dot(a, b, dims=None):
    if dims is None:
        return jnp.dot(a, b, preferred_element_type=F32)
    return lax.dot_general(a, b, dims, preferred_element_type=F32)


def grid_of(chips):
    return (4, 4, 4) if chips == 64 else (chips // 4, 2, 2)


def padded_rows(rows):
    return -(-rows // 16) * 16


def tile_share(tiles, chips):
    return tiles // chips, tiles % chips


class Place:
    def __init__(self, chips):
        self.chips = chips
        self.nz, self.ny, self.nx = grid_of(chips)
        self.me = lax.axis_index("ctx")
        self.core = lax.axis_index("fsdp")
        self.z = self.me // (self.ny * self.nx)
        self.y = lax.rem(self.me // self.nx, self.ny)
        self.x = lax.rem(self.me, self.nx)

    def at(self, dz, dy, dx):
        z = lax.rem(self.z + dz + self.nz, self.nz)
        y = lax.rem(self.y + dy + self.ny, self.ny)
        x = lax.rem(self.x + dx + self.nx, self.nx)
        return (z * self.ny + y) * self.nx + x

    def pair(self, i):
        return self.me ^ i


def enter(place):
    barrier = pltpu.get_barrier_semaphore()

    def greet(i):
        pl.semaphore_signal(barrier, 1, device_id=(place.pair(i), place.core), device_id_type=MESH)

    each(1, place.chips, greet)
    pl.semaphore_signal(barrier, 1, device_id=(place.me, 1 - place.core), device_id_type=MESH)
    pl.semaphore_wait(barrier, place.chips)


def remote(src, dst, send, recv, chip, core):
    return pltpu.make_async_remote_copy(
        src_ref=src, dst_ref=dst, send_sem=send, recv_sem=recv, device_id=(chip, core), device_id_type=MESH
    )


def each(first, last, do):
    def step(i, carry):
        do(i)
        return carry

    lax.fori_loop(first, last, step, 0)


def when(condition, do):
    if condition is None:
        do()
    else:
        pl.when(condition)(do)


def rows_at(start, count):
    return pl.ds(pl.multiple_of(start, 8), count)


def lanes_at(tile, count):
    return pl.ds(pl.multiple_of(tile * LANES, LANES), count * LANES)


def move(src, dst, sem):
    copy = pltpu.make_async_copy(src, dst, sem)
    copy.start()
    copy.wait()


class Tiles:
    def __init__(self, columns, chips):
        self.chips = chips
        self.least, self.richer = tile_share(columns // LANES, chips)
        assert 0 < self.least and 2 * self.richer <= chips

    def more(self, chip, core):
        return jnp.where(core == 0, chip < self.richer, chip >= self.chips - self.richer)

    def first(self, chip, core):
        late = jnp.maximum(chip - (self.chips - self.richer), 0)
        return self.least * chip + jnp.where(core == 0, jnp.minimum(chip, self.richer), late)

    def cut(self, ref, chip, core):
        start = self.first(chip, core)
        return (
            ref.at[:, lanes_at(start, self.least)],
            ref.at[:, lanes_at(jnp.minimum(start + self.least, self.first(self.chips, core) - 1), 1)],
        )


class Gather:
    @staticmethod
    def shape(chips, a):
        return (chips, *a.shape)

    @staticmethod
    def scratch(chips, a):
        nz, ny, nx = grid_of(chips)
        return [DMA((nz,))] * 2 + [DMA((nz, nx))] * 2 + [DMA((nz, ny))] * 2 + [DMA((nz, nx, ny))] * 4 + [DMA, DMA((nz,))]

    def __init__(self, place, mine, out, sems):
        self.p, self.mine, self.out = place, mine, out
        (self.sl, self.rl, self.sx, self.rx, self.sy, self.ry, self.s1, self.r1, self.s2, self.r2, self.own, self.sr) = sems
        self.half = mine.shape[0] // 2

    def line(self, k):
        p = self.p
        return remote(self.mine, self.out.at[p.me], self.sl.at[k], self.rl.at[k], p.at(k, 0, 0), p.core)

    def direct(self, k):
        p = self.p
        to = lax.rem(p.z + k, p.nz)
        middle = p.nz // 2
        far = ((to == p.nz - 1) & (p.z < middle)) | ((to == 0) & (p.z >= middle))
        return jnp.logical_not(far)

    def relay(self, k):
        p = self.p
        source = lax.rem(p.z - k + p.nz, p.nz)
        middle = p.nz // 2
        up = (p.z == p.nz - 2) & (source < middle)
        down = (p.z == 1) & (source >= middle)
        b = p.at(-k, 0, 0)
        index = jnp.where(up, k + 1, k - 1)
        copy = remote(self.out.at[b], self.out.at[b], self.sr.at[k], self.rl.at[index], p.at(jnp.where(up, 1, -1), 0, 0), p.core)
        return copy, up | down

    def across(self, k, i):
        p = self.p
        b = p.at(-k, 0, 0)
        src = self.mine if isinstance(k, int) and k == 0 else self.out.at[b]
        return remote(src, self.out.at[b], self.sx.at[k, i], self.rx.at[k, i], p.at(0, 0, i), p.core)

    def along(self, k, j):
        p = self.p
        b = p.at(-k, 0, 0)
        src = self.mine if isinstance(k, int) and k == 0 else self.out.at[b]
        return remote(src, self.out.at[b], self.sy.at[k, j], self.ry.at[k, j], p.at(0, j, 0), p.core)

    def corner1(self, k, i, j):
        p = self.p
        part = self.out.at[p.at(-k, 0, -i), pl.ds(0, self.half)]
        return remote(part, part, self.s1.at[k, i, j], self.r1.at[k, i, j], p.at(0, j, 0), p.core)

    def corner2(self, k, i, j):
        p = self.p
        part = self.out.at[p.at(-k, -j, 0), pl.ds(self.half, self.half)]
        return remote(part, part, self.s2.at[k, i, j], self.r2.at[k, i, j], p.at(0, 0, i), p.core)

    def spread(self, k):
        for i in range(1, self.p.nx):
            self.across(k, i).start()
        for j in range(1, self.p.ny):
            self.along(k, j).start()

    def begin(self):
        for k in range(1, self.p.nz):
            pl.when(self.direct(k))(self.line(k).start)
        self.spread(0)
        pltpu.make_async_copy(self.mine, self.out.at[self.p.me], self.own).start()

    def turn(self, k):
        p = self.p
        for i in range(1, p.nx):
            self.across(k, i).wait_recv()
            for j in range(1, p.ny):
                self.corner1(k, i, j).start()
        for j in range(1, p.ny):
            self.along(k, j).wait_recv()
            for i in range(1, p.nx):
                self.corner2(k, i, j).start()

    def steps(self):
        p = self.p
        assert p.nz == 4
        first = jnp.where(p.z == 0, 3, 1)
        last = jnp.where(p.z == 0, 1, jnp.where(p.z == 3, 3, 2))
        order = [first, 6 - first - last, last]

        def come(k):
            self.line(k).wait_recv()
            copy, needed = self.relay(k)
            pl.when(needed)(copy.start)
            self.spread(k)

        return (
            [functools.partial(self.turn, 0)]
            + [functools.partial(come, k) for k in order]
            + [functools.partial(self.turn, k) for k in order]
        )

    def end(self):
        p = self.p
        pltpu.make_async_copy(self.mine, self.out.at[p.me], self.own).wait()
        for k in range(p.nz):
            if k:
                pl.when(self.direct(k))(self.line(k).wait_send)
                copy, needed = self.relay(k)
                pl.when(needed)(copy.wait_send)
            for i in range(1, p.nx):
                self.across(k, i).wait_send()
            for j in range(1, p.ny):
                self.along(k, j).wait_send()
            for i in range(1, p.nx):
                for j in range(1, p.ny):
                    self.corner1(k, i, j).wait()
                    self.corner2(k, i, j).wait()


class Columns:
    @staticmethod
    def shape(chips, a):
        least, _ = tile_share(a.shape[1] // LANES, chips)
        return (chips * a.shape[0], (2 * least + 1) * LANES)

    @staticmethod
    def scratch(chips, a):
        return [DMA((chips,))] * 8 + [pltpu.VMEM((a.shape[0], LANES), a.dtype)]

    def __init__(self, place, weight, out, sems):
        self.p, self.w, self.out = place, weight, out
        self.ms, self.mr, self.es, self.er, self.fs, self.fr, self.gs, self.gr, self.nought = sems
        self.tiles = Tiles(weight.shape[1], place.chips)
        self.rows = weight.shape[0]

    def slots(self, chip, own):
        rows = rows_at(chip * self.rows, self.rows)
        least = self.tiles.least
        return self.out.at[rows, lanes_at(0 if own else least + 1, least)], self.out.at[rows, lanes_at(least, 1)]

    def sends(self, i):
        p = self.p
        chip = p.pair(i)
        (a, b), (c, d) = self.tiles.cut(self.w, chip, p.core), self.slots(p.me, True)
        return (
            remote(a, c, self.ms.at[i], self.mr.at[i], chip, p.core),
            remote(b, d, self.es.at[i], self.er.at[i], chip, p.core),
            self.tiles.more(chip, p.core),
        )

    def gets(self, i):
        p = self.p
        chip = p.pair(i)
        (a, b), (c, d) = self.tiles.cut(self.w, chip, p.core), self.slots(chip, True)
        return (
            remote(a, c, self.ms.at[i], self.mr.at[i], chip, p.core),
            remote(b, d, self.es.at[i], self.er.at[i], chip, p.core),
        )

    def passes(self, i):
        p = self.p
        chip = p.pair(i)
        a, b = self.slots(chip, True)
        if isinstance(i, int) and i == 0:
            a, b = self.tiles.cut(self.w, p.me, p.core)
        c, d = self.slots(chip, False)
        return (
            remote(a, c, self.fs.at[i], self.fr.at[i], p.me, 1 - p.core),
            remote(b, d, self.gs.at[i], self.gr.at[i], p.me, 1 - p.core),
        )

    def here(self):
        p = self.p
        (a, b), (c, d) = self.tiles.cut(self.w, p.me, p.core), self.slots(p.me, True)
        return pltpu.make_async_copy(a, c, self.ms.at[0]), pltpu.make_async_copy(b, d, self.es.at[0])

    def begin(self):
        p = self.p

        def send(i):
            main, extra, more = self.sends(i)
            main.start()
            pl.when(more)(extra.start)

        each(1, p.chips, send)
        own, pass_on = self.here(), self.passes(0)
        own[0].start()
        pass_on[0].start()

        @pl.when(self.tiles.more(p.me, p.core))
        def _():
            own[1].start()
            pass_on[1].start()

    def steps(self):
        return [self.hand_on]

    def hand_on(self):
        p = self.p
        mine = self.tiles.more(p.me, p.core)

        def hand(i):
            main, extra = self.gets(i)
            to_main, to_extra = self.passes(i)
            main.wait_recv()
            to_main.start()

            @pl.when(mine)
            def _():
                extra.wait_recv()
                to_extra.start()

        each(1, p.chips, hand)

    def end(self):
        p = self.p
        mine = self.tiles.more(p.me, p.core)
        theirs = self.tiles.more(p.me, 1 - p.core)
        own = self.here()
        own[0].wait()
        pl.when(mine)(own[1].wait)

        @pl.when(jnp.logical_not(mine | theirs))
        def _():
            self.nought[...] = jnp.zeros_like(self.nought)
            each(0, p.chips, lambda c: move(self.nought, self.slots(c, True)[1], self.es.at[0]))

        def sent(i):
            main, extra, more = self.sends(i)
            main.wait_send()
            pl.when(more)(extra.wait_send)

        each(1, p.chips, sent)

        def handed(i):
            main, extra = self.passes(i)
            main.wait()
            pl.when(mine)(extra.wait_send)
            pl.when(theirs)(extra.wait_recv)

        handed(0)
        each(1, p.chips, handed)


class Blocks:
    @staticmethod
    def shape(chips, a):
        return (chips * 2 * a.shape[1], a.shape[2])

    @staticmethod
    def scratch(chips, a):
        return [DMA((chips,))] * 4

    def __init__(self, place, blocks, out, sems):
        self.p, self.b, self.out = place, blocks, out
        self.s, self.r, self.fs, self.fr = sems
        self.rows = blocks.shape[1]

    def slot(self, chip, core):
        return self.out.at[rows_at((2 * chip + core) * self.rows, self.rows)]

    def sends(self, i):
        p = self.p
        chip = p.pair(i)
        return remote(self.b.at[chip], self.slot(p.me, p.core), self.s.at[i], self.r.at[i], chip, p.core)

    def passes(self, i):
        p = self.p
        part = self.slot(p.pair(i), p.core)
        mine = self.b.at[p.me] if isinstance(i, int) and i == 0 else part
        return remote(mine, part, self.fs.at[i], self.fr.at[i], p.me, 1 - p.core)

    def here(self):
        p = self.p
        return pltpu.make_async_copy(self.b.at[p.me], self.slot(p.me, p.core), self.s.at[0])

    def begin(self):
        each(1, self.p.chips, lambda i: self.sends(i).start())
        self.here().start()
        self.passes(0).start()

    def steps(self):
        return [self.hand_on]

    def hand_on(self):
        def hand(i):
            self.sends(i).wait_recv()
            self.passes(i).start()

        each(1, self.p.chips, hand)

    def end(self):
        p = self.p
        self.here().wait()
        each(1, p.chips, lambda i: self.sends(i).wait_send())
        self.passes(0).wait()
        each(1, p.chips, lambda i: self.passes(i).wait())


def drive(parts):
    for part in parts:
        part.begin()
    todo = [part.steps() for part in parts]
    total = max(len(steps) for steps in todo)
    for at in range(total):
        for steps in todo:
            index = at - (total - len(steps))
            if index >= 0:
                steps[index]()
    for part in parts:
        part.end()


def take(refs, counts):
    out, at = [], 0
    for count in counts:
        out.append(refs[at : at + count])
        at += count
    return out


def bring_kernel(chips, plan, *refs):
    n = len(plan)
    ins, outs, held = refs[:n], refs[n : 2 * n], refs[2 * n :]
    place = Place(chips)
    enter(place)
    held = take(held, [count for _, count in plan])
    drive([kind(place, a, o, h) for (kind, _), a, o, h in zip(plan, ins, outs, held)])


def bring(chips, number, name, *jobs):
    held = [kind.scratch(chips, a) for kind, a in jobs]
    return pl.pallas_call(
        functools.partial(bring_kernel, chips, [(kind, len(h)) for (kind, _), h in zip(jobs, held)]),
        in_specs=[ANY] * len(jobs),
        out_specs=[ANY] * len(jobs),
        out_shape=[jax.ShapeDtypeStruct(kind.shape(chips, a), a.dtype) for kind, a in jobs],
        scratch_shapes=[s for h in held for s in h],
        compiler_params=pltpu.CompilerParams(collective_id=number, has_side_effects=True, vmem_limit_bytes=16 << 20),
        name=name,
    )(*[a for _, a in jobs])


class Paired:
    @staticmethod
    def scratch(chips, shape, dtype):
        return [DMA((chips,))] * 5 + [pltpu.VMEM((chips, *shape), dtype)] * 2

    def __init__(self, place, held, views, gives=None, sums=None, comes=lambda j: None):
        self.p = place
        self.cs, self.cr, self.s, self.r, self.load, self.total, self.stage = held
        self.mine, self.theirs, self.target, self.source = views
        self.gives, self.sums, self.comes = gives, sums, comes

    def across(self, i):
        p = self.p
        return remote(self.theirs(p.pair(i)), self.stage.at[i], self.cs.at[i], self.cr.at[i], p.me, 1 - p.core)

    def fetch(self, i):
        return pltpu.make_async_copy(self.mine(self.p.pair(i)), self.total.at[i], self.load.at[i])

    def sends(self, i):
        p = self.p
        j = p.pair(i)
        return remote(self.total.at[i], self.target(j), self.s.at[i], self.r.at[i], j, p.core)

    def gets(self, i):
        p = self.p
        j = p.pair(i)
        return remote(self.total.at[i], self.source(j), self.s.at[i], self.r.at[i], j, p.core)

    def here(self):
        return pltpu.make_async_copy(self.total.at[0], self.source(self.p.me), self.s.at[0])

    def begin(self):
        chips = self.p.chips
        when(self.gives, lambda: each(0, chips, lambda i: self.across(i).start()))
        when(self.sums, lambda: each(0, chips, lambda i: self.fetch(i).start()))

    def add(self, i):
        self.fetch(i).wait()
        self.across(i).wait_recv()
        self.total[i] = (self.total[i].astype(F32) + self.stage[i].astype(F32)).astype(self.total.dtype)

    def some(self, first, last):
        def do(i):
            self.add(i)
            self.sends(i).start()

        when(self.sums, lambda: each(first, last, do))

    def own(self):
        def do():
            self.add(0)
            self.here().start()

        when(self.sums, do)

    def end(self):
        chips = self.p.chips
        when(self.gives, lambda: each(0, chips, lambda i: self.across(i).wait_send()))

        def sent():
            self.here().wait()
            each(1, chips, lambda i: self.sends(i).wait_send())

        when(self.sums, sent)

        def came(i):
            when(self.comes(self.p.pair(i)), lambda: self.gets(i).wait_recv())

        each(1, chips, came)

    def steps(self):
        chips = self.p.chips
        return [functools.partial(self.some, 1, chips), self.own]


class Scatter:
    @staticmethod
    def stages(chips, a):
        nz, _, n = grid_of(chips)
        _, t, d = a.shape
        h = t // 2
        return [(2, nz, n, n, h, d), (2, nz, n, h, d), (2, nz, n, h, d), (nz, t, d), (nz, t, d)]

    @staticmethod
    def scratch(chips, a):
        nz, _, n = grid_of(chips)
        _, t, d = a.shape
        h = t // 2
        most = max(n, nz)
        sems = [DMA((2, nz, n, n))] * 2 + [DMA((2, nz, n))] * 2 + [DMA((nz,))] * 2 + [DMA((most,)), DMA]
        return sems + [pltpu.VMEM((most, h, d), a.dtype), pltpu.VMEM((h, d), a.dtype)]

    def __init__(self, place, blocks, stages, held):
        self.p, self.b = place, blocks
        self.got1, self.sum1, self.got2, self.sum2, self.got3 = stages
        (self.s1, self.r1, self.s2, self.r2, self.s3, self.r3, self.load, self.store, self.parts, self.low) = held
        self.h = blocks.shape[1] // 2
        self.n = place.nx

    def chip(self, half, dz, du, dv):
        return self.p.at(dz, dv, du) if half == 0 else self.p.at(dz, du, dv)

    def rows(self, half):
        return pl.ds(half * self.h, self.h)

    def send1(self, half, dz, v, i):
        return remote(
            self.b.at[self.chip(half, dz, i, v), self.rows(half)],
            self.got1.at[half, dz, v, i],
            self.s1.at[half, dz, v, i],
            self.r1.at[half, dz, v, i],
            self.chip(half, 0, i, 0),
            self.p.core,
        )

    def send2(self, half, dz, v):
        return remote(
            self.sum1.at[half, dz, v],
            self.got2.at[half, dz, v],
            self.s2.at[half, dz, v],
            self.r2.at[half, dz, v],
            self.chip(half, 0, 0, v),
            self.p.core,
        )

    def beside(self):
        return jnp.where(lax.rem(self.p.z, 2) == 0, 1, self.p.nz - 1)

    def beyond(self, side):
        other = jnp.where(self.p.z < 2, 2, 0) + side
        return lax.rem(other - self.p.z + self.p.nz, self.p.nz)

    def inner(self):
        return (self.p.z == 1) | (self.p.z == 2)

    def near(self):
        p, dz = self.p, self.beside()
        return remote(self.sum2.at[dz], self.got3.at[0], self.s3.at[0], self.r3.at[0], p.at(dz, 0, 0), p.core)

    def lift(self, side):
        p, dz = self.p, self.beyond(side)
        to = p.at(self.beside(), 0, 0)
        return remote(self.sum2.at[dz], self.got3.at[2 + side], self.s3.at[1 + side], self.r3.at[2 + side], to, p.core)

    def far(self, side):
        p, dz = self.p, self.beyond(side)
        return remote(self.sum2.at[dz], self.got3.at[1], self.s3.at[1 + side], self.r3.at[1], p.at(dz, 0, 0), p.core)

    def fetch(self, refs):
        loads = [pltpu.make_async_copy(r, self.parts.at[i], self.load.at[i]) for i, r in enumerate(refs)]
        for copy in loads:
            copy.start()
        for copy in loads:
            copy.wait()

    def add(self, refs, to):
        self.fetch(refs)
        total = self.parts[0].astype(F32)
        for i in range(1, len(refs)):
            total = total + self.parts[i].astype(F32)
        self.low[...] = total.astype(self.low.dtype)
        move(self.low, to, self.store)

    def order(self):
        nz = self.p.nz
        return [nz // 2] + [k for k in range(1, nz) if k != nz // 2] + [0]

    def begin(self):
        for dz in self.order():
            for half in (0, 1):
                for v in list(range(1, self.n)) + [0]:
                    for i in range(1, self.n):
                        self.send1(half, dz, v, i).start()

    def first(self, dz):
        for half in (0, 1):
            for v in list(range(1, self.n)) + [0]:
                for i in range(1, self.n):
                    self.send1(half, dz, v, i).wait_recv()
                mine = self.b.at[self.chip(half, dz, 0, v), self.rows(half)]
                self.add([mine] + [self.got1.at[half, dz, v, i] for i in range(1, self.n)], self.sum1.at[half, dz, v])
                if v:
                    self.send2(half, dz, v).start()

    def second(self, dz):
        for half in (0, 1):
            for v in range(1, self.n):
                self.send2(half, dz, v).wait_recv()
            parts = [self.sum1.at[half, dz, 0]] + [self.got2.at[half, dz, v] for v in range(1, self.n)]
            self.add(parts, self.sum2.at[dz, self.rows(half)])
        if dz:
            pl.when(self.beside() == dz)(self.near().start)
            for side in (0, 1):
                pl.when((self.beyond(side) == dz) & jnp.logical_not(self.inner()))(self.lift(side).start)

    def relay(self):
        @pl.when(self.inner())
        def _():
            for side in (0, 1):
                self.lift(side).wait_recv()
                for half in (0, 1):
                    mine = self.sum2.at[self.beyond(side), self.rows(half)]
                    self.add([mine, self.got3.at[2 + side, self.rows(half)]], mine)
                self.far(side).start()

    def last(self):
        self.near().wait_recv()
        self.far(0).wait_recv()
        for half in (0, 1):
            rows = self.rows(half)
            self.fetch([self.sum2.at[0, rows], self.got3.at[0, rows], self.got3.at[1, rows]])
            self.finish(half)

    def steps(self):
        assert self.p.nz == 4
        order = self.order()
        steps = [functools.partial(self.first, order[0])]
        for old, new in zip(order[:-1], order[1:]):
            steps += [functools.partial(self.first, new), functools.partial(self.second, old)]
        return steps + [self.relay, functools.partial(self.second, order[-1]), self.last]

    def end(self):
        for dz in range(self.p.nz):
            for half in (0, 1):
                for v in range(self.n):
                    for i in range(1, self.n):
                        self.send1(half, dz, v, i).wait_send()
                    if v:
                        self.send2(half, dz, v).wait_send()
        self.near().wait_send()
        inner = self.inner()
        for side in (0, 1):
            pl.when(inner)(self.far(side).wait_send)
            pl.when(jnp.logical_not(inner))(self.lift(side).wait_send)


class NormBack(Scatter):
    @staticmethod
    def scratch(chips, a):
        d = a.shape[2]
        more = [pltpu.VMEM((2, 8, d), F32), pltpu.VMEM((2, d), F32), pltpu.VMEM((2, d), F32), pltpu.VMEM((chips, 2, d), F32)]
        return Scatter.scratch(chips, a) + more + [DMA((chips,))] * 2 + [DMA((3,))]

    def __init__(self, place, blocks, stages, held, operands, results, features):
        super().__init__(place, blocks, stages, held[:10])
        self.sums, self.mine, self.other, self.slots, self.ss, self.sr, self.pairs = held[10:]
        self.xhat, self.grad, self.gain, self.inverse = operands
        self.input_grad, self.stats = results
        self.features = features

    def begin(self):
        super().begin()
        self.sums[...] = jnp.zeros_like(self.sums)

    def finish(self, half):
        d = self.xhat.shape[1]

        def some(c):
            at = pl.multiple_of(c * 16, 16)
            total = self.parts[0, pl.ds(at, 16)].astype(F32)
            for i in (1, 2):
                total = total + self.parts[i, pl.ds(at, 16)].astype(F32)
            rows = pl.ds(pl.multiple_of(half * self.h + c * 16, 16), 16)
            xhat = self.xhat[rows]
            both = total * xhat
            self.sums[0] += both[:8] + both[8:]
            self.sums[1] += total[:8] + total[8:]
            scaled = total * self.gain[...]
            mean = jnp.sum(scaled, 1, keepdims=True) / self.features
            slope = jnp.sum(scaled * xhat, 1, keepdims=True) / self.features
            change = (scaled - mean - xhat * slope) * self.inverse[rows]
            self.input_grad[rows] = self.grad[rows].astype(F32) + change

        each(0, self.h // 16, some)

    def swap_stats(self):
        p = self.p
        return remote(self.mine, self.other, self.pairs.at[0], self.pairs.at[1], p.me, 1 - p.core)

    def share_stats(self, i):
        p = self.p
        return remote(self.mine, self.slots.at[p.me], self.ss.at[i], self.sr.at[i], p.pair(i), p.core)

    def get_stats(self, i):
        p = self.p
        return remote(self.mine, self.slots.at[p.pair(i)], self.ss.at[i], self.sr.at[i], p.pair(i), p.core)

    def stats_out(self):
        self.mine[0:1] = jnp.sum(self.sums[0], 0, keepdims=True)
        self.mine[1:2] = jnp.sum(self.sums[1], 0, keepdims=True)
        self.swap_stats().start()
        self.swap_stats().wait()
        self.mine[...] += self.other[...]
        self.slots[self.p.me] = self.mine[...]
        each(1, self.p.chips, lambda i: self.share_stats(i).start())

    def steps(self):
        return super().steps() + [self.stats_out]

    def end(self):
        super().end()

        def done(i):
            self.share_stats(i).wait_send()
            self.get_stats(i).wait_recv()

        each(1, self.p.chips, done)
        self.stats[...] = self.slots[0]

        def more(c):
            self.stats[...] += self.slots[c]

        each(1, self.p.chips, more)


def return_parts(place, part, out, held):
    tiles = Tiles(out.shape[1], place.chips)
    least, rows, core, me = tiles.least, out.shape[0], place.core, place.me
    n = len(held) // 2

    def at(j, tile, count):
        return part.at[rows_at(j * rows, rows), lanes_at(tile, count)]

    main = Paired(
        place,
        held[:n],
        (
            lambda j: at(j, 0, least),
            lambda j: at(j, least + 1, least),
            lambda j: tiles.cut(out, me, core)[0],
            lambda j: tiles.cut(out, j, core)[0],
        ),
    )
    extra = Paired(
        place,
        held[n:],
        (
            lambda j: at(j, least, 1),
            lambda j: at(j, least, 1),
            lambda j: tiles.cut(out, me, core)[1],
            lambda j: tiles.cut(out, j, core)[1],
        ),
        tiles.more(me, 1 - core),
        tiles.more(me, core),
        lambda j: tiles.more(j, core),
    )
    return [main, extra]


def trade_parts(place, part, out, held):
    rows = out.shape[1]

    def at(j, core):
        return part.at[rows_at((2 * j + core) * rows, rows)]

    views = (
        lambda j: at(j, place.core),
        lambda j: at(j, 1 - place.core),
        lambda j: out.at[place.me],
        lambda j: out.at[j],
    )
    return [Paired(place, held, views)]


def send_kernel(chips, features, counts, *refs):
    x_ref, a_ref, b_ref, blocks, xhat, grad, gain, inverse = refs[:8]
    input_grad, stats, wide_out, small_out, wide, small = refs[8:14]
    stages = refs[14:19]
    wide_tile, small_tile, stored = refs[19:22]
    norm_held, wide_held, small_held = take(refs[22:], counts)
    step = pl.program_id(0)
    count = pl.num_programs(0) - 1
    width = x_ref.shape[2]
    place = Place(chips)
    norm = NormBack(place, blocks, stages, norm_held, (xhat, grad, gain, inverse), (input_grad, stats), features)
    parts = return_parts(place, wide, wide_out, wide_held)
    parts += trade_parts(place, small, small_out, small_held)

    def stores(at):
        slot = lax.rem(at, 2)
        rows = rows_at(at * width, width)
        return (
            pltpu.make_async_copy(wide_tile.at[slot], wide.at[rows], stored.at[0, slot]),
            pltpu.make_async_copy(small_tile.at[slot], small.at[rows], stored.at[1, slot]),
        )

    def done(at):
        for copy in stores(at):
            copy.wait()

    @pl.when(step == 0)
    def _():
        enter(place)
        norm.begin()

    @pl.when(step < count)
    def _():
        slot = lax.rem(step, 2)
        pl.when(step >= 2)(lambda: done(step - 2))
        x = flat(x_ref)
        small_tile[slot] = dot(x, a_ref[...], ROWS_ROWS).astype(BF16)
        for at, n in chunks(b_ref.shape[1], 1152):
            wide_tile[slot, :, at : at + n] = dot(x, b_ref[:, at : at + n], ROWS_ROWS).astype(BF16)
        for copy in stores(step):
            copy.start()

    @pl.when(step == count)
    def _():
        done(step - 2)
        done(step - 1)
        for part in parts:
            part.begin()
        ahead, *rest = norm.steps()
        ahead()
        for part in parts:
            for do in part.steps():
                do()
        for do in rest:
            do()
        for part in [norm] + parts:
            part.end()


def send(chips, number, features, blocks, x, a, b, columns, xhat, grad, gain, inverse):
    _, tokens, d = blocks.shape
    length = chips * tokens
    rows = d // chips
    least, _ = tile_share(columns // LANES, chips)
    low, wide = a.shape[1], b.shape[1]
    width = 768 if d % 768 == 0 else 512
    count = d // width
    held = [
        NormBack.scratch(chips, blocks),
        Paired.scratch(chips, (rows, least * LANES), BF16) + Paired.scratch(chips, (rows, LANES), BF16),
        Paired.scratch(chips, (rows // 2, low), BF16),
    ]
    half = lambda *shape: jax.ShapeDtypeStruct(shape, BF16)
    results = pl.pallas_call(
        functools.partial(send_kernel, chips, features, [len(h) for h in held]),
        grid=(count + 1,),
        in_specs=[
            pl.BlockSpec((chips, tokens, width), lambda i: (0, 0, jnp.minimum(i, count - 1))),
            resident(a.shape),
            resident(b.shape),
            ANY,
            resident(xhat.shape),
            resident(grad.shape),
            resident(gain.shape),
            resident(inverse.shape),
        ],
        out_specs=[resident((tokens, d)), resident((2, d))] + [ANY] * 9,
        out_shape=[
            jax.ShapeDtypeStruct((tokens, d), F32),
            jax.ShapeDtypeStruct((2, d), F32),
            half(rows, columns),
            half(chips, rows // 2, low),
            half(d, wide),
            half(d, low),
        ]
        + [half(*s) for s in Scatter.stages(chips, blocks)],
        scratch_shapes=[pltpu.VMEM((2, width, wide), BF16), pltpu.VMEM((2, width, low), BF16), DMA((2, 2))]
        + [s for h in held for s in h],
        compiler_params=pltpu.CompilerParams(collective_id=number, has_side_effects=True, vmem_limit_bytes=60 << 20),
        cost_estimate=pl.CostEstimate(
            flops=2 * length * d * (low + wide), transcendentals=0, bytes_accessed=2 * length * d
        ),
        name="send",
    )(x, a, b, blocks, xhat, grad, gain, inverse)
    return results[:4]


def rotate(values, cosines, sines):
    middle = values.shape[-1] // 2
    turned = jnp.concatenate([-values[..., middle:], values[..., :middle]], -1)
    return values * cosines + turned * sines


def rotate_back(values, cosines, sines):
    middle = values.shape[-1] // 2
    turned = jnp.concatenate([values[..., middle:], -values[..., :middle]], -1)
    return values * cosines + turned * sines


def flat(ref):
    return ref[...].reshape(ref.shape[0] * ref.shape[1], ref.shape[2])


def chunks(width, most):
    return [(at, min(most, width - at)) for at in range(0, width, most)]


def resident(shape, column=0):
    return pl.BlockSpec(shape, lambda i: (0, column), pipeline_mode=pl.Buffered(1))


def per_row(rows, width):
    return pl.BlockSpec((rows, width), lambda i: (i, 0))


def forward_kernel(chips, plan, lead, events, *refs):
    n = len(plan)
    x_ref, small_ref, wide_ref, cos_ref, sin_ref = refs[:5]
    ins, refs = refs[5 : 5 + n], refs[5 + n :]
    q_out, k_out, v_out, hidden_ref, slope_ref, low_ref, o_ref, lse_ref = refs[:8]
    outs, refs = refs[8 : 8 + n], refs[8 + n :]
    q_all, k_all, v_all, acc, top = refs[:5]
    held = take(refs[5:], [count for _, count in plan])
    step = pl.program_id(0)
    half = pl.num_programs(0) // 2
    heads, rows, _ = q_out.shape
    place = Place(chips)
    parts = [kind(place, a, o, h) for (kind, _), a, o, h in zip(plan, ins, outs, held)]

    @pl.when(step == 0)
    def _():
        enter(place)
        for part in parts:
            part.begin()

    @pl.when(step < half)
    def _():
        here = pl.ds(pl.multiple_of(step * rows, rows), rows)
        x = flat(x_ref)
        cosines, sines = cos_ref[...], sin_ref[...]
        joined = dot(x, small_ref[...])
        for h in range(heads):
            q = rotate(joined[:, h * HEAD : (h + 1) * HEAD], cosines, sines).astype(BF16) * HEAD ** (-0.5)
            q_out[h] = q
            q_all[h, here] = q
        at = heads * HEAD
        k = rotate(joined[:, at : at + HEAD], cosines, sines).astype(BF16)
        v = joined[:, at + HEAD : at + 2 * HEAD].astype(BF16)
        k_out[...] = k
        v_out[...] = v
        k_all[here] = k
        v_all[here] = jnp.concatenate([v, jnp.ones_like(v)], 1)
        for at, width in chunks(wide_ref.shape[1], 384):
            up = dot(x, wide_ref[:, at : at + width])
            bell = 0.5 + 0.5 * lax.erf(up * 0.5**0.5)
            hidden_ref[:, at : at + width] = (up * bell).astype(BF16)
            slope = bell + up * jnp.exp(up * up * -0.5) * (2 * jnp.pi) ** (-0.5)
            slope_ref[:, at : at + width] = slope.astype(BF16)

    @pl.when(step >= half)
    def _():
        index = step - half
        here = pl.ds(pl.multiple_of(index * rows, rows), rows)
        lows = []
        for h in range(heads):
            q = q_all[h, here]
            acc[...] = jnp.zeros_like(acc)
            top[...] = jnp.full_like(top, MASKED)

            def block(start, masked):
                s = dot(q, k_all[pl.ds(start, rows), :], ROWS_COLS)
                if masked:
                    key = lax.broadcasted_iota(jnp.int32, s.shape, 1)
                    query = lax.broadcasted_iota(jnp.int32, s.shape, 0)
                    s = jnp.where(key <= query, s, MASKED)
                old = top[...]
                new = jnp.maximum(old, jnp.max(s, 1, keepdims=True))
                p = jnp.exp(s - new).astype(BF16)
                acc[...] = acc[...] * jnp.exp(old - new) + dot(p, v_all[pl.ds(start, rows), :])
                top[...] = new

            each(0, index, lambda i: block(pl.multiple_of(i * rows, rows), False))
            block(pl.multiple_of(index * rows, rows), True)
            total = acc[...]
            norm = total[:, HEAD : HEAD + 1]
            out = total[:, :HEAD] / norm
            o_ref[h] = out
            lows.append(out.astype(BF16))
            lse = jnp.broadcast_to(top[...] + jnp.log(norm), (rows, LANES))
            lse_ref[h] = lse.T[:1]
        if lead:
            lows = [jnp.zeros((rows, lead), BF16)] + lows
        low_ref[...] = jnp.concatenate(lows, 1)

    todo = []
    longest = max(len(part.steps()) for part in parts)
    for at in range(longest):
        for part in parts:
            steps = part.steps()
            index = at - (longest - len(steps))
            if index >= 0:
                todo.append(steps[index])
    cuts = [0, *[c for _, c in events], len(todo)]
    for (back, _), first, last in zip([*events, (0, None)], cuts[:-1], cuts[1:]):

        @pl.when(step == pl.num_programs(0) - 1 - back)
        def _():
            for do in todo[first:last]:
                do()

    @pl.when(step == pl.num_programs(0) - 1)
    def _():
        for part in parts:
            part.end()


def forward(x, small, wide, cosines, sines, heads, lead, number, jobs):
    chips, tokens, d = x.shape
    length = chips * tokens
    step = max(1, 512 // tokens)
    rows = step * tokens
    half = chips // step
    width = -(-(heads + 2) * HEAD // LANES) * LANES
    n = wide.shape[1]
    low = lead + heads * HEAD
    held = [kind.scratch(chips, a) for kind, a in jobs]
    plan = [(kind, len(h)) for (kind, _), h in zip(jobs, held)]
    early = lambda i: jnp.minimum(i, half - 1)
    late = lambda i: jnp.maximum(i - half, 0)
    first = lambda w: pl.BlockSpec((rows, w), lambda i: (early(i), 0))
    events = ((6, 2), (5, 3), (4, 4), (3, 5), (2, 6), (1, 7)) if half == 4 else ((4, 1), (2, 3), (1, 4))
    results = pl.pallas_call(
        functools.partial(forward_kernel, chips, plan, lead, events),
        grid=(2 * half,),
        in_specs=[
            pl.BlockSpec((step, tokens, d), lambda i: (early(i), 0, 0)),
            resident((d, width)),
            resident((d, n)),
            first(HEAD),
            first(HEAD),
        ]
        + [ANY] * len(jobs),
        out_specs=[
            pl.BlockSpec((heads, rows, HEAD), lambda i: (0, early(i), 0)),
            first(HEAD),
            first(HEAD),
            first(n),
            first(n),
            pl.BlockSpec((rows, low), lambda i: (late(i), 0)),
            pl.BlockSpec((heads, rows, HEAD), lambda i: (0, late(i), 0)),
            pl.BlockSpec((heads, 1, rows), lambda i: (0, 0, late(i))),
        ]
        + [ANY] * len(jobs),
        out_shape=[
            jax.ShapeDtypeStruct((heads, length, HEAD), BF16),
            jax.ShapeDtypeStruct((length, HEAD), BF16),
            jax.ShapeDtypeStruct((length, HEAD), BF16),
            jax.ShapeDtypeStruct((length, n), BF16),
            jax.ShapeDtypeStruct((length, n), BF16),
            jax.ShapeDtypeStruct((length, low), BF16),
            jax.ShapeDtypeStruct((heads, length, HEAD), F32),
            jax.ShapeDtypeStruct((heads, 1, length), F32),
        ]
        + [jax.ShapeDtypeStruct(kind.shape(chips, a), a.dtype) for kind, a in jobs],
        scratch_shapes=[
            pltpu.VMEM((heads, length, HEAD), BF16),
            pltpu.VMEM((length, HEAD), BF16),
            pltpu.VMEM((length, 2 * HEAD), BF16),
            pltpu.VMEM((rows, 2 * HEAD), F32),
            pltpu.VMEM((rows, 1), F32),
        ]
        + [s for h in held for s in h],
        compiler_params=pltpu.CompilerParams(collective_id=number, has_side_effects=True, vmem_limit_bytes=58 << 20),
        cost_estimate=pl.CostEstimate(
            flops=2 * length * d * (n + width) + 2 * heads * length * length * HEAD,
            transcendentals=2 * length * n + heads * length * length // 2,
            bytes_accessed=2 * length * d,
        ),
        name="forward",
    )(x, small, wide, cosines, sines, *[a for _, a in jobs])
    return results[:8], results[8:]


def backward_kernel(chips, lead, counts, *refs):
    g_ref, dense_ref, down_ref, slope_ref, q_ref, k_ref, v_ref, o_ref, lse_ref, cos_ref, sin_ref = refs[:11]
    wide, small = refs[11:13]
    grad_ref, out_ref, wide_out, small_out = refs[13:17]
    g_all, acc, dk, dv = refs[17:21]
    wide_held, small_held = take(refs[21:], counts)
    heads, rows, _ = q_ref.shape
    length = g_all.shape[1]
    count = pl.num_programs(0) - length // rows
    step = pl.program_id(0)
    scale = HEAD ** (-0.5)
    place = Place(chips)
    parts = return_parts(place, wide, wide_out, wide_held) + trade_parts(place, small, small_out, small_held)

    @pl.when(step == 0)
    def _():
        enter(place)
        for part in parts:
            part.begin()

    @pl.when(step < count)
    def _():
        g = flat(g_ref)
        low = g.shape[0]
        here = pl.ds(pl.multiple_of(step * low, low), low)
        grad = dot(g, dense_ref[...]).astype(BF16)
        for h in range(heads):
            g_all[h, here] = grad[:, lead + h * HEAD : lead + (h + 1) * HEAD]
        for at, width in chunks(down_ref.shape[1], 384):
            part = dot(g, down_ref[:, at : at + width])
            grad_ref[:, at : at + width] = (part * slope_ref[:, at : at + width].astype(F32)).astype(BF16)

    @pl.when(step == count)
    def _():
        dk[...] = jnp.zeros_like(dk)
        dv[...] = jnp.zeros_like(dv)
        out_ref[...] = jnp.zeros_like(out_ref)

    @pl.when(step >= count)
    def _():
        index = step - count
        here = pl.ds(pl.multiple_of(index * rows, rows), rows)
        cosines, sines = cos_ref[here], sin_ref[here]
        grads = []
        for h in range(heads):
            q = q_ref[h]
            g = g_all[h, here]
            lse = lse_ref[h]
            delta = jnp.sum((g.astype(F32) * o_ref[h]).T, 0, keepdims=True)
            acc[...] = jnp.zeros_like(acc)

            def block(start, masked):
                at = pl.ds(start, rows)
                k = k_ref[at, :]
                p = jnp.exp(dot(k, q, ROWS_COLS) - lse)
                if masked:
                    key = lax.broadcasted_iota(jnp.int32, p.shape, 0)
                    query = lax.broadcasted_iota(jnp.int32, p.shape, 1)
                    p = jnp.where(key <= query, p, 0.0)
                dp = dot(v_ref[at, :], g, ROWS_COLS)
                ds = (p * (dp - delta)).astype(BF16)
                dv[at, :] += dot(p.astype(BF16), g)
                dk[at, :] += dot(ds, q)
                acc[...] += dot(ds, k, ROWS_ROWS)

            each(0, index, lambda i: block(pl.multiple_of(i * rows, rows), False))
            block(pl.multiple_of(index * rows, rows), True)
            grads.append(rotate_back(acc[...] * scale, cosines, sines).astype(BF16))
        out_ref[here, : heads * HEAD] = jnp.concatenate(grads, 1)

    @pl.when(step == 1)
    def _():
        for part in parts:
            for do in part.steps():
                do()

    @pl.when(step == pl.num_programs(0) - 1)
    def _():
        keys = rotate_back(dk[...], cos_ref[...], sin_ref[...]).astype(BF16)
        both = jnp.concatenate([keys, dv[...].astype(BF16)], 1)
        out_ref[:, heads * HEAD : (heads + 2) * HEAD] = both
        for part in parts:
            part.end()


def backward(g, small, lead, down, slope, q, k, v, o, lse, cosines, sines, number, down_part, dense_part, columns):
    chips, tokens, d = g.shape
    heads, length, _ = q.shape
    group = max(1, 256 // tokens)
    low = group * tokens
    count = chips // group
    rows = min(512, length)
    width = lead + heads * HEAD
    n = down.shape[1]
    out_width = -(-(heads + 2) * HEAD // LANES) * LANES
    high = d // chips
    least, _ = tile_share(columns // LANES, chips)
    held = [
        Paired.scratch(chips, (high, least * LANES), BF16) + Paired.scratch(chips, (high, LANES), BF16),
        Paired.scratch(chips, (high // 2, width), BF16),
    ]
    early = lambda i: jnp.minimum(i, count - 1)
    late = lambda i: jnp.maximum(i - count, 0)
    first = pl.BlockSpec((low, n), lambda i: (early(i), 0))
    per_query = pl.BlockSpec((heads, rows, HEAD), lambda i: (0, late(i), 0))
    whole = resident((length, HEAD))
    return pl.pallas_call(
        functools.partial(backward_kernel, chips, lead, [len(h) for h in held]),
        grid=(count + length // rows,),
        in_specs=[
            pl.BlockSpec((group, tokens, d), lambda i: (early(i), 0, 0)),
            resident((d, width), small.shape[1] // width - 1),
            resident((d, n)),
            first,
            per_query,
            whole,
            whole,
            per_query,
            pl.BlockSpec((heads, 1, rows), lambda i: (0, 0, late(i))),
            whole,
            whole,
            ANY,
            ANY,
        ],
        out_specs=[first, resident((length, out_width)), ANY, ANY],
        out_shape=[
            jax.ShapeDtypeStruct((length, n), BF16),
            jax.ShapeDtypeStruct((length, out_width), BF16),
            jax.ShapeDtypeStruct((high, columns), BF16),
            jax.ShapeDtypeStruct((chips, high // 2, width), BF16),
        ],
        scratch_shapes=[
            pltpu.VMEM((heads, length, HEAD), BF16),
            pltpu.VMEM((rows, HEAD), F32),
            pltpu.VMEM((length, HEAD), F32),
            pltpu.VMEM((length, HEAD), F32),
        ]
        + [s for h in held for s in h],
        compiler_params=pltpu.CompilerParams(collective_id=number, has_side_effects=True, vmem_limit_bytes=60 << 20),
        cost_estimate=pl.CostEstimate(
            flops=2 * length * d * (n + width) + 5 * heads * length * length * HEAD,
            transcendentals=heads * length * length // 2,
            bytes_accessed=2 * length * d,
        ),
        name="backward",
    )(g, small, down, slope, q, k, v, o, lse, cosines, sines, down_part, dense_part)


def out_kernel(a_ref, b_ref, small_ref, wide_ref, out_ref):
    tokens, d = out_ref.shape[-2:]
    step = a_ref.shape[0] // tokens
    a, b = a_ref[...], b_ref[...]
    for at, width in chunks(d, 512):
        part = dot(a, small_ref[at : at + width], ROWS_COLS) + dot(b, wide_ref[at : at + width], ROWS_COLS)
        part = part.astype(BF16).reshape(step, tokens, width)
        if out_ref.ndim == 4:
            out_ref[:, 0, :, at : at + width] = part
        else:
            out_ref[:, :, at : at + width] = part


def out_product(a, b, small, column, wide, chips, name, by_plane=False):
    length, width = a.shape
    tokens, d = length // chips, small.shape[0]
    step = max(1, 512 // tokens)
    rows = step * tokens
    n = wide.shape[1]
    shape, spec = (chips, tokens, d), pl.BlockSpec((step, tokens, d), lambda i: (i, 0, 0))
    if by_plane:
        nz, ny, nx = grid_of(chips)
        per = ny * nx // step
        shape = (ny * nx, nz, tokens, d)
        spec = pl.BlockSpec((step, 1, tokens, d), lambda i: (lax.rem(i, per), i // per, 0, 0))
    return pl.pallas_call(
        out_kernel,
        grid=(chips // step,),
        in_specs=[per_row(rows, width), per_row(rows, n), resident((d, width), column), resident((d, n))],
        out_specs=spec,
        out_shape=jax.ShapeDtypeStruct(shape, BF16),
        compiler_params=pltpu.CompilerParams(vmem_limit_bytes=56 << 20),
        cost_estimate=pl.CostEstimate(
            flops=2 * length * d * (n + width), transcendentals=0, bytes_accessed=2 * length * d
        ),
        name=name,
    )(a, b, small, wide)


def weight_kernel(x_ref, a_ref, b_ref, small_ref, wide_ref):
    chips, tokens, width = x_ref.shape
    x = x_ref[...].reshape(chips * tokens, width)
    small_ref[...] = dot(x, a_ref[...], ROWS_ROWS).astype(BF16)
    for at, n in chunks(wide_ref.shape[1], 1152):
        wide_ref[:, at : at + n] = dot(x, b_ref[:, at : at + n], ROWS_ROWS).astype(BF16)


def weight_product(x, a, b, name):
    chips, tokens, d = x.shape
    length = chips * tokens
    width = 768 if d % 768 == 0 else 512
    return pl.pallas_call(
        weight_kernel,
        grid=(d // width,),
        in_specs=[pl.BlockSpec((chips, tokens, width), lambda i: (0, 0, i)), resident(a.shape), resident(b.shape)],
        out_specs=[per_row(width, a.shape[1]), per_row(width, b.shape[1])],
        out_shape=[jax.ShapeDtypeStruct((d, a.shape[1]), BF16), jax.ShapeDtypeStruct((d, b.shape[1]), BF16)],
        compiler_params=pltpu.CompilerParams(vmem_limit_bytes=56 << 20),
        cost_estimate=pl.CostEstimate(
            flops=2 * length * d * (a.shape[1] + b.shape[1]), transcendentals=0, bytes_accessed=2 * length * d
        ),
        name=name,
    )(x, a, b)


def share_heads(columns, chips):
    rows, width = columns.shape
    heads = width // HEAD
    most = -(-heads // chips)
    richer = heads - chips * (most - 1)
    cut = richer * most * HEAD
    first = jnp.moveaxis(columns[:, :cut].reshape(rows, richer, most * HEAD), 1, 0)
    if richer == chips:
        return first
    rest = jnp.moveaxis(columns[:, cut:].reshape(rows, chips - richer, (most - 1) * HEAD), 1, 0)
    return jnp.concatenate([first, jnp.pad(rest, ((0, 0), (0, 0), (0, HEAD)))], 0)


def join_heads(parts, heads):
    chips, rows, width = parts.shape
    most = width // HEAD
    richer = heads - chips * (most - 1)
    first = jnp.moveaxis(parts[:richer], 0, 1).reshape(rows, -1)
    if richer == chips:
        return first
    rest = jnp.moveaxis(parts[richer:, :, : width - HEAD], 0, 1).reshape(rows, -1)
    return jnp.concatenate([first, rest], 1)


def swap(values):
    return lax.ppermute(values, "fsdp", [(0, 1), (1, 0)])


def in_order(mine, other, core, axis):
    return jnp.where(
        core == 0,
        jnp.concatenate([mine, other], axis),
        jnp.concatenate([other, mine], axis),
    )


def half_of(values, core, axis):
    first, second = jnp.split(values, 2, axis)
    return jnp.where(core == 0, first, second), jnp.where(core == 0, second, first)


def angles(length):
    inverse_freq = ROPE_BASE ** (-jnp.arange(0, HEAD, 2).astype(F32) / HEAD)
    phases = jnp.arange(length, dtype=jnp.int32).astype(F32)[:, None] * inverse_freq[None, :]
    phases = jnp.concatenate([phases, phases], -1)
    return jnp.cos(phases), jnp.sin(phases)


def body(layer_input, cotangent, norm_gain, norm_bias, qkv_weight, up_weight, dense_weight, down_weight):
    chips = lax.axis_size("ctx")
    core = lax.axis_index("fsdp")
    inputs = layer_input[0].astype(F32)
    tokens, features = inputs.shape
    length = tokens * chips
    heads = features // HEAD
    most = -(-heads // chips)
    qwide = most * HEAD
    rows = qkv_weight.shape[0]
    high = padded_rows(rows)
    wide_columns = up_weight.shape[1]
    lead = (qwide + 2 * HEAD) % LANES

    def pad(values):
        apart = values.reshape(*values.shape[:-1], chips, rows)
        apart = jnp.pad(apart, [(0, 0)] * (apart.ndim - 1) + [(0, high - rows)])
        return apart.reshape(*values.shape[:-1], chips * high)

    def unpad(values):
        apart = values.reshape(*values.shape[:-1], chips, high)[..., :rows]
        return apart.reshape(*values.shape[:-1], features)

    def pad_rows(weight):
        return jnp.pad(weight, ((0, high - rows), (0, 0)))

    center = inputs - jnp.mean(inputs, -1, keepdims=True)
    inverse = lax.rsqrt(jnp.mean(center * center, -1, keepdims=True) + EPS)
    xhat = center * inverse
    normed_low = pad((xhat * norm_gain + norm_bias).astype(BF16))
    grad_low = pad(cotangent[0])

    mine, other = half_of(pad_rows(jnp.concatenate([qkv_weight, dense_weight], 1)), core, 0)
    other = swap(other)
    qkv_columns = qkv_weight.shape[1]
    qkv_rows = in_order(mine[:, :qkv_columns], other[:, :qkv_columns], core, 1)
    dense_rows = in_order(mine[:, qkv_columns:], other[:, qkv_columns:], core, 1)
    blocks = jnp.concatenate(
        [
            share_heads(qkv_rows[:, :features], chips),
            jnp.broadcast_to(qkv_rows[:, features:], (chips, high // 2, 2 * HEAD)),
            share_heads(dense_rows, chips),
        ],
        2,
    )
    normed_all, up_cols, small = bring(
        chips, 0, "bring", (Gather, normed_low), (Columns, pad_rows(up_weight)), (Blocks, blocks)
    )

    cosines, sines = angles(length)
    dense_block = small.shape[1] // (lead + qwide) - 1
    (queries, keys, values, hidden_low, slope, attended_low, attention, log_sum), (grad_all, down_cols) = forward(
        normed_all,
        small,
        up_cols,
        cosines,
        sines,
        most,
        lead,
        2,
        [(Gather, grad_low), (Columns, pad_rows(down_weight))],
    )
    branch = out_product(attended_low, hidden_low, small, dense_block, down_cols, chips, "forward_out", True)
    branch, grad_all = lax.optimization_barrier((branch, grad_all))
    nz, ny, nx = grid_of(chips)
    planes = [[z * ny * nx + i for i in range(ny * nx)] for z in range(nz)]
    lines = [[z * ny * nx + i for z in range(nz)] for i in range(ny * nx)]
    branch = branch.reshape(ny * nx, nz * tokens, -1)
    branch = lax.psum_scatter(branch, "ctx", scatter_dimension=0, axis_index_groups=planes, tiled=False)

    dense_part, down_part = weight_product(grad_all, attended_low, hidden_low, "late_weights")
    grad_up, grad_joined, down_grad, dense_total = backward(
        grad_all,
        small,
        lead,
        down_cols,
        slope,
        queries,
        keys,
        values,
        attention,
        log_sum,
        cosines,
        sines,
        3,
        down_part,
        dense_part,
        wide_columns,
    )
    branch, grad_joined = lax.optimization_barrier((branch, grad_joined))
    branch = branch.reshape(nz, tokens, -1)
    branch = lax.psum_scatter(branch, "ctx", scatter_dimension=0, axis_index_groups=lines, tiled=False)
    layer_output = (inputs + unpad(branch).astype(F32)).astype(BF16)
    grad_normed = out_product(grad_joined, grad_up, small, 0, up_cols, chips, "back_out")

    input_grad, stats, up_grad, total = send(
        chips,
        1,
        features,
        grad_normed,
        normed_all,
        grad_joined,
        grad_up,
        wide_columns,
        pad(xhat),
        grad_low,
        pad(norm_gain[None]),
        inverse,
    )
    up_grad = up_grad[:rows].astype(F32)
    down_grad = down_grad[:rows].astype(F32)
    qkv_rows = jnp.concatenate(
        [
            join_heads(total[:, :, :qwide], heads),
            jnp.sum(total[:, :, qwide : qwide + 2 * HEAD].astype(F32), 0).astype(BF16),
        ],
        1,
    )
    dense_rows = join_heads(dense_total[:, :, lead:], heads)

    def own_columns(values):
        mine, other = half_of(values, core, 1)
        return in_order(mine, swap(other), core, 0)[:rows].astype(F32)

    stats = unpad(stats)
    return (
        layer_output[None],
        unpad(input_grad)[None],
        stats[0],
        stats[1],
        own_columns(qkv_rows),
        up_grad,
        own_columns(dense_rows),
        down_grad,
    )


def solution(mesh):
    split = P("ctx", "fsdp")
    stream = P("fsdp", "ctx", None)
    return jax.shard_map(
        body,
        mesh=mesh,
        in_specs=(stream, stream, P(), P(), split, split, split, split),
        out_specs=(stream, stream, P(), P(), split, split, split, split),
        check_vma=False,
    )
```
